32 devices in a mesh: dp: 8 (over y, x, core), seq: 4 (over z).
Axes of the slice: x: 2, y: 2, z: 4, core: 2. Of those that a mesh axis runs over, the one named last changes fastest.
Arguments:
- tokens: bfloat16 [16, 256, 768], P('dp', 'seq'), may hold values from -6 to 6
- key_mask: int32 [16, 256], P('dp'), may hold values from 0 to 1, as said below
- expert_ids: int32 [16, 256, 2], P('dp', 'seq'), may hold values from 0 to 3, all different within a row; in each aligned block of 64 rows (0 to 63, 64 to 127, ..., all dimensions but the last counted through in order) at most 40 rows name the same one
- ln1_gain: bfloat16 [768], P('dp'), may hold values from 0.5 to 1.5
- ln1_bias: bfloat16 [768], P('dp'), may hold values from -0.59765625 to 0.59765625
- w_qkv: bfloat16 [768, 2304], P('dp'), may hold values from -0.3125 to 0.3125
- w_attn_out: bfloat16 [768, 768], P('dp'), may hold values from -0.875 to 0.875
- ln2_gain: bfloat16 [768], P('dp'), may hold values from 0.5 to 1.5
- ln2_bias: bfloat16 [768], P('dp'), may hold values from -0.59765625 to 0.59765625
- router: bfloat16 [768, 4], P('dp'), may hold values from -0.15625 to 0.15625
- w_in: bfloat16 [4, 768, 3072], P(None, 'dp'), may hold values from -0.21875 to 0.21875
- w_out: bfloat16 [4, 3072, 768], P(None, 'dp'), may hold values from -0.21875 to 0.21875
- cotangent: bfloat16 [16, 256, 768], P('dp', 'seq'), may hold values from -6 to 6
Outputs:
- out: bfloat16 [16, 256, 768], P('dp', 'seq')
- grad_tokens: float32 [16, 256, 768], P('dp', 'seq')
- grad_ln1_gain: float32 [768], P('dp')
- grad_ln1_bias: float32 [768], P('dp')
- grad_w_qkv: float32 [768, 2304], P('dp')
- grad_w_attn_out: float32 [768, 768], P('dp')
- grad_ln2_gain: float32 [768], P('dp')
- grad_ln2_bias: float32 [768], P('dp')
- grad_router: float32 [768, 4], P('dp')
- grad_w_in: float32 [4, 768, 3072], P(None, 'dp')
- grad_w_out: float32 [4, 3072, 768], P(None, 'dp')
The draws below stay inside these ranges and needn't reach their ends.
Inputs may be any that keep to these rules, and one draw needn't show every extreme that they name: `key_mask`: each image's ones form a prefix of its positions, at least 192 long. `expert_ids`: each token names 2 different experts; among one image's positions on one index of seq, no expert is named by more than 40 tokens, and this bound is reached.
All inputs are finite; a program needn't handle non-finite values.
Results may differ from the reference program's by a relative error of at most 0.017.
The reference program's roundings to bfloat16 on the way count: a program that leaves them out, or rounds other values in their place, can miss the bound.
Values may be sent and summed in bfloat16 or wider, within the bound.
A program may use at most 320 MiB of HBM per device.

```python
import math
import jax
import jax.numpy as jnp
import numpy as np
from jax import lax

D = 768
HEADS = 12
HEAD = 64
FF = 3072
EXPERTS = 4
TOPK = 2
LEN = 256
MOST = 40
IMG_DEV = 2
IMAGES = 16
POS_DEV = 64


def draw_key_mask(key, part):
    lengths = jax.random.randint(key, (IMAGES, 1), LEN - LEN // 4, LEN + 1)
    places = jnp.arange(LEN, dtype=jnp.int32)[None, :]
    return (places < lengths).astype(jnp.int32)


def steps_of(own_key, extent, split, smallest, high):
    def one(position, shards_of):
        steps = jax.random.uniform(jax.random.fold_in(jax.random.fold_in(own_key, 6), position), (shards_of,), jnp.float32, smallest / len(split), high / len(split))
        return jnp.repeat(jnp.exp(steps), extent[position] // shards_of).reshape((-1,) + (1,) * (len(extent) - position - 1))

    loudness = one(*split[0])
    for cut in split[1:]:
        loudness = loudness * one(*cut)
    return loudness


def routed_block(key, own, number, rows, number_of, top, most, slope):
    ranking = jax.random.permutation(key, number_of)
    crowded, usual = load_shares(number_of, rows * top, most, slope, True), load_shares(number_of, rows * top, most, slope, False)
    places = jnp.arange(number_of)

    def named(sizes, turn):
        used = int((sizes > 0).sum())
        fixed = max(1, used // 4)
        moved = fixed + (places - fixed + turn * (used - fixed)) % max(1, number_of - fixed)
        return jnp.zeros((number_of,), jnp.int32).at[ranking[jnp.where(places < fixed, places, moved)]].set(jnp.asarray(sizes, jnp.int32))

    sizes = jnp.where(number % 4 == 0, named(crowded, number // 4), named(usual, number - number // 4 - 1))
    mixed = jax.random.permutation(jax.random.fold_in(own, 3), number_of)
    donor, receiver = mixed[0:number_of // 2 * 2:2], mixed[1:number_of // 2 * 2:2]
    margin = jnp.minimum(sizes[donor] - 1, most - sizes[receiver]) // 2
    margin = jnp.where((donor == ranking[0]) | (receiver == ranking[0]) | (sizes[receiver] == 0), 0, jnp.maximum(margin, 0))
    moved = jax.random.randint(jax.random.fold_in(own, 4), (number_of // 2,), 0, 1 << 20) % (margin + 1)
    sizes = sizes.at[donor].add(-moved).at[receiver].add(moved)
    members = jnp.searchsorted(jnp.cumsum(sizes), jnp.arange(rows * top), side="right").astype(jnp.int32)
    grid = members.reshape(top, rows).T
    grid = grid[jax.random.permutation(jax.random.fold_in(own, 1), rows)]
    turn = jax.random.randint(jax.random.fold_in(own, 2), (rows, 1), 0, top)
    return jnp.take_along_axis(grid, (jnp.arange(top)[None, :] + turn) % top, axis=1)


def load_shares(number_of, total, bound, lean, full):
    loads = [(1 << 20) // math.isqrt(standing ** lean) + 1 for standing in range(1, number_of + 1)]
    largest = bound if full else min(bound, max(-(-total // number_of), total * loads[0] // sum(loads)))
    least = 1 if total - largest >= number_of - 1 else 0
    given, rest = [largest] + [least] * (number_of - 1), total - largest - least * (number_of - 1)
    while rest > 0:
        movable = [i for i in range(1, number_of) if given[i] < largest] or [i for i in range(1, number_of) if given[i] < bound]
        mass, budget = sum([loads[i] for i in movable]), rest
        for i in movable:
            extra = min(bound - given[i], max(1, budget * loads[i] // mass), rest)
            given[i] = given[i] + extra
            rest = rest - extra
    return np.array(given)


def bell_draw(rng, extent, scale, limit, split=(), kind=jnp.bfloat16):
    values = scale * jax.random.normal(rng, extent, jnp.float32)
    if split:
        values = values * steps_of(rng, extent, split, -0.22, 0.18)
    return jnp.clip(values, -limit, limit).astype(kind)


def setup_inputs(seed: int = 0) -> dict:
    key_of = jax.random.split(jax.random.key(seed), 14)
    tokens = bell_draw(key_of[0], (IMAGES, LEN, D), 1.0, 6.0, ((0, 8), (1, 4)))
    key_mask = draw_key_mask(jax.random.fold_in(key_of[13], 71), 0)
    expert_ids_keys = jax.random.split(jax.random.fold_in(key_of[2], 1), IMAGES * LEN // POS_DEV)
    expert_ids_turns = jax.random.permutation(jax.random.fold_in(key_of[2], 3), IMAGES * LEN // POS_DEV)
    expert_ids = jax.vmap(lambda own, number: routed_block(jax.random.fold_in(key_of[2], 2), own, number, POS_DEV, EXPERTS, TOPK, MOST, 1))(expert_ids_keys, expert_ids_turns).reshape((IMAGES, LEN, TOPK))
    ln1_gain = jnp.clip(1.0 + 0.1 * jax.random.normal(key_of[3], (D,), jnp.float32), 0.5, 1.5).astype(jnp.bfloat16)
    ln1_bias = bell_draw(key_of[4], (D,), 0.1, 0.59765625, ((0, 8),))
    w_qkv = bell_draw(key_of[5], (D, 3 * D), (D // 2) ** -0.5, 0.3125, ((0, 8),))
    w_attn_out = bell_draw(key_of[6], (D, D), (D // 16) ** -0.5, 0.875, ((0, 8),))
    ln2_gain = jnp.clip(1.0 + 0.1 * jax.random.normal(key_of[7], (D,), jnp.float32), 0.5, 1.5).astype(jnp.bfloat16)
    ln2_bias = bell_draw(key_of[8], (D,), 0.1, 0.59765625, ((0, 8),))
    router = bell_draw(key_of[9], (D, EXPERTS), (2 * D) ** -0.5, 0.15625, ((0, 8),))
    w_in = bell_draw(key_of[10], (EXPERTS, D, FF), D ** -0.5, 0.21875, ((1, 8),))
    w_out = bell_draw(key_of[11], (EXPERTS, FF, D), (FF // 4) ** -0.5, 0.21875, ((1, 8),))
    cotangent = bell_draw(key_of[12], (IMAGES, LEN, D), 1.0, 6.0, ((0, 8), (1, 4)))
    return {"tokens": tokens, "key_mask": key_mask, "expert_ids": expert_ids, "ln1_gain": ln1_gain, "ln1_bias": ln1_bias, "w_qkv": w_qkv, "w_attn_out": w_attn_out, "ln2_gain": ln2_gain, "ln2_bias": ln2_bias, "router": router, "w_in": w_in, "w_out": w_out, "cotangent": cotangent}


@jax.custom_vjp
def low(v):
    return lax.optimization_barrier(v.astype(jnp.bfloat16)).astype(jnp.float32)

@jax.custom_vjp
def low_back(v):
    return v

def low_keep(v):
    return (low(v), None)

def low_pass(kept, grad):
    return (grad,)

def back_keep(v):
    return (v, None)

def back_low(kept, grad):
    return (low(grad),)
low.defvjp(low_keep, low_pass)
low_back.defvjp(back_keep, back_low)
highest = lax.Precision.HIGHEST

def layer_norm(inputs, norm_gain, norm_shift):
    centre = inputs - lax.optimization_barrier(jnp.mean(inputs, axis=-1, keepdims=True))
    spread = lax.optimization_barrier(jnp.mean(centre * centre, axis=-1, keepdims=True))
    return centre * lax.rsqrt(spread + 1e-06) * norm_gain + norm_shift

def softmax_rows(scores):
    row_max = lax.optimization_barrier(jnp.max(scores, axis=-1, keepdims=True))
    expo_terms = jnp.exp(scores - row_max)
    return expo_terms / lax.optimization_barrier(jnp.sum(expo_terms, axis=-1, keepdims=True))

def block_forward(params, tokens, key_mask, expert_ids):
    norm1_gain, norm1_shift, qkv_weight, proj_weight, norm2_gain, norm2_shift, router_weight, inner_weight, outer_weight = params
    images = tokens.shape[0]
    normed = low(layer_norm(tokens, norm1_gain, norm1_shift))
    packed = jnp.einsum('bpd,de->bpe', normed, qkv_weight, precision=highest)
    packed = low_back(low(packed)).reshape(images, LEN, 3, HEADS, HEAD)
    queries = packed[:, :, 0]
    key_rows = packed[:, :, 1]
    values = packed[:, :, 2]
    scores = low_back(jnp.einsum('bqhc,bkhc->bhqk', queries, key_rows, precision=highest) * HEAD ** (-0.5))
    scores = jnp.where(key_mask[:, None, None, :] > 0, scores, -1e+30)
    attn_probs = low(softmax_rows(scores))
    mixed_heads = jnp.einsum('bhqk,bkhc->bqhc', attn_probs, values, precision=highest)
    mixed_heads = low_back(low(mixed_heads)).reshape(images, LEN, D)
    attn_out = low_back(jnp.einsum('bpd,de->bpe', mixed_heads, proj_weight, precision=highest))
    residual = tokens + attn_out
    normed2 = low(layer_norm(residual, norm2_gain, norm2_shift))
    logits = low_back(jnp.einsum('bpd,de->bpe', normed2, router_weight, precision=highest))
    gate_probs = softmax_rows(logits)
    chosen = lax.optimization_barrier(jnp.sum((expert_ids[..., None] == jnp.arange(EXPERTS, dtype=jnp.int32)).astype(jnp.float32), axis=2))
    mixing = chosen * gate_probs
    total = residual
    for expert in range(EXPERTS):
        expert_rows = low_back(normed2)
        hidden = low_back(jnp.einsum('bpd,df->bpf', expert_rows, inner_weight[expert], precision=highest))
        active = low(jax.nn.gelu(hidden, approximate=False))
        result = low_back(jnp.einsum('bpf,fd->bpd', active, outer_weight[expert], precision=highest))
        total = total + mixing[..., expert:expert + 1] * result
    return total

def reference(tokens, key_mask, expert_ids, ln1_gain, ln1_bias, w_qkv, w_attn_out, ln2_gain, ln2_bias, router, w_in, w_out, cotangent):
    params = tuple((weight.astype(jnp.float32) for weight in (ln1_gain, ln1_bias, w_qkv, w_attn_out, ln2_gain, ln2_bias, router, w_in, w_out)))
    inputs = tokens.astype(jnp.float32)
    blocks = IMAGES // IMG_DEV
    mask_blocks = key_mask.reshape(blocks, IMG_DEV, LEN)
    route_blocks = expert_ids.reshape(blocks, IMG_DEV, LEN, TOPK)

    def forward(inputs, params):

        def run_block(pieces):
            return jax.checkpoint(block_forward)(params, pieces[0], pieces[1], pieces[2])
        outputs = lax.map(run_block, (inputs.reshape(blocks, IMG_DEV, LEN, D), mask_blocks, route_blocks))
        return outputs.reshape(IMAGES, LEN, D)
    outputs, pullback = jax.vjp(forward, inputs, params)
    grad_inputs, grads = pullback(cotangent.astype(jnp.float32))
    return (outputs.astype(jnp.bfloat16), grad_inputs, grads[0], grads[1], grads[2], grads[3], grads[4], grads[5], grads[6], grads[7], grads[8])
```

```python
import jax
import jax.numpy as jnp
from jax import lax
from jax.experimental import pallas as pl
from jax.experimental.pallas import tpu as pltpu
from jax.sharding import PartitionSpec as P

MESH = pl.DeviceIdType.MESH
F32, BF16 = jnp.float32, jnp.bfloat16
HEADS = 12
HEAD = 64
NT = (((1,), (1,)), ((), ()))
TN = (((0,), (0,)), ((), ()))


def dot(a, b, dims=(((1,), (0,)), ((), ()))):
    return lax.dot_general(a, b, dims, preferred_element_type=F32)


def mult(value, by):
    return pl.multiple_of(value, by)


class Place:
    def __init__(self):
        self.dp = lax.axis_index("dp")
        self.s = lax.axis_index("seq")
        self.core = lax.rem(self.dp, 2)
        self.x = lax.rem(lax.div(self.dp, 2), 2)
        self.y = lax.div(self.dp, 4)

    def chip(self, k):
        x = 1 - self.x if k % 2 else self.x
        y = 1 - self.y if k // 2 else self.y
        return y * 2 + x

    def peer(self, k):
        return self.chip(k) * 2 + self.core

    def partner(self):
        return self.dp + 1 - 2 * self.core

    def around(self, k):
        return lax.rem(self.dp + k, 8)

    def zring(self, k):
        return lax.rem(self.s + k, 4)


def entry_barrier(me, plane, zs):
    sem = pltpu.get_barrier_semaphore()
    count = 0
    if plane:
        for k in range(1, 8):
            pl.semaphore_signal(
                sem, inc=1, device_id={"dp": me.around(k)}, device_id_type=MESH
            )
            count += 1
    if zs:
        for k in range(1, 4):
            pl.semaphore_signal(
                sem, inc=1, device_id={"seq": me.zring(k)}, device_id_type=MESH
            )
            count += 1
    pl.semaphore_wait(sem, count)


def remote(src, dst, send, recv, **where):
    return pltpu.make_async_remote_copy(
        src_ref=src, dst_ref=dst, send_sem=send, recv_sem=recv, device_id=where, device_id_type=MESH
    )


class PlaneGather:
    def __init__(self, me, src, place, send, recv, local=True):
        self.me = me
        self.place = place
        self.sends = [remote(src, place(me.dp), send.at[0], recv.at[0], dp=me.partner())]
        for k in range(1, 4):
            self.sends.append(remote(src, place(me.dp), send.at[k], recv.at[k], dp=me.peer(k)))
        self.onward = []
        for k in range(1, 4):
            there = place(me.peer(k))
            self.onward.append(remote(there, there, send.at[3 + k], recv.at[3 + k], dp=me.partner()))
        self.local = pltpu.make_async_copy(src, place(me.dp), send.at[7]) if local else None

    def start(self):
        for copy in self.sends[1:]:
            copy.start()
        self.sends[0].start()
        if self.local is not None:
            self.local.start()

    def forward(self):
        for k in range(1, 4):
            self.sends[k].wait_recv()
            self.onward[k - 1].start()

    def finish(self):
        self.sends[0].wait_recv()
        for copy in self.onward:
            copy.wait_recv()
        for copy in self.sends + self.onward:
            copy.wait_send()
        if self.local is not None:
            self.local.wait()


class Spread:
    def __init__(self, me, src, place, send, recv, axis, local=True):
        count, step, own = (8, me.around, me.dp) if axis == "dp" else (4, me.zring, me.s)
        self.copies = [
            remote(src, place(own), send.at[k], recv.at[k], **{axis: step(k)})
            for k in range(1, count)
        ]
        self.local = pltpu.make_async_copy(src, place(own), send.at[0]) if local else None

    def start(self):
        for copy in self.copies:
            copy.start()
        if self.local is not None:
            self.local.start()

    def arrive(self):
        for copy in self.copies:
            copy.wait_recv()
        if self.local is not None:
            self.local.wait()

    def drain(self):
        for copy in self.copies:
            copy.wait_send()


def norm_rows(rows, gain, shift):
    centre = rows - jnp.mean(rows, axis=-1, keepdims=True)
    spread = jnp.mean(centre * centre, axis=-1, keepdims=True)
    return centre * lax.rsqrt(spread + 1e-06) * gain + shift


def forward_kernel(
    x, mask, ids, pk, wqkv, wo, win, g,
    o_wqkv, o_wo, o_xall, o_pvec, o_win, o_gz, o_gp, o_n2z, o_n2p, o_mixz, o_mixp, o_res, o_gates,
    pkall, n1s, qkvs, heads, n2s, mixs, rpad,
    ag_send, ag_recv, z_send, z_recv, a_send, a_recv, m_send, m_recv,
):
    me = Place()
    entry_barrier(me, True, True)
    zx = Spread(me, x, lambda s: o_xall.at[:, pl.ds(mult(64 * s, 64), 64), :], z_send.at[0], z_recv.at[0], "seq")
    small = Spread(me, pk, lambda d: pkall.at[d], m_send.at[0], m_recv.at[0], "dp")
    gq = PlaneGather(me, wqkv, lambda d: o_wqkv.at[pl.ds(mult(96 * d, 32), 96), :], ag_send.at[0], ag_recv.at[0])
    gw = PlaneGather(me, wo, lambda d: o_wo.at[pl.ds(mult(96 * d, 32), 96), :], ag_send.at[1], ag_recv.at[1])
    zg = Spread(me, g, lambda s: o_gz.at[s], z_send.at[1], z_recv.at[1], "seq")
    gg = PlaneGather(me, g, lambda d: o_gp.at[d], ag_send.at[2], ag_recv.at[2])
    small.start()
    zx.start()
    gq.start()
    gw.start()
    small.arrive()
    total = jnp.zeros((16, 768), F32)
    row = lax.broadcasted_iota(jnp.int32, (128, 768), 0)
    col = lax.broadcasted_iota(jnp.int32, (128, 768), 1)
    for j in range(8):
        spot = jnp.where((row < 96) & (row + 96 * j == col), 1.0, 0.0).astype(BF16)
        total = total + dot(pkall[j], spot)
    o_pvec[...] = total
    rpad[...] = jnp.zeros_like(rpad)
    rpad[0:16, :] = total.astype(BF16)
    zx.arrive()
    zg.start()

    def ln_step(t, carry):
        i, h = lax.div(t, 2), lax.rem(t, 2)
        rows = o_xall[i, pl.ds(mult(128 * h, 128), 128), :].astype(F32)
        n1s[i, pl.ds(mult(128 * h, 128), 128), :] = norm_rows(
            rows, o_pvec[4:5, :], o_pvec[5:6, :]
        ).astype(BF16)
        return carry

    lax.fori_loop(0, 4, ln_step, 0)
    gq.forward()
    gw.forward()
    a2a = []
    for k in range(1, 8):
        t = me.around(k)
        a2a.append(
            remote(
                win.at[:, :, pl.ds(mult(384 * t, 128), 384)],
                o_win.at[:, pl.ds(mult(96 * me.dp, 32), 96), :],
                a_send.at[k], a_recv.at[k], dp=t,
            )
        )
    for copy in a2a:
        copy.start()
    own = pltpu.make_async_copy(
        win.at[:, :, pl.ds(mult(384 * me.dp, 128), 384)],
        o_win.at[:, pl.ds(mult(96 * me.dp, 32), 96), :],
        a_send.at[0],
    )
    own.start()
    gg.start()
    gq.finish()
    gw.finish()

    def qkv_step(t, carry):
        kind, i = lax.div(t, 2), lax.rem(t, 2)
        w = o_wqkv[:, pl.ds(mult(768 * kind, 128), 768)]
        qkvs[kind, i] = dot(n1s[i], w).astype(BF16)
        return carry

    lax.fori_loop(0, 6, qkv_step, 0)
    first = mult(64 * me.s, 64)

    def attend(t, carry):
        i, j = lax.div(t, 6), lax.rem(t, 6)
        lanes = pl.ds(mult(128 * j, 128), 128)
        q = qkvs[0, i, pl.ds(first, 64), lanes]
        keys = qkvs[1, i, :, lanes]
        vals = qkvs[2, i, :, lanes]
        left = lax.broadcasted_iota(jnp.int32, (64, 128), 1) < HEAD
        zero = jnp.zeros_like(q)
        both = jnp.concatenate([jnp.where(left, q, zero), jnp.where(left, zero, q)], axis=0)
        scores = dot(both, keys, NT) * HEAD ** (-0.5)
        valid = mask[pl.ds(i, 1), :] > 0
        scores = jnp.where(valid, scores, -1e30)
        terms = jnp.exp(scores - jnp.max(scores, axis=-1, keepdims=True))
        probs = terms / jnp.sum(terms, axis=-1, keepdims=True)
        mixed = dot(probs.astype(BF16), vals)
        heads[pl.ds(mult(64 * i, 64), 64), lanes] = jnp.where(left, mixed[:64], mixed[64:]).astype(BF16)
        return carry

    lax.fori_loop(0, 12, attend, 0)
    for i in range(2):
        rows = slice(64 * i, 64 * i + 64)
        tokens = o_xall[i, pl.ds(first, 64), :].astype(F32)
        res = tokens + dot(heads[rows, :], o_wo[...])
        o_res[rows, :] = res
        n2s[rows, :] = norm_rows(res, o_pvec[6:7, :], o_pvec[7:8, :]).astype(BF16)
    zn = Spread(me, n2s, lambda s: o_n2z.at[s], z_send.at[2], z_recv.at[2], "seq")
    gn = PlaneGather(me, n2s, lambda d: o_n2p.at[d], ag_send.at[3], ag_recv.at[3])
    zm = Spread(me, mixs, lambda s: o_mixz.at[s], z_send.at[3], z_recv.at[3], "seq")
    gm = Spread(me, mixs, lambda d: o_mixp.at[d], m_send.at[1], m_recv.at[1], "dp")
    logits = dot(n2s[...], rpad[...], NT)
    gn.start()
    zn.start()
    lane = lax.broadcasted_iota(jnp.int32, (128, 128), 1)
    logits = jnp.where(lane < 4, logits, -1e30)
    terms = jnp.exp(logits - jnp.max(logits, axis=-1, keepdims=True))
    gates = terms / jnp.sum(terms, axis=-1, keepdims=True)
    o_gates[...] = gates
    chosen = (lane == ids[:, 0:1]) | (lane == ids[:, 1:2])
    mix = jnp.where(chosen, gates, 0.0)
    mixs[...] = mix.T[0:8, :]
    gm.start()
    zm.start()
    gg.forward()
    gn.forward()
    for copy in a2a:
        copy.wait()
    own.wait()
    gg.finish()
    gn.finish()
    for one in (zg, zn, zm, gm):
        one.arrive()
    for one in (small, zx, zg, zn, zm, gm):
        one.drain()


VM = pl.BlockSpec(memory_space=pltpu.VMEM)
ANY = pl.BlockSpec(memory_space=pl.ANY)
DMA = pltpu.SemaphoreType.DMA


def sds(shape, dtype=BF16):
    return jax.ShapeDtypeStruct(shape, dtype)


def run_forward(x, mask, ids, pk, wqkv, wo, win, g):
    return pl.pallas_call(
        forward_kernel,
        out_shape=[
            sds((768, 2304)), sds((768, 768)), sds((2, 256, 768)), sds((16, 768), F32),
            sds((4, 768, 384)), sds((4, 128, 768)), sds((8, 128, 768)), sds((4, 128, 768)),
            sds((8, 128, 768)), sds((4, 8, 128), F32), sds((8, 8, 128), F32),
            sds((128, 768), F32), sds((128, 128), F32),
        ],
        in_specs=[ANY, VM, VM, VM, ANY, ANY, ANY, ANY],
        out_specs=[VM, VM, VM, VM, ANY, ANY, ANY, ANY, ANY, ANY, ANY, VM, VM],
        scratch_shapes=[
            pltpu.VMEM((8, 16, 128), BF16),
            pltpu.VMEM((2, 256, 768), BF16),
            pltpu.VMEM((3, 2, 256, 768), BF16),
            pltpu.VMEM((128, 768), BF16),
            pltpu.VMEM((128, 768), BF16),
            pltpu.VMEM((8, 128), F32),
            pltpu.VMEM((128, 768), BF16),
            DMA((4, 8)), DMA((4, 8)), DMA((4, 4)), DMA((4, 4)),
            DMA((8,)), DMA((8,)), DMA((2, 8)), DMA((2, 8)),
        ],
        compiler_params=pltpu.CompilerParams(
            collective_id=0, has_side_effects=True, vmem_limit_bytes=60 * 2**20
        ),
        name="forward",
    )(x, mask, ids, pk, wqkv, wo, win, g)


def pack_small(ln1_gain, ln1_bias, ln2_gain, ln2_bias, router):
    rows = jnp.concatenate(
        [router.T, ln1_gain[None], ln1_bias[None], ln2_gain[None], ln2_bias[None]], axis=0
    )
    return jnp.pad(rows, ((0, 8), (0, 32)))


ERFC = (
    0.19786723623605862, 0.190899613780153, 0.23209140755646218, -0.027655803526181202,
    0.6019196159005862, -0.6722756114657328, 0.7990689737520851, -0.3864325349090697,
    0.06451709047710916,
)


def normal_parts(h):
    bell = jnp.exp(-0.5 * (h * h))
    t = 1.0 / (1.0 + (0.35 * 0.5**0.5) * jnp.abs(h))
    poly = jnp.full_like(t, 0.5 * ERFC[8])
    for c in ERFC[7::-1]:
        poly = poly * t + 0.5 * c
    tail = poly * t * bell
    return jnp.where(h < 0, tail, 1.0 - tail), h * bell * 0.3989422804014327


def mix_columns(mixes):
    pad = jnp.zeros((120, 128), F32)
    return jnp.concatenate([jnp.concatenate([m, pad], axis=0).T for m in mixes], axis=0)


def backward_kernel(
    wqkv, wo, xall, pvec, win, gz, gp, n2z, n2p, mixz, mixp, res, gates, wout, mask, ids,
    o_out, o_tok, o_gwo, o_gwi, o_att, o_small,
    n2o, go, mixo, gwi, outp, grp, outs, grs, p_recv, c_send, c_recv, gate_send, gate_recv,
    grall, n1s, qkvs, dqkv, left_buf, gq, gq_precv, gq_csend, gq_crecv, zq, grf, gwb,
    small, small_z, small_p, small_sum,
    ag_send, ag_recv, m_send, m_recv, p_ssem, p_rsem, c_ssem, c_rsem, g_ssem, g_rsem,
    z_send, z_recv, q_psend, q_precv, q_csend, q_crecv, w_send, w_recv,
):
    me = Place()
    entry_barrier(me, True, True)
    gathers, mixers = [], []
    for k in range(1, 4):
        gathers.append([
            PlaneGather(me, n2z.at[me.zring(k)], lambda d, k=k: n2o.at[k - 1, d],
                        ag_send.at[2 * k - 2], ag_recv.at[2 * k - 2]),
            PlaneGather(me, gz.at[me.zring(k)], lambda d, k=k: go.at[k - 1, d],
                        ag_send.at[2 * k - 1], ag_recv.at[2 * k - 1]),
        ])
        mixers.append(Spread(me, mixz.at[me.zring(k)], lambda d, k=k: mixo.at[k - 1, d],
                             m_send.at[k - 1], m_recv.at[k - 1], "dp"))
    for one in mixers:
        one.start()
    for one in gathers[0]:
        one.start()
    o_gwo[...] = jnp.zeros_like(o_gwo)
    gwi[...] = jnp.zeros_like(gwi)
    lane128 = lax.broadcasted_iota(jnp.int32, (256, 128), 1)

    def expert_step(e, n2c, gc, columns):
        gate = jnp.sum(jnp.where(lane128 == e, columns, 0.0), axis=1, keepdims=True)
        hidden = dot(n2c, win[e])
        pull = dot(gc, wout[e], NT)
        phi, slope = normal_parts(hidden)
        active = hidden * phi
        taken = (gate * active).astype(BF16)
        grad_hidden = (gate * pull * (phi + slope)).astype(BF16)
        o_gwo[e] += dot(taken, gc, TN)
        gwi[e] += dot(n2c, grad_hidden, TN)
        return active, pull, taken, grad_hidden

    def own_chunk(c):
        columns = mix_columns([mixp[2 * c], mixp[2 * c + 1]])
        n2c = n2p[pl.ds(2 * c, 2)].reshape(256, 768)
        gc = gp[pl.ds(2 * c, 2)].reshape(256, 768)
        outp[...] = jnp.zeros_like(outp)
        grp[...] = jnp.zeros_like(grp)

        def step(e, gate_grads):
            active, pull, taken, grad_hidden = expert_step(e, n2c, gc, columns)
            outp[...] += dot(taken, wout[e])
            grp[...] += dot(grad_hidden, win[e], NT)
            part = jnp.sum(active * pull, axis=1, keepdims=True)
            return jnp.where(lane128 == e, part, gate_grads)

        gate_grads = lax.fori_loop(0, 4, step, jnp.zeros((256, 128), F32))
        for b in range(2):
            outs[2 * c + b] = outp[128 * b : 128 * b + 128].astype(BF16)
            grs[2 * c + b] = grp[128 * b : 128 * b + 128].astype(BF16)
            gate_send[2 * c + b] = gate_grads[128 * b : 128 * b + 128].T[0:8, :]

    partner = me.partner()
    mine = me.chip(0)
    pair, across, gate_copies = [], [], []

    def exchange(k):
        c = me.chip(k)
        other = 2 * c + 1 - me.core
        copies = [
            remote(grs.at[other], p_recv.at[0, k], p_ssem.at[0, k], p_rsem.at[0, k], dp=partner),
            remote(outs.at[other], p_recv.at[1, k], p_ssem.at[1, k], p_rsem.at[1, k], dp=partner),
        ]
        for copy in copies:
            copy.start()
        pair.append(copies)
        for b in range(2):
            if k == 0 and b == 0:
                continue
            target = 2 * c + (me.core if b == 0 else 1 - me.core)
            copy = remote(gate_send.at[target], gate_recv.at[2 * k + b],
                          g_ssem.at[2 * k + b], g_rsem.at[2 * k + b], dp=target)
            copy.start()
            gate_copies.append(copy)

    def push(k, which, source):
        kept = 2 * me.chip(k) + me.core
        total = source[kept].astype(F32) + p_recv[which, k].astype(F32)
        c_send[which, k - 1] = total.astype(BF16)
        copy = remote(c_send.at[which, k - 1], c_recv.at[which, k - 1],
                      c_ssem.at[which, k - 1], c_rsem.at[which, k - 1], dp=me.peer(k))
        copy.start()
        across.append(copy)

    def push_both(k):
        for copy in pair[k - 1]:
            copy.wait_recv()
        push(k, 0, grs)
        push(k, 1, outs)

    own_chunk(me.chip(1))
    exchange(1)
    own_chunk(me.chip(2))
    push_both(1)
    exchange(2)
    for one in gathers[0]:
        one.forward()
    own_chunk(me.chip(3))
    push_both(2)
    exchange(3)
    own_chunk(mine)
    push_both(3)
    exchange(0)
    for one in gathers[1]:
        one.start()
    for copy in pair[3]:
        copy.wait_recv()
    for copy in across:
        copy.wait_recv()
    for copy in gate_copies:
        copy.wait_recv()

    def summed(which, source):
        total = source[me.dp].astype(F32) + p_recv[which, 0].astype(F32)
        for k in range(3):
            total = total + c_recv[which, k].astype(F32)
        return total

    gate_sum = gate_send[me.dp]
    for k in range(1, 8):
        gate_sum = gate_sum + gate_recv[k]
    lane = lax.broadcasted_iota(jnp.int32, (128, 128), 1)
    chosen = (lane == ids[:, 0:1]) | (lane == ids[:, 1:2])
    grad_gate = jnp.concatenate([gate_sum, jnp.zeros((120, 128), F32)], axis=0).T
    grad_gate = jnp.where(chosen, grad_gate, 0.0)
    probs4 = gates[...]
    grad_logits = probs4 * (grad_gate - jnp.sum(probs4 * grad_gate, axis=-1, keepdims=True))
    grad_logits = grad_logits.astype(BF16)
    router = jnp.concatenate(
        [pvec[0:4, :].astype(BF16), jnp.zeros((124, 768), BF16)], axis=0
    )
    own_n2 = n2p[me.dp]
    small[...] = dot(grad_logits, own_n2, TN)[0:8, :]
    grad_n2 = summed(0, grs) + dot(grad_logits, router)

    def norm_back(values, grad, gain):
        centre = values - jnp.mean(values, axis=-1, keepdims=True)
        rstd = lax.rsqrt(jnp.mean(centre * centre, axis=-1, keepdims=True) + 1e-06)
        xhat = centre * rstd
        u = grad * gain
        back = rstd * (
            u - jnp.mean(u, axis=-1, keepdims=True)
            - xhat * jnp.mean(u * xhat, axis=-1, keepdims=True)
        )
        return back, jnp.sum(grad * xhat, axis=0, keepdims=True), jnp.sum(grad, axis=0, keepdims=True)

    back, gain2, shift2 = norm_back(res[...], grad_n2, pvec[6:7, :])
    small[6:7, :] = gain2
    small[7:8, :] = shift2
    grad_res = back + gp[me.dp].astype(F32)
    grf[...] = grad_res
    first = mult(64 * me.s, 64)
    for i in range(2):
        grall[i, pl.ds(first, 64), :] = grad_res[64 * i : 64 * i + 64].astype(BF16)
    zr = [
        remote(grall.at[:, pl.ds(first, 64), :], grall.at[:, pl.ds(first, 64), :],
               z_send.at[0, k], z_recv.at[0, k], seq=me.zring(k))
        for k in range(1, 4)
    ]
    for copy in zr:
        copy.start()
    o_out[...] = (res[...] + summed(1, outs)).astype(BF16)

    def other_step(k, c, e):
        columns = mix_columns([mixo[k, 2 * c], mixo[k, 2 * c + 1]])
        n2c = n2o[k, pl.ds(2 * c, 2)].reshape(256, 768)
        gc = go[k, pl.ds(2 * c, 2)].reshape(256, 768)
        expert_step(e, n2c, gc, columns)

    for one in gathers[0]:
        one.finish()
    for one in mixers:
        one.arrive()

    def first_plane(t, carry):
        other_step(0, lax.div(t, 4), lax.rem(t, 4))
        return carry

    lax.fori_loop(0, 8, first_plane, 0)
    for one in gathers[1]:
        one.forward()
    for one in gathers[2]:
        one.start()
    lax.fori_loop(8, 16, first_plane, 0)
    for copy in zr:
        copy.wait_recv()

    def ln_step(t, carry):
        i, h = lax.div(t, 2), lax.rem(t, 2)
        at = pl.ds(mult(128 * h, 128), 128)
        rows = xall[i, at, :].astype(F32)
        n1s[i, at, :] = norm_rows(rows, pvec[4:5, :], pvec[5:6, :]).astype(BF16)
        return carry

    lax.fori_loop(0, 4, ln_step, 0)

    def qkv_step(t, carry):
        kind, i = lax.div(t, 2), lax.rem(t, 2)
        w = wqkv[:, pl.ds(mult(768 * kind, 128), 768)]
        qkvs[kind, i] = dot(n1s[i], w).astype(BF16)
        return carry

    lax.fori_loop(0, 6, qkv_step, 0)
    for i in range(2):
        left_buf[0, 256 * i : 256 * i + 256, :] = n1s[i]
        dqkv[3, 256 * i : 256 * i + 256, :] = grall[i]
        n1s[i] = dot(grall[i], wo[...], NT).astype(BF16)

    def attend(t, carry):
        i, j = lax.div(t, 6), lax.rem(t, 6)
        lanes = pl.ds(mult(128 * j, 128), 128)
        rows = pl.ds(mult(256 * i, 256), 256)
        left = lax.broadcasted_iota(jnp.int32, (256, 128), 1) < HEAD

        def both(v):
            zero = jnp.zeros_like(v)
            return jnp.concatenate([jnp.where(left, v, zero), jnp.where(left, zero, v)], axis=0)

        queries = both(qkvs[0, i, :, lanes])
        keys = qkvs[1, i, :, lanes]
        vals = qkvs[2, i, :, lanes]
        grads = both(n1s[i, :, lanes])
        scores = dot(queries, keys, NT) * HEAD ** (-0.5)
        scores = jnp.where(mask[pl.ds(i, 1), :] > 0, scores, -1e30)
        terms = jnp.exp(scores - jnp.max(scores, axis=-1, keepdims=True))
        probs = terms / jnp.sum(terms, axis=-1, keepdims=True)
        low = probs.astype(BF16)
        mixed = dot(low, vals)
        left_buf[1, rows, lanes] = jnp.where(left, mixed[:256], mixed[256:]).astype(BF16)
        dqkv[2, rows, lanes] = dot(low, grads, TN).astype(BF16)
        grad_probs = dot(grads, vals, NT)
        inner = jnp.sum(probs * grad_probs, axis=-1, keepdims=True)
        grad_scores = (probs * (grad_probs - inner)).astype(BF16)
        grad_q = dot(grad_scores, keys)
        scale = HEAD ** (-0.5)
        dqkv[0, rows, lanes] = (jnp.where(left, grad_q[:256], grad_q[256:]) * scale).astype(BF16)
        dqkv[1, rows, lanes] = (dot(grad_scores, queries, TN) * scale).astype(BF16)
        return carry

    lax.fori_loop(0, 12, attend, 0)
    which = lax.div(me.s, 3)

    def quarter(t, carry):
        at = pl.ds(mult(256 * t, 256), 256)
        gq[at, :] = dot(left_buf[which, :, at], dqkv[me.s], TN).astype(BF16)
        return carry

    lax.fori_loop(0, 3, quarter, 0)

    def block(c, core):
        return pl.ds(mult(96 * (2 * c + core), 32), 96)

    pair_q = []
    for k in range(4):
        copy = remote(gq.at[block(me.chip(k), 1 - me.core), :], gq_precv.at[k],
                      q_psend.at[k], q_precv.at[k], dp=partner)
        copy.start()
        pair_q.append(copy)
    for one in gathers[1]:
        one.finish()
    for one in gathers[2]:
        one.forward()
    grad_n1 = jnp.zeros((128, 768), F32)
    for kind in range(3):
        rows = jnp.concatenate(
            [dqkv[kind, pl.ds(256 * i + first, 64), :] for i in range(2)], axis=0
        )
        grad_n1 = grad_n1 + dot(rows, wqkv[:, 768 * kind : 768 * kind + 768], NT)
    tokens = jnp.concatenate([xall[i, pl.ds(first, 64), :] for i in range(2)], axis=0).astype(F32)
    back, gain1, shift1 = norm_back(tokens, grad_n1, pvec[4:5, :])
    o_tok[...] = back + grf[...]
    small[4:5, :] = gain1
    small[5:6, :] = shift1
    across_q = []
    for k in range(1, 4):
        pair_q[k].wait_recv()
        total = gq[block(me.chip(k), me.core), :].astype(F32) + gq_precv[k].astype(F32)
        gq_csend[k - 1] = total.astype(BF16)
        copy = remote(gq_csend.at[k - 1], gq_crecv.at[k - 1], q_csend.at[k], q_crecv.at[k], dp=me.peer(k))
        copy.start()
        across_q.append(copy)
    zs = Spread(me, small, lambda s: small_z.at[s], z_send.at[1], z_recv.at[1], "seq")
    zs.start()
    for one in gathers[2]:
        one.finish()

    reshards = []

    def last_planes(e):
        def step(t, carry):
            other_step(1 + lax.div(t, 4), lax.rem(t, 4), e)
            return carry

        lax.fori_loop(0, 8, step, 0)

        def cast(t, carry):
            at = pl.ds(mult(96 * t, 32), 96)
            gwb[e, at, :] = gwi[e, at, :].astype(BF16)
            return carry

        lax.fori_loop(0, 8, cast, 0)
        for k in range(1, 8):
            t = me.around(k)
            copy = remote(gwb.at[e, pl.ds(mult(96 * t, 32), 96), :],
                          o_gwi.at[e, :, pl.ds(mult(384 * me.dp, 128), 384)],
                          w_send.at[e, k], w_recv.at[e, k], dp=t)
            copy.start()
            reshards.append(copy)
        local = pltpu.make_async_copy(
            gwb.at[e, pl.ds(mult(96 * me.dp, 32), 96), :],
            o_gwi.at[e, :, pl.ds(mult(384 * me.dp, 128), 384)],
            w_send.at[e, 0],
        )
        local.start()
        reshards.append(local)

    last_planes(0)
    pair_q[0].wait_recv()
    total = gq[block(mine, me.core), :].astype(F32) + gq_precv[0].astype(F32)
    for k, copy in enumerate(across_q):
        copy.wait_recv()
        total = total + gq_crecv[k].astype(F32)
    zq[...] = total.astype(BF16)
    zz = Spread(me, zq, lambda s: o_att.at[s], z_send.at[2], z_recv.at[2], "seq")
    zz.start()
    zs.arrive()
    small_sum[...] = small_z[0] + small_z[1] + small_z[2] + small_z[3]
    ps = Spread(me, small_sum, lambda d: small_p.at[d], m_send.at[3], m_recv.at[3], "dp")
    ps.start()
    last_planes(1)
    last_planes(2)
    ps.arrive()
    total = small_p[0]
    for k in range(1, 8):
        total = total + small_p[k]
    o_small[...] = total
    last_planes(3)
    zz.arrive()
    for copy in reshards:
        copy.wait()
    for copies in pair:
        for copy in copies:
            copy.wait_send()
    for copy in across + gate_copies + zr + pair_q + across_q:
        copy.wait_send()
    for one in mixers + [zs, zz, ps]:
        one.drain()


def run_backward(wqkv, wo, xall, pvec, win, gz, gp, n2z, n2p, mixz, mixp, res, gates, wout, mask, ids):
    V = pltpu.VMEM
    return pl.pallas_call(
        backward_kernel,
        out_shape=[
            sds((128, 768)), sds((128, 768), F32), sds((4, 384, 768), F32),
            sds((4, 96, 3072)), sds((4, 96, 768)), sds((8, 768), F32),
        ],
        in_specs=[VM, VM, VM, VM, VM, ANY, VM, ANY, VM, ANY, VM, VM, VM, VM, VM, VM],
        out_specs=[VM, VM, VM, ANY, ANY, VM],
        scratch_shapes=[
            V((3, 8, 128, 768), BF16), V((3, 8, 128, 768), BF16), V((3, 8, 8, 128), F32),
            V((4, 768, 384), F32), V((256, 768), F32), V((256, 768), F32),
            V((8, 128, 768), BF16), V((8, 128, 768), BF16),
            V((2, 4, 128, 768), BF16), V((2, 3, 128, 768), BF16), V((2, 3, 128, 768), BF16),
            V((8, 8, 128), F32), V((8, 8, 128), F32),
            V((2, 256, 768), BF16), V((2, 256, 768), BF16), V((3, 2, 256, 768), BF16),
            V((4, 512, 768), BF16), V((2, 512, 768), BF16),
            V((768, 768), BF16), V((4, 96, 768), BF16), V((3, 96, 768), BF16), V((3, 96, 768), BF16),
            V((96, 768), BF16), V((128, 768), F32), V((4, 768, 384), BF16),
            V((8, 768), F32), V((4, 8, 768), F32), V((8, 8, 768), F32), V((8, 768), F32),
            DMA((6, 8)), DMA((6, 8)), DMA((4, 8)), DMA((4, 8)),
            DMA((2, 4)), DMA((2, 4)), DMA((2, 3)), DMA((2, 3)), DMA((8,)), DMA((8,)),
            DMA((3, 4)), DMA((3, 4)), DMA((4,)), DMA((4,)), DMA((4,)), DMA((4,)),
            DMA((4, 8)), DMA((4, 8)),
        ],
        compiler_params=pltpu.CompilerParams(
            collective_id=1, has_side_effects=True, vmem_limit_bytes=67043328
        ),
        name="backward",
    )(wqkv, wo, xall, pvec, win, gz, gp, n2z, n2p, mixz, mixp, res, gates, wout, mask, ids)


def plane_body(tokens, key_mask, expert_ids, ln1_gain, ln1_bias, w_qkv, w_attn_out, ln2_gain,
               ln2_bias, router, w_in, w_out, cotangent):
    ids = expert_ids.reshape(128, 2)
    pk = pack_small(ln1_gain, ln1_bias, ln2_gain, ln2_bias, router)
    (wqkv, wo, xall, pvec, win, gz, gp, n2z, n2p, mixz, mixp, res, gates) = run_forward(
        tokens, key_mask, ids, pk, w_qkv, w_attn_out, w_in, cotangent.reshape(128, 768)
    )
    out, tok, gwo, gwi, att, small = run_backward(
        wqkv, wo, xall, pvec, win, gz, gp, n2z, n2p, mixz, mixp, res, gates, w_out, key_mask, ids
    )
    own = lax.dynamic_slice_in_dim(small, 96 * lax.axis_index("dp"), 96, axis=1)
    att = att.astype(F32)
    grad_qkv = jnp.concatenate([att[0], att[1], att[2]], axis=1)
    shape = tokens.shape
    return (
        out.reshape(shape), tok.reshape(shape), own[4], own[5], grad_qkv, att[3], own[6], own[7],
        own[0:4].T, gwi.astype(F32), gwo,
    )


TOPK = 2
MOST = 40
MICRO = 2


def layer_norm(inputs, norm_gain, norm_shift):
    centre = inputs - jnp.mean(inputs, axis=-1, keepdims=True)
    spread = jnp.mean(centre * centre, axis=-1, keepdims=True)
    return centre * lax.rsqrt(spread + 1e-06) * norm_gain + norm_shift


def softmax_rows(scores):
    row_max = jnp.max(scores, axis=-1, keepdims=True)
    expo_terms = jnp.exp(scores - row_max)
    return expo_terms / jnp.sum(expo_terms, axis=-1, keepdims=True)


def exact_gelu(inputs):
    return jax.nn.gelu(inputs, approximate=False)


def attention_scores(queries, key_rows, key_valid):
    scores = jnp.einsum(
        "bqhc,bkhc->bhqk", queries, key_rows, preferred_element_type=jnp.float32
    ) * HEAD ** (-0.5)
    return jnp.where(key_valid, scores, -1e30)


def reduce_end(grads):
    shares = (
        lax.psum_scatter(grads[0], "dp", scatter_dimension=0, tiled=True),
        lax.psum_scatter(grads[1], "dp", scatter_dimension=0, tiled=True),
        lax.psum_scatter(grads[2], "dp", scatter_dimension=0, tiled=True),
        lax.psum_scatter(grads[3], "dp", scatter_dimension=0, tiled=True),
        lax.psum_scatter(grads[4], "dp", scatter_dimension=0, tiled=True),
        lax.psum_scatter(grads[5], "dp", scatter_dimension=0, tiled=True),
        lax.psum_scatter(grads[6], "dp", scatter_dimension=0, tiled=True),
        lax.psum_scatter(grads[7], "dp", scatter_dimension=1, tiled=True),
        lax.psum_scatter(grads[8], "dp", scatter_dimension=1, tiled=True),
    )
    quarters = (
        lax.psum_scatter(
            shares[0].astype(jnp.bfloat16), "seq", scatter_dimension=0, tiled=True
        ).astype(jnp.float32),
        lax.psum_scatter(
            shares[1].astype(jnp.bfloat16), "seq", scatter_dimension=0, tiled=True
        ).astype(jnp.float32),
        lax.psum_scatter(
            shares[2].astype(jnp.bfloat16), "seq", scatter_dimension=0, tiled=True
        ).astype(jnp.float32),
        lax.psum_scatter(
            shares[3].astype(jnp.bfloat16), "seq", scatter_dimension=0, tiled=True
        ).astype(jnp.float32),
        lax.psum_scatter(
            shares[4].astype(jnp.bfloat16), "seq", scatter_dimension=0, tiled=True
        ).astype(jnp.float32),
        lax.psum_scatter(
            shares[5].astype(jnp.bfloat16), "seq", scatter_dimension=0, tiled=True
        ).astype(jnp.float32),
        lax.psum_scatter(
            shares[6].astype(jnp.bfloat16), "seq", scatter_dimension=0, tiled=True
        ).astype(jnp.float32),
        lax.psum_scatter(
            shares[7].astype(jnp.bfloat16), "seq", scatter_dimension=1, tiled=True
        ).astype(jnp.float32),
        lax.psum_scatter(
            shares[8].astype(jnp.bfloat16), "seq", scatter_dimension=1, tiled=True
        ).astype(jnp.float32),
    )
    return (
        lax.all_gather(quarters[0].astype(jnp.bfloat16), "seq", axis=0, tiled=True).astype(
            jnp.float32
        ),
        lax.all_gather(quarters[1].astype(jnp.bfloat16), "seq", axis=0, tiled=True).astype(
            jnp.float32
        ),
        lax.all_gather(quarters[2].astype(jnp.bfloat16), "seq", axis=0, tiled=True).astype(
            jnp.float32
        ),
        lax.all_gather(quarters[3].astype(jnp.bfloat16), "seq", axis=0, tiled=True).astype(
            jnp.float32
        ),
        lax.all_gather(quarters[4].astype(jnp.bfloat16), "seq", axis=0, tiled=True).astype(
            jnp.float32
        ),
        lax.all_gather(quarters[5].astype(jnp.bfloat16), "seq", axis=0, tiled=True).astype(
            jnp.float32
        ),
        lax.all_gather(quarters[6].astype(jnp.bfloat16), "seq", axis=0, tiled=True).astype(
            jnp.float32
        ),
        lax.all_gather(quarters[7].astype(jnp.bfloat16), "seq", axis=1, tiled=True).astype(
            jnp.float32
        ),
        lax.all_gather(quarters[8].astype(jnp.bfloat16), "seq", axis=1, tiled=True).astype(
            jnp.float32
        ),
    )


def micro_step(weights, tokens_part, mask_part, routes_part, grad_part):
    (
        norm1_gain,
        norm1_shift,
        qkv_weight,
        proj_weight,
        norm2_gain,
        norm2_shift,
        router_weight,
        inner_weight,
        outer_weight,
    ) = weights
    batch, places, features = tokens_part.shape
    groups = lax.axis_size("seq")
    length = mask_part.shape[1]
    group_width = features // groups
    local_heads = HEADS // groups
    experts = inner_weight.shape[0]
    capacity = batch * MOST
    token_count = batch * places
    gain_one = norm1_gain.astype(jnp.float32)
    shift_one = norm1_shift.astype(jnp.float32)
    gain_two = norm2_gain.astype(jnp.float32)
    shift_two = norm2_shift.astype(jnp.float32)
    inputs = tokens_part.astype(jnp.float32).reshape(token_count, features)
    normed = layer_norm(inputs, gain_one, shift_one).astype(jnp.bfloat16)
    packed = jnp.dot(normed, qkv_weight, preferred_element_type=jnp.float32).astype(jnp.bfloat16)
    packed = packed.reshape(batch, places, 3, groups, group_width)
    spread = lax.all_to_all(packed, "seq", split_axis=3, concat_axis=1, tiled=True)
    queries = spread[:, :, 0, 0].reshape(batch, length, local_heads, HEAD)
    key_rows = spread[:, :, 1, 0].reshape(batch, length, local_heads, HEAD)
    values = spread[:, :, 2, 0].reshape(batch, length, local_heads, HEAD)
    key_valid = mask_part[:, None, None, :] > 0
    scores = attention_scores(queries, key_rows, key_valid)
    row_max = jnp.max(scores, axis=-1, keepdims=True)
    expo_terms = jnp.exp(scores - row_max)
    row_total = jnp.sum(expo_terms, axis=-1, keepdims=True)
    log_total = row_max + jnp.log(row_total)
    attn_probs = (expo_terms / row_total).astype(jnp.bfloat16)
    mixed_heads = jnp.einsum(
        "bhqk,bkhc->bqhc", attn_probs, values, preferred_element_type=jnp.float32
    ).astype(jnp.bfloat16)
    joined = lax.all_to_all(
        mixed_heads.reshape(batch, length, 1, group_width),
        "seq",
        split_axis=1,
        concat_axis=2,
        tiled=True,
    )
    head_rows = joined.reshape(token_count, features)
    residual = inputs + jnp.dot(head_rows, proj_weight, preferred_element_type=jnp.float32)
    normed_two = layer_norm(residual, gain_two, shift_two).astype(jnp.bfloat16)
    gate_probs = softmax_rows(
        jnp.dot(normed_two, router_weight, preferred_element_type=jnp.float32)
    )
    routes = routes_part.reshape(token_count, TOPK)
    pair_experts = routes.reshape(-1)
    expert_range = jnp.arange(experts, dtype=jnp.int32)
    pair_onehot = (pair_experts[:, None] == expert_range[None, :]).astype(jnp.int32)
    earlier = jnp.cumsum(pair_onehot, axis=0) - pair_onehot
    slot_index = pair_experts * capacity + jnp.sum(earlier * pair_onehot, axis=1)
    expert_rows = (
        jnp.zeros((experts * capacity, features), jnp.bfloat16)
        .at[slot_index]
        .set(jnp.repeat(normed_two, TOPK, axis=0))
    )
    expert_rows = expert_rows.reshape(experts, capacity, features)
    hidden = jnp.einsum(
        "ecd,edf->ecf", expert_rows, inner_weight, preferred_element_type=jnp.float32
    )
    active = exact_gelu(hidden).astype(jnp.bfloat16)
    results = jnp.einsum(
        "ecf,efd->ecd", active, outer_weight, preferred_element_type=jnp.float32
    ).reshape(experts * capacity, features)
    picked = results[slot_index].reshape(token_count, TOPK, features)
    mixing = jnp.take_along_axis(gate_probs, routes, axis=1)
    outputs = residual + jnp.sum(mixing[:, :, None] * picked, axis=1)
    grad_out = grad_part.astype(jnp.float32).reshape(token_count, features)
    grad_gate = jnp.sum(grad_out[:, None, :] * picked, axis=2)
    grad_pairs = (
        (mixing[:, :, None] * grad_out[:, None, :])
        .reshape(token_count * TOPK, features)
        .astype(jnp.bfloat16)
    )
    grad_results = (
        jnp.zeros((experts * capacity, features), jnp.bfloat16).at[slot_index].set(grad_pairs)
    )
    grad_results = grad_results.reshape(experts, capacity, features)
    grad_active = jnp.einsum(
        "ecd,efd->ecf", grad_results, outer_weight, preferred_element_type=jnp.float32
    )
    gelu_pull = jax.vjp(exact_gelu, hidden)[1]
    grad_hidden = gelu_pull(grad_active)[0].astype(jnp.bfloat16)
    grad_outer = jnp.einsum(
        "ecf,ecd->efd", active, grad_results, preferred_element_type=jnp.float32
    )
    grad_inner = jnp.einsum(
        "ecd,ecf->edf", expert_rows, grad_hidden, preferred_element_type=jnp.float32
    )
    grad_rows = jnp.einsum(
        "ecf,edf->ecd", grad_hidden, inner_weight, preferred_element_type=jnp.float32
    ).astype(jnp.bfloat16)
    grad_rows = grad_rows.reshape(experts * capacity, features)
    grad_normed_two = jnp.sum(
        grad_rows[slot_index].reshape(token_count, TOPK, features).astype(jnp.float32), axis=1
    )
    chosen = (routes[:, :, None] == expert_range[None, None, :]).astype(jnp.float32)
    grad_gates = jnp.sum(grad_gate[:, :, None] * chosen, axis=1)
    grad_logits = gate_probs * (
        grad_gates - jnp.sum(gate_probs * grad_gates, axis=-1, keepdims=True)
    )
    grad_logits = grad_logits.astype(jnp.bfloat16)
    grad_router = jnp.dot(normed_two.T, grad_logits, preferred_element_type=jnp.float32)
    grad_normed_two = grad_normed_two + jnp.dot(
        grad_logits, router_weight.T, preferred_element_type=jnp.float32
    )
    norm_pull_two = jax.vjp(layer_norm, residual, gain_two, shift_two)[1]
    grad_residual, grad_gain_two, grad_shift_two = norm_pull_two(grad_normed_two)
    grad_residual = grad_residual + grad_out
    grad_attn = grad_residual.astype(jnp.bfloat16)
    grad_proj = jnp.dot(head_rows.T, grad_attn, preferred_element_type=jnp.float32)
    grad_heads = jnp.dot(grad_attn, proj_weight.T, preferred_element_type=jnp.float32).astype(
        jnp.bfloat16
    )
    grad_spread = lax.all_to_all(
        grad_heads.reshape(batch, places, groups, group_width),
        "seq",
        split_axis=2,
        concat_axis=1,
        tiled=True,
    )
    grad_mixed = grad_spread.reshape(batch, length, local_heads, HEAD)
    scores_again = attention_scores(queries, key_rows, key_valid)
    probs_full = jnp.exp(scores_again - log_total)
    probs_low = probs_full.astype(jnp.bfloat16)
    grad_values = jnp.einsum(
        "bhqk,bqhc->bkhc", probs_low, grad_mixed, preferred_element_type=jnp.float32
    )
    grad_probs = jnp.einsum(
        "bqhc,bkhc->bhqk", grad_mixed, values, preferred_element_type=jnp.float32
    )
    grad_scores = probs_full * (
        grad_probs - jnp.sum(probs_full * grad_probs, axis=-1, keepdims=True)
    )
    grad_scores = grad_scores.astype(jnp.bfloat16)
    grad_queries = jnp.einsum(
        "bhqk,bkhc->bqhc", grad_scores, key_rows, preferred_element_type=jnp.float32
    ) * HEAD ** (-0.5)
    grad_keys = jnp.einsum(
        "bhqk,bqhc->bkhc", grad_scores, queries, preferred_element_type=jnp.float32
    ) * HEAD ** (-0.5)
    stacked = jnp.stack([grad_queries, grad_keys, grad_values], axis=2).astype(jnp.bfloat16)
    stacked = stacked.reshape(batch, length, 3, 1, group_width)
    returned = lax.all_to_all(stacked, "seq", split_axis=1, concat_axis=3, tiled=True)
    grad_packed = returned.reshape(token_count, 3 * features)
    grad_qkv = jnp.dot(normed.T, grad_packed, preferred_element_type=jnp.float32)
    grad_normed = jnp.dot(grad_packed, qkv_weight.T, preferred_element_type=jnp.float32)
    norm_pull_one = jax.vjp(layer_norm, inputs, gain_one, shift_one)[1]
    grad_inputs, grad_gain_one, grad_shift_one = norm_pull_one(grad_normed)
    grad_tokens = (grad_inputs + grad_residual).reshape(batch, places, features)
    grads = (
        grad_gain_one,
        grad_shift_one,
        grad_qkv,
        grad_proj,
        grad_gain_two,
        grad_shift_two,
        grad_router,
        grad_inner,
        grad_outer,
    )
    return (outputs.astype(jnp.bfloat16).reshape(batch, places, features), grad_tokens, grads)


def body(
    tokens,
    key_mask,
    expert_ids,
    ln1_gain,
    ln1_bias,
    w_qkv,
    w_attn_out,
    ln2_gain,
    ln2_bias,
    router,
    w_in,
    w_out,
    cotangent,
):
    per_batch = tokens.shape[0] // MICRO
    totals = None
    out_parts = []
    grad_parts = []
    for batch_step in range(MICRO):
        fetched = (
            lax.all_gather(ln1_gain, "dp", axis=0, tiled=True),
            lax.all_gather(ln1_bias, "dp", axis=0, tiled=True),
            lax.all_gather(w_qkv, "dp", axis=0, tiled=True),
            lax.all_gather(w_attn_out, "dp", axis=0, tiled=True),
            lax.all_gather(ln2_gain, "dp", axis=0, tiled=True),
            lax.all_gather(ln2_bias, "dp", axis=0, tiled=True),
            lax.all_gather(router, "dp", axis=0, tiled=True),
            lax.all_gather(w_in, "dp", axis=1, tiled=True),
            lax.all_gather(w_out, "dp", axis=1, tiled=True),
        )
        first = batch_step * per_batch
        last = first + per_batch
        out_part, grad_part, grads = micro_step(
            fetched,
            tokens[first:last],
            key_mask[first:last],
            expert_ids[first:last],
            cotangent[first:last],
        )
        out_parts.append(out_part)
        grad_parts.append(grad_part)
        totals = grads if totals is None else jax.tree.map(jnp.add, totals, grads)
    totals = reduce_end(totals)
    return (
        jnp.concatenate(out_parts, axis=0),
        jnp.concatenate(grad_parts, axis=0),
        totals[0],
        totals[1],
        totals[2],
        totals[3],
        totals[4],
        totals[5],
        totals[6],
        totals[7],
        totals[8],
    )


def solution(mesh):
    placed = (
        P("dp", "seq", None),
        P("dp", None),
        P("dp", "seq", None),
        P("dp"),
        P("dp"),
        P("dp", None),
        P("dp", None),
        P("dp"),
        P("dp"),
        P("dp", None),
        P(None, "dp", None),
        P(None, "dp", None),
        P("dp", "seq", None),
    )
    whole = mesh.shape['dp'] == 8 and mesh.shape['seq'] == 4
    return jax.shard_map(
        plane_body if whole else body,
        mesh=mesh,
        in_specs=placed,
        out_specs=(
            P("dp", "seq", None),
            P("dp", "seq", None),
            P("dp"),
            P("dp"),
            P("dp", None),
            P("dp", None),
            P("dp"),
            P("dp"),
            P("dp", None),
            P(None, "dp", None),
            P(None, "dp", None),
        ),
        check_vma=False,
    )
```

```python
import jax
import jax.numpy as jnp
from jax import lax
from jax.experimental import pallas as pl
from jax.experimental.pallas import tpu as pltpu
from jax.sharding import PartitionSpec as P

MESH = pl.DeviceIdType.MESH
F32, BF16 = jnp.float32, jnp.bfloat16
HEADS = 12
HEAD = 64
NT = (((1,), (1,)), ((), ()))
TN = (((0,), (0,)), ((), ()))


def dot(a, b, dims=(((1,), (0,)), ((), ()))):
    return lax.dot_general(a, b, dims, preferred_element_type=F32)


def mult(value, by):
    return pl.multiple_of(value, by)


class Place:
    def __init__(self):
        self.dp = lax.axis_index("dp")
        self.s = lax.axis_index("seq")
        self.core = lax.rem(self.dp, 2)
        self.x = lax.rem(lax.div(self.dp, 2), 2)
        self.y = lax.div(self.dp, 4)

    def chip(self, k):
        x = 1 - self.x if k % 2 else self.x
        y = 1 - self.y if k // 2 else self.y
        return y * 2 + x

    def peer(self, k):
        return self.chip(k) * 2 + self.core

    def near(self):
        x = self.x + (1 - self.core) * (1 - 2 * self.x)
        y = self.y + self.core * (1 - 2 * self.y)
        return (y * 2 + x) * 2 + self.core

    def far(self):
        x = self.x + self.core * (1 - 2 * self.x)
        y = self.y + (1 - self.core) * (1 - 2 * self.y)
        return (y * 2 + x) * 2 + self.core

    def partner(self):
        return self.dp + 1 - 2 * self.core

    def around(self, k):
        return lax.rem(self.dp + k, 8)

    def zring(self, k):
        return lax.rem(self.s + k, 4)


def entry_barrier(me):
    sem = pltpu.get_barrier_semaphore()
    for k in range(1, 8):
        pl.semaphore_signal(
            sem, inc=1, device_id={"dp": me.around(k)}, device_id_type=MESH
        )
    for k in range(1, 4):
        pl.semaphore_signal(
            sem, inc=1, device_id={"seq": me.zring(k)}, device_id_type=MESH
        )
    pl.semaphore_wait(sem, 10)


def remote(src, dst, send, recv, **where):
    return pltpu.make_async_remote_copy(
        src_ref=src, dst_ref=dst, send_sem=send, recv_sem=recv, device_id=where, device_id_type=MESH
    )


class PlaneGather:
    def __init__(self, me, src, place, send, recv, local=True):
        own = place(me.dp)
        self.sends = [
            remote(src, own, send.at[0], recv.at[0], dp=me.partner()),
            remote(src, own, send.at[1], recv.at[1], dp=me.peer(1)),
            remote(src, own, send.at[2], recv.at[2], dp=me.peer(2)),
        ]
        near = place(me.near())
        self.relay = remote(near, near, send.at[3], recv.at[3], dp=me.far())
        self.onward = []
        for k in range(1, 4):
            there = place(me.peer(k))
            self.onward.append(remote(there, there, send.at[3 + k], recv.at[3 + k], dp=me.partner()))
        self.local = pltpu.make_async_copy(src, own, send.at[7]) if local else None

    def start(self):
        for k in (1, 2, 0):
            self.sends[k].start()
        if self.local is not None:
            self.local.start()

    def forward(self):
        self.sends[1].wait_recv()
        self.sends[2].wait_recv()
        self.relay.start()
        self.onward[0].start()
        self.onward[1].start()

    def diagonal(self):
        self.relay.wait_recv()
        self.onward[2].start()

    def finish(self):
        self.sends[0].wait_recv()
        for copy in self.onward:
            copy.wait_recv()
        for copy in self.sends + self.onward + [self.relay]:
            copy.wait_send()
        if self.local is not None:
            self.local.wait()


class Spread:
    def __init__(self, me, src, place, send, recv, axis, local=True):
        count, step, own = (8, me.around, me.dp) if axis == "dp" else (4, me.zring, me.s)
        self.copies = [
            remote(src, place(own), send.at[k], recv.at[k], **{axis: step(k)})
            for k in range(1, count)
        ]
        self.local = pltpu.make_async_copy(src, place(own), send.at[0]) if local else None

    def start(self):
        for copy in self.copies:
            copy.start()
        if self.local is not None:
            self.local.start()

    def arrive(self):
        for copy in self.copies:
            copy.wait_recv()
        if self.local is not None:
            self.local.wait()

    def drain(self):
        for copy in self.copies:
            copy.wait_send()


class Deal:
    def __init__(self, me, source, place, send, recv):
        self.copies = [
            remote(source(me.zring(k)), place(me.s), send.at[k], recv.at[k], seq=me.zring(k))
            for k in range(1, 4)
        ]

    def start(self):
        for copy in self.copies:
            copy.start()

    def arrive(self):
        for copy in self.copies:
            copy.wait_recv()

    def drain(self):
        for copy in self.copies:
            copy.wait_send()


class RowSum:
    def __init__(self, me, grads, landed, passed, came, send, recv):
        self.me, self.grads, self.landed, self.passed, self.came = me, grads, landed, passed, came
        self.pair = [
            remote(grads.at[self.rows(k, 1 - me.core), :], landed.at[k], send.at[k], recv.at[k], dp=me.partner())
            for k in range(4)
        ]
        self.across = [
            remote(passed.at[k - 1], came.at[k - 1], send.at[3 + k], recv.at[3 + k], dp=me.peer(k))
            for k in range(1, 4)
        ]

    def rows(self, k, core):
        return pl.ds(mult(96 * (2 * self.me.chip(k) + core), 32), 96)

    def start(self):
        for copy in self.pair:
            copy.start()

    def pass_on(self):
        for k in (3, 1, 2):
            self.pair[k].wait_recv()
            kept = self.grads[self.rows(k, self.me.core), :].astype(F32)
            self.passed[k - 1] = (kept + self.landed[k].astype(F32)).astype(BF16)
            self.across[k - 1].start()

    def total(self):
        self.pair[0].wait_recv()
        total = self.grads[self.rows(0, self.me.core), :].astype(F32) + self.landed[0].astype(F32)
        for k in range(3):
            self.across[k].wait_recv()
            total = total + self.came[k].astype(F32)
        return total

    def drain(self):
        for copy in self.pair + self.across:
            copy.wait_send()


def norm_rows(rows, gain, shift):
    centre = rows - jnp.mean(rows, axis=-1, keepdims=True)
    spread = jnp.mean(centre * centre, axis=-1, keepdims=True)
    return centre * lax.rsqrt(spread + 1e-06) * gain + shift


def norm_back(values, grad, gain):
    centre = values - jnp.mean(values, axis=-1, keepdims=True)
    rstd = lax.rsqrt(jnp.mean(centre * centre, axis=-1, keepdims=True) + 1e-06)
    xhat = centre * rstd
    u = grad * gain
    back = rstd * (
        u - jnp.mean(u, axis=-1, keepdims=True)
        - xhat * jnp.mean(u * xhat, axis=-1, keepdims=True)
    )
    return back, jnp.sum(grad * xhat, axis=0, keepdims=True), jnp.sum(grad, axis=0, keepdims=True)


ERFC = (
    0.19786723623605862, 0.190899613780153, 0.23209140755646218, -0.027655803526181202,
    0.6019196159005862, -0.6722756114657328, 0.7990689737520851, -0.3864325349090697,
    0.06451709047710916,
)


def normal_parts(h):
    bell = jnp.exp(-0.5 * (h * h))
    t = 1.0 / (1.0 + (0.35 * 0.5**0.5) * jnp.abs(h))
    poly = jnp.full_like(t, 0.5 * ERFC[8])
    for c in ERFC[7::-1]:
        poly = poly * t + 0.5 * c
    tail = poly * t * bell
    return jnp.where(h < 0, tail, 1.0 - tail), h * bell * 0.3989422804014327


def mix_columns(mixes):
    pad = jnp.zeros((120, 128), F32)
    return jnp.concatenate([jnp.concatenate([m, pad], axis=0).T for m in mixes], axis=0)


def by_head(v):
    lane = lax.broadcasted_iota(jnp.int32, v.shape, 1)
    zero = jnp.zeros_like(v)
    return jnp.concatenate(
        [jnp.where((lane >= HEAD * h) & (lane < HEAD * h + HEAD), v, zero) for h in range(3)], axis=0
    )


def from_heads(v):
    lane = lax.broadcasted_iota(jnp.int32, (256, 256), 1)
    total = jnp.where(lane < HEAD, v[0:256], 0.0)
    for h in range(1, 3):
        own = (lane >= HEAD * h) & (lane < HEAD * h + HEAD)
        total = jnp.where(own, v[256 * h : 256 * h + 256], total)
    return total


def block_kernel(
    x, mask, ids, pk, w3, wo, win, g, wout,
    o_out, o_tok, o_gwo, o_att, o_gwi, o_small, o_gao,
    pkall, pvec, xall, n1, w3a, woa, wina, qkv, pr, hd, hx, res, gates, mixs, n2a, ga, mixa,
    outp, grp, outs, grs, p_recv, c_send, c_recv, gate_send, gate_recv, gwi, gwb,
    grf, ghs, ghx, dqkv, gnp, gnx, gq, gqo, q_land, q_pass, q_came, o_land, o_pass, o_came, zq, zo, zoa,
    small, small_z, small_p, small_sum,
    S, R,
):
    me = Place()
    entry_barrier(me)
    dp, s = me.dp, me.s
    first = mult(64 * s, 64)
    rows96 = lambda d: pl.ds(mult(96 * d, 32), 96)
    small_in = Spread(me, pk, lambda d: pkall.at[d], S.at[10], R.at[10], "dp")
    zx = Spread(me, x, lambda q: xall.at[:, pl.ds(mult(64 * q, 64), 64), :], S.at[16], R.at[16], "seq")
    gather_w3 = PlaneGather(me, w3, lambda d: w3a.at[rows96(d), :], S.at[0], R.at[0])
    gather_wo = PlaneGather(me, wo, lambda d: woa.at[rows96(d), :], S.at[1], R.at[1])
    gather_g = PlaneGather(me, g, lambda d: ga.at[s, d], S.at[2], R.at[2])
    gather_n2 = PlaneGather(me, n2a.at[s, dp], lambda d: n2a.at[s, d], S.at[3], R.at[3], local=False)
    zg = Spread(me, g, lambda q: ga.at[q, dp], S.at[17], R.at[17], "seq", local=False)
    zn = Spread(me, n2a.at[s, dp], lambda q: n2a.at[q, dp], S.at[18], R.at[18], "seq", local=False)
    zm = Spread(me, mixs, lambda q: mixa.at[q, dp], S.at[19], R.at[19], "seq", local=False)
    mix_own = Spread(me, mixs, lambda d: mixa.at[s, d], S.at[11], R.at[11], "dp")
    gathers, mixers = [], []
    for k in range(1, 4):
        q = me.zring(k)
        gathers.append([
            PlaneGather(me, n2a.at[q, dp], lambda d, q=q: n2a.at[q, d], S.at[2 + 2 * k], R.at[2 + 2 * k], local=False),
            PlaneGather(me, ga.at[q, dp], lambda d, q=q: ga.at[q, d], S.at[3 + 2 * k], R.at[3 + 2 * k], local=False),
        ])
        mixers.append(
            Spread(me, mixa.at[q, dp], lambda d, q=q: mixa.at[q, d], S.at[11 + k], R.at[11 + k], "dp", local=False)
        )
    small_in.start()
    zx.start()
    gather_w3.start()
    gather_wo.start()
    gather_g.start()
    small_in.arrive()
    total = jnp.zeros((16, 768), F32)
    row = lax.broadcasted_iota(jnp.int32, (128, 768), 0)
    col = lax.broadcasted_iota(jnp.int32, (128, 768), 1)
    for j in range(8):
        spot = jnp.where((row < 96) & (row + 96 * j == col), 1.0, 0.0).astype(BF16)
        total = total + dot(pkall[j], spot)
    pvec[...] = total
    woa[768:832, :] = jnp.zeros((64, 768), BF16)
    o_gwo[...] = jnp.zeros_like(o_gwo)
    gwi[...] = jnp.zeros_like(gwi)
    gather_w3.forward()
    gather_wo.forward()
    gather_g.forward()
    a2a = []
    for e in range(4):
        p, h = e // 2, e % 2
        for k in range(1, 8):
            t = me.around(k)
            a2a.append(
                remote(
                    win.at[e, :, pl.ds(mult(384 * t, 128), 384)],
                    wina.at[p, rows96(dp), 384 * h : 384 * h + 384],
                    S.at[31 + e, k], R.at[31 + e, k], dp=t,
                )
            )
        a2a.append(
            pltpu.make_async_copy(
                win.at[e, :, pl.ds(mult(384 * dp, 128), 384)],
                wina.at[p, rows96(dp), 384 * h : 384 * h + 384],
                S.at[31 + e, 0],
            )
        )
    for copy in a2a:
        copy.start()
    gather_w3.diagonal()
    gather_wo.diagonal()
    gather_g.diagonal()
    zx.arrive()
    zg.start()

    def ln_step(i, carry):
        n1[i] = norm_rows(xall[i].astype(F32), pvec[4:5, :], pvec[5:6, :]).astype(BF16)
        return carry

    lax.fori_loop(0, 2, ln_step, 0)
    gather_w3.finish()

    def attend(i, carry):
        for kind in range(3):
            qkv[kind, i] = dot(n1[i], w3a[:, 256 * kind : 256 * kind + 256]).astype(BF16)
        scores = dot(by_head(qkv[0, i]), qkv[1, i], NT) * HEAD ** (-0.5)
        scores = jnp.where(mask[pl.ds(i, 1), :] > 0, scores, -1e30)
        terms = jnp.exp(scores - jnp.max(scores, axis=-1, keepdims=True))
        probs = terms / jnp.sum(terms, axis=-1, keepdims=True)
        pr[i] = probs
        hd[i] = from_heads(dot(probs.astype(BF16), qkv[2, i])).astype(BF16)
        return carry

    lax.fori_loop(0, 2, attend, 0)
    deal_heads = Deal(me, lambda q: hd.at[:, pl.ds(mult(64 * q, 64), 64), :], lambda q: hx.at[q], S.at[20], R.at[20])
    deal_heads.start()
    hx[s] = hd[:, pl.ds(first, 64), :]
    gather_wo.finish()
    deal_heads.arrive()
    tokens = xall[:, pl.ds(first, 64), :].reshape(128, 768).astype(F32)
    mixed = tokens
    for q in range(4):
        mixed = mixed + dot(hx[q].reshape(128, 256), woa[192 * q : 192 * q + 256, :])
    res[...] = mixed
    own_n2 = norm_rows(mixed, pvec[6:7, :], pvec[7:8, :]).astype(BF16)
    n2a[s, dp] = own_n2
    gather_n2.start()
    zn.start()
    router = jnp.concatenate([pvec[0:4, :].astype(BF16), jnp.zeros((124, 768), BF16)], axis=0)
    lane = lax.broadcasted_iota(jnp.int32, (128, 128), 1)
    logits = jnp.where(lane < 4, dot(own_n2, router, NT), -1e30)
    terms = jnp.exp(logits - jnp.max(logits, axis=-1, keepdims=True))
    probs4 = terms / jnp.sum(terms, axis=-1, keepdims=True)
    gates[...] = probs4
    chosen = (lane == ids[:, 0:1]) | (lane == ids[:, 1:2])
    mixs[...] = jnp.where(chosen, probs4, 0.0).T[0:8, :]
    mix_own.start()
    zm.start()
    gather_g.finish()
    gather_n2.forward()
    gather_n2.diagonal()
    zg.arrive()
    for copy in a2a:
        copy.wait()
    gather_n2.finish()
    gathers[0][1].start()
    mix_own.arrive()
    zn.arrive()
    gathers[0][0].start()
    zm.arrive()
    for one in mixers:
        one.start()

    def pair_step(p, n2c, gc, columns):
        many = n2c.shape[0]
        lanes = lax.broadcasted_iota(jnp.int32, (many, 128), 1)
        low = jnp.sum(jnp.where(lanes == 2 * p, columns, 0.0), axis=1, keepdims=True)
        high = jnp.sum(jnp.where(lanes == 2 * p + 1, columns, 0.0), axis=1, keepdims=True)
        gate = jnp.where(lax.broadcasted_iota(jnp.int32, (many, 768), 1) < 384, low, high)
        hidden = dot(n2c, wina[p])
        pull = dot(gc, wout[p], NT)
        phi, slope = normal_parts(hidden)
        active = hidden * phi
        taken = (gate * active).astype(BF16)
        grad_hidden = (gate * pull * (phi + slope)).astype(BF16)
        o_gwo[p] += dot(taken, gc, TN)
        gwi[p] += dot(n2c, grad_hidden, TN)
        return active, pull, taken, grad_hidden

    def own_chunk(c):
        columns = mix_columns([mixa[s, 2 * c], mixa[s, 2 * c + 1]])
        n2c = n2a[s, pl.ds(2 * c, 2)].reshape(256, 768)
        gc = ga[s, pl.ds(2 * c, 2)].reshape(256, 768)
        lanes = lax.broadcasted_iota(jnp.int32, (256, 128), 1)
        outp[...] = jnp.zeros_like(outp)
        grp[...] = jnp.zeros_like(grp)

        def step(p, gate_grads):
            active, pull, taken, grad_hidden = pair_step(p, n2c, gc, columns)
            outp[...] += dot(taken, wout[p])
            grp[...] += dot(grad_hidden, wina[p], NT)
            inner = active * pull
            low = jnp.sum(inner[:, :384], axis=1, keepdims=True)
            high = jnp.sum(inner[:, 384:], axis=1, keepdims=True)
            return jnp.where(lanes == 2 * p, low, jnp.where(lanes == 2 * p + 1, high, gate_grads))

        gate_grads = lax.fori_loop(0, 2, step, jnp.zeros((256, 128), F32))
        for b in range(2):
            outs[2 * c + b] = outp[128 * b : 128 * b + 128].astype(BF16)
            grs[2 * c + b] = grp[128 * b : 128 * b + 128].astype(BF16)
            gate_send[2 * c + b] = gate_grads[128 * b : 128 * b + 128].T[0:8, :]

    partner = me.partner()
    mine = me.chip(0)
    pair, across, gate_copies = [], [], []

    def exchange(k):
        c = me.chip(k)
        other = 2 * c + 1 - me.core
        copies = [
            remote(grs.at[other], p_recv.at[0, k], S.at[29, k], R.at[29, k], dp=partner),
            remote(outs.at[other], p_recv.at[1, k], S.at[29, 4 + k], R.at[29, 4 + k], dp=partner),
        ]
        for copy in copies:
            copy.start()
        pair.append(copies)
        for b in range(2):
            if k == 0 and b == 0:
                continue
            target = 2 * c + (me.core if b == 0 else 1 - me.core)
            copy = remote(gate_send.at[target], gate_recv.at[2 * k + b],
                          S.at[28, 2 * k + b], R.at[28, 2 * k + b], dp=target)
            copy.start()
            gate_copies.append(copy)

    def push(k, which, source):
        kept = 2 * me.chip(k) + me.core
        total = source[kept].astype(F32) + p_recv[which, k].astype(F32)
        c_send[which, k - 1] = total.astype(BF16)
        at = 3 * which + k - 1
        copy = remote(c_send.at[which, k - 1], c_recv.at[which, k - 1], S.at[30, at], R.at[30, at], dp=me.peer(k))
        copy.start()
        across.append(copy)

    def push_both(k):
        for copy in pair[len(across) // 2]:
            copy.wait_recv()
        push(k, 0, grs)
        push(k, 1, outs)

    own_chunk(me.chip(3))
    exchange(3)
    own_chunk(me.chip(1))
    push_both(3)
    exchange(1)
    for one in gathers[0]:
        one.forward()
    own_chunk(me.chip(2))
    push_both(1)
    exchange(2)
    for one in gathers[0]:
        one.diagonal()
    own_chunk(mine)
    push_both(2)
    exchange(0)
    for one in gathers[1]:
        one.start()
    for copy in pair[3] + across + gate_copies:
        copy.wait_recv()

    def summed(which, source):
        total = source[dp].astype(F32) + p_recv[which, 0].astype(F32)
        for k in range(3):
            total = total + c_recv[which, k].astype(F32)
        return total

    gate_sum = gate_send[dp]
    for k in range(1, 8):
        gate_sum = gate_sum + gate_recv[k]
    grad_gate = jnp.concatenate([gate_sum, jnp.zeros((120, 128), F32)], axis=0).T
    lane = lax.broadcasted_iota(jnp.int32, (128, 128), 1)
    chosen = (lane == ids[:, 0:1]) | (lane == ids[:, 1:2])
    grad_gate = jnp.where(chosen, grad_gate, 0.0)
    probs4 = gates[...]
    grad_logits = probs4 * (grad_gate - jnp.sum(probs4 * grad_gate, axis=-1, keepdims=True))
    grad_logits = grad_logits.astype(BF16)
    router = jnp.concatenate([pvec[0:4, :].astype(BF16), jnp.zeros((124, 768), BF16)], axis=0)
    small[...] = dot(grad_logits, n2a[s, dp], TN)[0:8, :]
    grad_n2 = summed(0, grs) + dot(grad_logits, router)
    back, gain2, shift2 = norm_back(res[...], grad_n2, pvec[6:7, :])
    small[6:7, :] = gain2
    small[7:8, :] = shift2
    grad_res = back + ga[s, dp].astype(F32)
    grf[...] = grad_res
    grb = grad_res.astype(BF16)
    lane = lax.broadcasted_iota(jnp.int32, (128, 256), 1)
    for q in range(4):
        pulled = dot(grb, woa[192 * q : 192 * q + 256, :], NT)
        ghs[q] = jnp.where(lane < 192, pulled, 0.0).astype(BF16).reshape(2, 64, 256)
    deal_grads = Deal(me, lambda q: ghs.at[q], lambda q: ghx.at[q], S.at[21], R.at[21])
    deal_grads.start()
    ghx[s] = ghs[s]
    for q in range(4):
        gqo[192 * q : 192 * q + 192, :] = dot(hx[q].reshape(128, 256), grb, TN)[0:192].astype(BF16)
    sum_o = RowSum(me, gqo, o_land, o_pass, o_came, S.at[27], R.at[27])
    sum_o.start()
    o_out[...] = (res[...] + summed(1, outs)).astype(BF16)

    def other_step(k, b, p):
        q = lax.rem(s + k, 4)
        columns = mix_columns([mixa[q, 4 * b + j] for j in range(4)])
        n2c = n2a[q, pl.ds(4 * b, 4)].reshape(512, 768)
        gc = ga[q, pl.ds(4 * b, 4)].reshape(512, 768)
        pair_step(p, n2c, gc, columns)

    def near_plane(t, carry):
        other_step(1, lax.div(t, 2), lax.rem(t, 2))
        return carry

    for one in mixers:
        one.arrive()
    for one in gathers[0]:
        one.finish()
    lax.fori_loop(0, 2, near_plane, 0)
    sum_o.pass_on()
    for one in gathers[1]:
        one.forward()
    deal_grads.arrive()

    def attend_back(i, carry):
        grads = by_head(ghx[:, pl.ds(i, 1)].reshape(256, 256))
        queries = by_head(qkv[0, i])
        keys, vals, probs = qkv[1, i], qkv[2, i], pr[i]
        at = pl.ds(mult(256 * i, 256), 256)
        scale = HEAD ** (-0.5)
        dqkv[at, 512:768] = dot(probs.astype(BF16), grads, TN).astype(BF16)
        grad_probs = dot(grads, vals, NT)
        inner = jnp.sum(probs * grad_probs, axis=-1, keepdims=True)
        grad_scores = (probs * (grad_probs - inner)).astype(BF16)
        dqkv[at, 0:256] = (from_heads(dot(grad_scores, keys)) * scale).astype(BF16)
        dqkv[at, 256:512] = (dot(grad_scores, queries, TN) * scale).astype(BF16)
        gnp[i] = dot(dqkv[at, :], w3a[...], NT).astype(BF16)
        return carry

    lax.fori_loop(0, 2, attend_back, 0)
    deal_norm = Deal(me, lambda q: gnp.at[:, pl.ds(mult(64 * q, 64), 64), :], lambda q: gnx.at[q], S.at[22], R.at[22])
    deal_norm.start()
    gnx[s] = gnp[:, pl.ds(first, 64), :]

    def weights(t, carry):
        at = pl.ds(mult(256 * t, 256), 256)
        gq[:, at] = dot(n1[...].reshape(512, 768), dqkv[:, at], TN).astype(BF16)
        return carry

    lax.fori_loop(0, 3, weights, 0)
    sum_q = RowSum(me, gq, q_land, q_pass, q_came, S.at[26], R.at[26])
    sum_q.start()
    for one in gathers[1]:
        one.diagonal()
    for one in gathers[2]:
        one.start()
    lax.fori_loop(2, 4, near_plane, 0)
    sum_q.pass_on()
    zo[...] = sum_o.total().astype(BF16)
    spread_o = Spread(me, zo, lambda q: zoa.at[q], S.at[25], R.at[25], "seq")
    spread_o.start()
    deal_norm.arrive()
    grad_n1 = jnp.zeros((128, 768), F32)
    for q in range(4):
        grad_n1 = grad_n1 + gnx[q].reshape(128, 768).astype(F32)
    tokens = xall[:, pl.ds(first, 64), :].reshape(128, 768).astype(F32)
    back, gain1, shift1 = norm_back(tokens, grad_n1, pvec[4:5, :])
    o_tok[...] = back + grf[...]
    small[4:5, :] = gain1
    small[5:6, :] = shift1
    spread_small = Spread(me, small, lambda q: small_z.at[q], S.at[23], R.at[23], "seq")
    spread_small.start()
    for one in gathers[2]:
        one.forward()
    for one in gathers[1]:
        one.finish()

    reshards = []

    def far_planes(p, k):
        def step(b, carry):
            other_step(k, b, p)
            return carry

        lax.fori_loop(0, 2, step, 0)

    def reshard(p):
        def cast(t, carry):
            at = pl.ds(mult(96 * t, 32), 96)
            gwb[p, at, :] = gwi[p, at, :].astype(BF16)
            return carry

        lax.fori_loop(0, 8, cast, 0)
        for h in range(2):
            e = 2 * p + h
            for k in range(8):
                t = me.around(k) if k else dp
                source = gwb.at[p, rows96(t), 384 * h : 384 * h + 384]
                target = o_gwi.at[e, :, pl.ds(mult(384 * dp, 128), 384)]
                if k:
                    copy = remote(source, target, S.at[35 + e, k], R.at[35 + e, k], dp=t)
                else:
                    copy = pltpu.make_async_copy(source, target, S.at[35 + e, 0])
                copy.start()
                reshards.append(copy)

    far_planes(0, 2)
    zq[...] = sum_q.total().astype(BF16)
    spread_q = Spread(me, zq, lambda q: o_att.at[q], S.at[24], R.at[24], "seq")
    spread_q.start()
    for one in gathers[2]:
        one.diagonal()
    for one in gathers[2]:
        one.finish()
    far_planes(0, 3)
    reshard(0)
    spread_small.arrive()
    small_sum[...] = small_z[0] + small_z[1] + small_z[2] + small_z[3]
    plane_small = Spread(me, small_sum, lambda d: small_p.at[d], S.at[15], R.at[15], "dp")
    plane_small.start()
    far_planes(1, 2)
    far_planes(1, 3)
    reshard(1)
    plane_small.arrive()
    total = small_p[0]
    for k in range(1, 8):
        total = total + small_p[k]
    o_small[...] = total
    spread_o.arrive()
    total = zoa[0].astype(F32)
    for q in range(1, 4):
        total = total + zoa[q].astype(F32)
    o_gao[...] = total
    spread_q.arrive()
    for copy in reshards:
        copy.wait()
    for copies in pair:
        for copy in copies:
            copy.wait_send()
    for copy in across + gate_copies:
        copy.wait_send()
    for one in mixers + [
        small_in, zx, zg, zn, zm, mix_own, deal_heads, deal_grads, deal_norm, sum_o, sum_q,
        spread_o, spread_q, spread_small, plane_small,
    ]:
        one.drain()


VM = pl.BlockSpec(memory_space=pltpu.VMEM)
ANY = pl.BlockSpec(memory_space=pl.ANY)
DMA = pltpu.SemaphoreType.DMA


def sds(shape, dtype=BF16):
    return jax.ShapeDtypeStruct(shape, dtype)


def run_block(x, mask, ids, pk, w3, wo, win, g, wout):
    V = pltpu.VMEM
    return pl.pallas_call(
        block_kernel,
        out_shape=[
            sds((128, 768)), sds((128, 768), F32), sds((2, 768, 768), F32), sds((4, 96, 768)),
            sds((4, 96, 3072)), sds((8, 768), F32), sds((96, 768), F32),
        ],
        in_specs=[ANY, VM, VM, VM, ANY, ANY, ANY, ANY, VM],
        out_specs=[VM, VM, VM, ANY, ANY, VM, VM],
        scratch_shapes=[
            V((8, 16, 128), BF16), V((16, 768), F32), V((2, 256, 768), BF16), V((2, 256, 768), BF16),
            V((768, 768), BF16), V((832, 768), BF16), V((2, 768, 768), BF16), V((3, 2, 256, 256), BF16),
            V((2, 768, 256), F32), V((2, 256, 256), BF16), V((4, 2, 64, 256), BF16), V((128, 768), F32),
            V((128, 128), F32), V((8, 128), F32), V((4, 8, 128, 768), BF16), V((4, 8, 128, 768), BF16),
            V((4, 8, 8, 128), F32),
            V((256, 768), F32), V((256, 768), F32), V((8, 128, 768), BF16), V((8, 128, 768), BF16),
            V((2, 4, 128, 768), BF16), V((2, 3, 128, 768), BF16), V((2, 3, 128, 768), BF16),
            V((8, 8, 128), F32), V((8, 8, 128), F32), V((2, 768, 768), F32), V((2, 768, 768), BF16),
            V((128, 768), F32), V((4, 2, 64, 256), BF16), V((4, 2, 64, 256), BF16), V((512, 768), BF16),
            V((2, 256, 768), BF16), V((4, 2, 64, 768), BF16), V((768, 768), BF16), V((768, 768), BF16),
            V((4, 96, 768), BF16), V((3, 96, 768), BF16), V((3, 96, 768), BF16),
            V((4, 96, 768), BF16), V((3, 96, 768), BF16), V((3, 96, 768), BF16),
            V((96, 768), BF16), V((96, 768), BF16), V((4, 96, 768), BF16),
            V((8, 768), F32), V((4, 8, 768), F32), V((8, 8, 768), F32), V((8, 768), F32),
            DMA((40, 8)), DMA((40, 8)),
        ],
        compiler_params=pltpu.CompilerParams(
            collective_id=0, has_side_effects=True, vmem_limit_bytes=67043328
        ),
        name="block",
    )(x, mask, ids, pk, w3, wo, win, g, wout)


def pack_small(ln1_gain, ln1_bias, ln2_gain, ln2_bias, router):
    rows = jnp.concatenate(
        [router.T, ln1_gain[None], ln1_bias[None], ln2_gain[None], ln2_bias[None]], axis=0
    )
    return jnp.pad(rows, ((0, 8), (0, 32)))


def plane_body(tokens, key_mask, expert_ids, ln1_gain, ln1_bias, w_qkv, w_attn_out, ln2_gain,
               ln2_bias, router, w_in, w_out, cotangent):
    pk = pack_small(ln1_gain, ln1_bias, ln2_gain, ln2_bias, router)
    heads = lax.dynamic_slice_in_dim(w_qkv.reshape(96, 3, 4, 192), lax.axis_index("seq"), 1, axis=2)
    w3 = jnp.pad(heads[:, :, 0], ((0, 0), (0, 0), (0, 64))).reshape(96, 768)
    out, tok, gwo, att, gwi, small, gao = run_block(
        tokens, key_mask, expert_ids.reshape(128, 2), pk, w3, w_attn_out, w_in,
        cotangent.reshape(128, 768), w_out.reshape(2, 768, 768),
    )
    own = lax.dynamic_slice_in_dim(small, 96 * lax.axis_index("dp"), 96, axis=1)
    att = att.reshape(4, 96, 3, 256)[:, :, :, :192].transpose(1, 2, 0, 3).reshape(96, 2304)
    shape = tokens.shape
    return (
        out.reshape(shape), tok.reshape(shape), own[4], own[5], att.astype(F32), gao, own[6], own[7],
        own[0:4].T, gwi.astype(F32), gwo.reshape(4, 384, 768),
    )


TOPK = 2
MOST = 40
MICRO = 2


def layer_norm(inputs, norm_gain, norm_shift):
    centre = inputs - jnp.mean(inputs, axis=-1, keepdims=True)
    spread = jnp.mean(centre * centre, axis=-1, keepdims=True)
    return centre * lax.rsqrt(spread + 1e-06) * norm_gain + norm_shift


def softmax_rows(scores):
    row_max = jnp.max(scores, axis=-1, keepdims=True)
    expo_terms = jnp.exp(scores - row_max)
    return expo_terms / jnp.sum(expo_terms, axis=-1, keepdims=True)


def exact_gelu(inputs):
    return jax.nn.gelu(inputs, approximate=False)


def attention_scores(queries, key_rows, key_valid):
    scores = jnp.einsum(
        "bqhc,bkhc->bhqk", queries, key_rows, preferred_element_type=jnp.float32
    ) * HEAD ** (-0.5)
    return jnp.where(key_valid, scores, -1e30)


def reduce_end(grads):
    shares = (
        lax.psum_scatter(grads[0], "dp", scatter_dimension=0, tiled=True),
        lax.psum_scatter(grads[1], "dp", scatter_dimension=0, tiled=True),
        lax.psum_scatter(grads[2], "dp", scatter_dimension=0, tiled=True),
        lax.psum_scatter(grads[3], "dp", scatter_dimension=0, tiled=True),
        lax.psum_scatter(grads[4], "dp", scatter_dimension=0, tiled=True),
        lax.psum_scatter(grads[5], "dp", scatter_dimension=0, tiled=True),
        lax.psum_scatter(grads[6], "dp", scatter_dimension=0, tiled=True),
        lax.psum_scatter(grads[7], "dp", scatter_dimension=1, tiled=True),
        lax.psum_scatter(grads[8], "dp", scatter_dimension=1, tiled=True),
    )
    quarters = (
        lax.psum_scatter(
            shares[0].astype(jnp.bfloat16), "seq", scatter_dimension=0, tiled=True
        ).astype(jnp.float32),
        lax.psum_scatter(
            shares[1].astype(jnp.bfloat16), "seq", scatter_dimension=0, tiled=True
        ).astype(jnp.float32),
        lax.psum_scatter(
            shares[2].astype(jnp.bfloat16), "seq", scatter_dimension=0, tiled=True
        ).astype(jnp.float32),
        lax.psum_scatter(
            shares[3].astype(jnp.bfloat16), "seq", scatter_dimension=0, tiled=True
        ).astype(jnp.float32),
        lax.psum_scatter(
            shares[4].astype(jnp.bfloat16), "seq", scatter_dimension=0, tiled=True
        ).astype(jnp.float32),
        lax.psum_scatter(
            shares[5].astype(jnp.bfloat16), "seq", scatter_dimension=0, tiled=True
        ).astype(jnp.float32),
        lax.psum_scatter(
            shares[6].astype(jnp.bfloat16), "seq", scatter_dimension=0, tiled=True
        ).astype(jnp.float32),
        lax.psum_scatter(
            shares[7].astype(jnp.bfloat16), "seq", scatter_dimension=1, tiled=True
        ).astype(jnp.float32),
        lax.psum_scatter(
            shares[8].astype(jnp.bfloat16), "seq", scatter_dimension=1, tiled=True
        ).astype(jnp.float32),
    )
    return (
        lax.all_gather(quarters[0].astype(jnp.bfloat16), "seq", axis=0, tiled=True).astype(
            jnp.float32
        ),
        lax.all_gather(quarters[1].astype(jnp.bfloat16), "seq", axis=0, tiled=True).astype(
            jnp.float32
        ),
        lax.all_gather(quarters[2].astype(jnp.bfloat16), "seq", axis=0, tiled=True).astype(
            jnp.float32
        ),
        lax.all_gather(quarters[3].astype(jnp.bfloat16), "seq", axis=0, tiled=True).astype(
            jnp.float32
        ),
        lax.all_gather(quarters[4].astype(jnp.bfloat16), "seq", axis=0, tiled=True).astype(
            jnp.float32
        ),
        lax.all_gather(quarters[5].astype(jnp.bfloat16), "seq", axis=0, tiled=True).astype(
            jnp.float32
        ),
        lax.all_gather(quarters[6].astype(jnp.bfloat16), "seq", axis=0, tiled=True).astype(
            jnp.float32
        ),
        lax.all_gather(quarters[7].astype(jnp.bfloat16), "seq", axis=1, tiled=True).astype(
            jnp.float32
        ),
        lax.all_gather(quarters[8].astype(jnp.bfloat16), "seq", axis=1, tiled=True).astype(
            jnp.float32
        ),
    )


def micro_step(weights, tokens_part, mask_part, routes_part, grad_part):
    (
        norm1_gain,
        norm1_shift,
        qkv_weight,
        proj_weight,
        norm2_gain,
        norm2_shift,
        router_weight,
        inner_weight,
        outer_weight,
    ) = weights
    batch, places, features = tokens_part.shape
    groups = lax.axis_size("seq")
    length = mask_part.shape[1]
    group_width = features // groups
    local_heads = HEADS // groups
    experts = inner_weight.shape[0]
    capacity = batch * MOST
    token_count = batch * places
    gain_one = norm1_gain.astype(jnp.float32)
    shift_one = norm1_shift.astype(jnp.float32)
    gain_two = norm2_gain.astype(jnp.float32)
    shift_two = norm2_shift.astype(jnp.float32)
    inputs = tokens_part.astype(jnp.float32).reshape(token_count, features)
    normed = layer_norm(inputs, gain_one, shift_one).astype(jnp.bfloat16)
    packed = jnp.dot(normed, qkv_weight, preferred_element_type=jnp.float32).astype(jnp.bfloat16)
    packed = packed.reshape(batch, places, 3, groups, group_width)
    spread = lax.all_to_all(packed, "seq", split_axis=3, concat_axis=1, tiled=True)
    queries = spread[:, :, 0, 0].reshape(batch, length, local_heads, HEAD)
    key_rows = spread[:, :, 1, 0].reshape(batch, length, local_heads, HEAD)
    values = spread[:, :, 2, 0].reshape(batch, length, local_heads, HEAD)
    key_valid = mask_part[:, None, None, :] > 0
    scores = attention_scores(queries, key_rows, key_valid)
    row_max = jnp.max(scores, axis=-1, keepdims=True)
    expo_terms = jnp.exp(scores - row_max)
    row_total = jnp.sum(expo_terms, axis=-1, keepdims=True)
    log_total = row_max + jnp.log(row_total)
    attn_probs = (expo_terms / row_total).astype(jnp.bfloat16)
    mixed_heads = jnp.einsum(
        "bhqk,bkhc->bqhc", attn_probs, values, preferred_element_type=jnp.float32
    ).astype(jnp.bfloat16)
    joined = lax.all_to_all(
        mixed_heads.reshape(batch, length, 1, group_width),
        "seq",
        split_axis=1,
        concat_axis=2,
        tiled=True,
    )
    head_rows = joined.reshape(token_count, features)
    residual = inputs + jnp.dot(head_rows, proj_weight, preferred_element_type=jnp.float32)
    normed_two = layer_norm(residual, gain_two, shift_two).astype(jnp.bfloat16)
    gate_probs = softmax_rows(
        jnp.dot(normed_two, router_weight, preferred_element_type=jnp.float32)
    )
    routes = routes_part.reshape(token_count, TOPK)
    pair_experts = routes.reshape(-1)
    expert_range = jnp.arange(experts, dtype=jnp.int32)
    pair_onehot = (pair_experts[:, None] == expert_range[None, :]).astype(jnp.int32)
    earlier = jnp.cumsum(pair_onehot, axis=0) - pair_onehot
    slot_index = pair_experts * capacity + jnp.sum(earlier * pair_onehot, axis=1)
    expert_rows = (
        jnp.zeros((experts * capacity, features), jnp.bfloat16)
        .at[slot_index]
        .set(jnp.repeat(normed_two, TOPK, axis=0))
    )
    expert_rows = expert_rows.reshape(experts, capacity, features)
    hidden = jnp.einsum(
        "ecd,edf->ecf", expert_rows, inner_weight, preferred_element_type=jnp.float32
    )
    active = exact_gelu(hidden).astype(jnp.bfloat16)
    results = jnp.einsum(
        "ecf,efd->ecd", active, outer_weight, preferred_element_type=jnp.float32
    ).reshape(experts * capacity, features)
    picked = results[slot_index].reshape(token_count, TOPK, features)
    mixing = jnp.take_along_axis(gate_probs, routes, axis=1)
    outputs = residual + jnp.sum(mixing[:, :, None] * picked, axis=1)
    grad_out = grad_part.astype(jnp.float32).reshape(token_count, features)
    grad_gate = jnp.sum(grad_out[:, None, :] * picked, axis=2)
    grad_pairs = (
        (mixing[:, :, None] * grad_out[:, None, :])
        .reshape(token_count * TOPK, features)
        .astype(jnp.bfloat16)
    )
    grad_results = (
        jnp.zeros((experts * capacity, features), jnp.bfloat16).at[slot_index].set(grad_pairs)
    )
    grad_results = grad_results.reshape(experts, capacity, features)
    grad_active = jnp.einsum(
        "ecd,efd->ecf", grad_results, outer_weight, preferred_element_type=jnp.float32
    )
    gelu_pull = jax.vjp(exact_gelu, hidden)[1]
    grad_hidden = gelu_pull(grad_active)[0].astype(jnp.bfloat16)
    grad_outer = jnp.einsum(
        "ecf,ecd->efd", active, grad_results, preferred_element_type=jnp.float32
    )
    grad_inner = jnp.einsum(
        "ecd,ecf->edf", expert_rows, grad_hidden, preferred_element_type=jnp.float32
    )
    grad_rows = jnp.einsum(
        "ecf,edf->ecd", grad_hidden, inner_weight, preferred_element_type=jnp.float32
    ).astype(jnp.bfloat16)
    grad_rows = grad_rows.reshape(experts * capacity, features)
    grad_normed_two = jnp.sum(
        grad_rows[slot_index].reshape(token_count, TOPK, features).astype(jnp.float32), axis=1
    )
    chosen = (routes[:, :, None] == expert_range[None, None, :]).astype(jnp.float32)
    grad_gates = jnp.sum(grad_gate[:, :, None] * chosen, axis=1)
    grad_logits = gate_probs * (
        grad_gates - jnp.sum(gate_probs * grad_gates, axis=-1, keepdims=True)
    )
    grad_logits = grad_logits.astype(jnp.bfloat16)
    grad_router = jnp.dot(normed_two.T, grad_logits, preferred_element_type=jnp.float32)
    grad_normed_two = grad_normed_two + jnp.dot(
        grad_logits, router_weight.T, preferred_element_type=jnp.float32
    )
    norm_pull_two = jax.vjp(layer_norm, residual, gain_two, shift_two)[1]
    grad_residual, grad_gain_two, grad_shift_two = norm_pull_two(grad_normed_two)
    grad_residual = grad_residual + grad_out
    grad_attn = grad_residual.astype(jnp.bfloat16)
    grad_proj = jnp.dot(head_rows.T, grad_attn, preferred_element_type=jnp.float32)
    grad_heads = jnp.dot(grad_attn, proj_weight.T, preferred_element_type=jnp.float32).astype(
        jnp.bfloat16
    )
    grad_spread = lax.all_to_all(
        grad_heads.reshape(batch, places, groups, group_width),
        "seq",
        split_axis=2,
        concat_axis=1,
        tiled=True,
    )
    grad_mixed = grad_spread.reshape(batch, length, local_heads, HEAD)
    scores_again = attention_scores(queries, key_rows, key_valid)
    probs_full = jnp.exp(scores_again - log_total)
    probs_low = probs_full.astype(jnp.bfloat16)
    grad_values = jnp.einsum(
        "bhqk,bqhc->bkhc", probs_low, grad_mixed, preferred_element_type=jnp.float32
    )
    grad_probs = jnp.einsum(
        "bqhc,bkhc->bhqk", grad_mixed, values, preferred_element_type=jnp.float32
    )
    grad_scores = probs_full * (
        grad_probs - jnp.sum(probs_full * grad_probs, axis=-1, keepdims=True)
    )
    grad_scores = grad_scores.astype(jnp.bfloat16)
    grad_queries = jnp.einsum(
        "bhqk,bkhc->bqhc", grad_scores, key_rows, preferred_element_type=jnp.float32
    ) * HEAD ** (-0.5)
    grad_keys = jnp.einsum(
        "bhqk,bqhc->bkhc", grad_scores, queries, preferred_element_type=jnp.float32
    ) * HEAD ** (-0.5)
    stacked = jnp.stack([grad_queries, grad_keys, grad_values], axis=2).astype(jnp.bfloat16)
    stacked = stacked.reshape(batch, length, 3, 1, group_width)
    returned = lax.all_to_all(stacked, "seq", split_axis=1, concat_axis=3, tiled=True)
    grad_packed = returned.reshape(token_count, 3 * features)
    grad_qkv = jnp.dot(normed.T, grad_packed, preferred_element_type=jnp.float32)
    grad_normed = jnp.dot(grad_packed, qkv_weight.T, preferred_element_type=jnp.float32)
    norm_pull_one = jax.vjp(layer_norm, inputs, gain_one, shift_one)[1]
    grad_inputs, grad_gain_one, grad_shift_one = norm_pull_one(grad_normed)
    grad_tokens = (grad_inputs + grad_residual).reshape(batch, places, features)
    grads = (
        grad_gain_one,
        grad_shift_one,
        grad_qkv,
        grad_proj,
        grad_gain_two,
        grad_shift_two,
        grad_router,
        grad_inner,
        grad_outer,
    )
    return (outputs.astype(jnp.bfloat16).reshape(batch, places, features), grad_tokens, grads)


def body(
    tokens,
    key_mask,
    expert_ids,
    ln1_gain,
    ln1_bias,
    w_qkv,
    w_attn_out,
    ln2_gain,
    ln2_bias,
    router,
    w_in,
    w_out,
    cotangent,
):
    per_batch = tokens.shape[0] // MICRO
    totals = None
    out_parts = []
    grad_parts = []
    for batch_step in range(MICRO):
        fetched = (
            lax.all_gather(ln1_gain, "dp", axis=0, tiled=True),
            lax.all_gather(ln1_bias, "dp", axis=0, tiled=True),
            lax.all_gather(w_qkv, "dp", axis=0, tiled=True),
            lax.all_gather(w_attn_out, "dp", axis=0, tiled=True),
            lax.all_gather(ln2_gain, "dp", axis=0, tiled=True),
            lax.all_gather(ln2_bias, "dp", axis=0, tiled=True),
            lax.all_gather(router, "dp", axis=0, tiled=True),
            lax.all_gather(w_in, "dp", axis=1, tiled=True),
            lax.all_gather(w_out, "dp", axis=1, tiled=True),
        )
        first = batch_step * per_batch
        last = first + per_batch
        out_part, grad_part, grads = micro_step(
            fetched,
            tokens[first:last],
            key_mask[first:last],
            expert_ids[first:last],
            cotangent[first:last],
        )
        out_parts.append(out_part)
        grad_parts.append(grad_part)
        totals = grads if totals is None else jax.tree.map(jnp.add, totals, grads)
    totals = reduce_end(totals)
    return (
        jnp.concatenate(out_parts, axis=0),
        jnp.concatenate(grad_parts, axis=0),
        totals[0],
        totals[1],
        totals[2],
        totals[3],
        totals[4],
        totals[5],
        totals[6],
        totals[7],
        totals[8],
    )


def solution(mesh):
    placed = (
        P("dp", "seq", None),
        P("dp", None),
        P("dp", "seq", None),
        P("dp"),
        P("dp"),
        P("dp", None),
        P("dp", None),
        P("dp"),
        P("dp"),
        P("dp", None),
        P(None, "dp", None),
        P(None, "dp", None),
        P("dp", "seq", None),
    )
    whole = mesh.shape['dp'] == 8 and mesh.shape['seq'] == 4
    return jax.shard_map(
        plane_body if whole else body,
        mesh=mesh,
        in_specs=placed,
        out_specs=(
            P("dp", "seq", None),
            P("dp", "seq", None),
            P("dp"),
            P("dp"),
            P("dp", None),
            P("dp", None),
            P("dp"),
            P("dp"),
            P("dp", None),
            P(None, "dp", None),
            P(None, "dp", None),
        ),
        check_vma=False,
    )
```

```python
import jax
import jax.numpy as jnp
from jax import lax
from jax.experimental import pallas as pl
from jax.experimental.pallas import tpu as pltpu
from jax.sharding import PartitionSpec as P

MESH = pl.DeviceIdType.MESH
F32, BF16 = jnp.float32, jnp.bfloat16
HEADS = 12
HEAD = 64
NT = (((1,), (1,)), ((), ()))
TN = (((0,), (0,)), ((), ()))


def dot(a, b, dims=(((1,), (0,)), ((), ()))):
    return lax.dot_general(a, b, dims, preferred_element_type=F32)


def mult(value, by):
    return pl.multiple_of(value, by)


class Place:
    def __init__(self):
        self.dp = lax.axis_index("dp")
        self.s = lax.axis_index("seq")
        self.core = lax.rem(self.dp, 2)
        self.x = lax.rem(lax.div(self.dp, 2), 2)
        self.y = lax.div(self.dp, 4)

    def chip(self, k):
        if isinstance(k, int):
            kx, ky = k % 2, k // 2
        else:
            kx, ky = lax.rem(k, 2), lax.div(k, 2)
        x = self.x + kx * (1 - 2 * self.x)
        y = self.y + ky * (1 - 2 * self.y)
        return y * 2 + x

    def peer(self, k):
        return self.chip(k) * 2 + self.core

    def near(self):
        x = self.x + (1 - self.core) * (1 - 2 * self.x)
        y = self.y + self.core * (1 - 2 * self.y)
        return (y * 2 + x) * 2 + self.core

    def far(self):
        x = self.x + self.core * (1 - 2 * self.x)
        y = self.y + (1 - self.core) * (1 - 2 * self.y)
        return (y * 2 + x) * 2 + self.core

    def partner(self):
        return self.dp + 1 - 2 * self.core

    def around(self, k):
        return lax.rem(self.dp + k, 8)

    def plane(self, k):
        low, high = lax.rem(self.s, 2), lax.div(self.s, 2)
        if isinstance(k, int):
            kl, kh = k % 2, k // 2
        else:
            kl, kh = lax.rem(k, 2), lax.div(k, 2)
        return 2 * (high + kh * (1 - 2 * high)) + low + kl * (1 - 2 * low)


def entry_barrier(me):
    sem = pltpu.get_barrier_semaphore()
    for k in range(1, 8):
        pl.semaphore_signal(
            sem, inc=1, device_id={"dp": me.around(k)}, device_id_type=MESH
        )
    for k in range(1, 4):
        pl.semaphore_signal(
            sem, inc=1, device_id={"seq": me.plane(k)}, device_id_type=MESH
        )
    pl.semaphore_wait(sem, 10)


def remote(src, dst, send, recv, **where):
    return pltpu.make_async_remote_copy(
        src_ref=src, dst_ref=dst, send_sem=send, recv_sem=recv, device_id=where, device_id_type=MESH
    )


class PlaneGather:
    def __init__(self, me, src, place, send, recv, local=True):
        own = place(me.dp)
        self.sends = [
            remote(src, own, send.at[0], recv.at[0], dp=me.partner()),
            remote(src, own, send.at[1], recv.at[1], dp=me.peer(1)),
            remote(src, own, send.at[2], recv.at[2], dp=me.peer(2)),
        ]
        near = place(me.near())
        self.relay = remote(near, near, send.at[3], recv.at[3], dp=me.far())
        self.onward = []
        for k in range(1, 4):
            there = place(me.peer(k))
            self.onward.append(remote(there, there, send.at[3 + k], recv.at[3 + k], dp=me.partner()))
        self.local = pltpu.make_async_copy(src, own, send.at[7]) if local else None

    def start(self):
        for k in (1, 2, 0):
            self.sends[k].start()
        if self.local is not None:
            self.local.start()

    def forward(self):
        self.sends[1].wait_recv()
        self.sends[2].wait_recv()
        self.relay.start()
        self.onward[0].start()
        self.onward[1].start()

    def diagonal(self):
        self.relay.wait_recv()
        self.onward[2].start()

    def finish(self):
        self.sends[0].wait_recv()
        for copy in self.onward:
            copy.wait_recv()
        for copy in self.sends + self.onward + [self.relay]:
            copy.wait_send()
        if self.local is not None:
            self.local.wait()


class Spread:
    def __init__(self, me, src, place, send, recv, axis, local=True, first=1):
        count, step, own = (8, me.around, me.dp) if axis == "dp" else (4, me.plane, me.s)
        self.copies = [
            remote(src, place(own), send.at[k], recv.at[k], **{axis: step(k)})
            for k in range(first, count)
        ]
        self.local = pltpu.make_async_copy(src, place(own), send.at[0]) if local else None

    def start(self):
        for copy in self.copies:
            copy.start()
        if self.local is not None:
            self.local.start()

    def arrive(self):
        for copy in self.copies:
            copy.wait_recv()
        if self.local is not None:
            self.local.wait()

    def drain(self):
        for copy in self.copies:
            copy.wait_send()


class Deal:
    def __init__(self, me, source, place, send, recv):
        self.copies = [
            remote(source(me.plane(k)), place(me.s), send.at[k], recv.at[k], seq=me.plane(k))
            for k in range(1, 4)
        ]

    def start(self):
        for copy in self.copies:
            copy.start()

    def arrive(self):
        for copy in self.copies:
            copy.wait_recv()

    def drain(self):
        for copy in self.copies:
            copy.wait_send()


class PlaneHop:
    def __init__(self, me, blocks, send, recv):
        near = me.plane(1)
        self.copies, self.onward = [], []
        for c in range(4):
            d = 2 * c + me.core
            here, there = blocks.at[me.s, d], blocks.at[near, d]
            self.copies.append(remote(here, here, send.at[c], recv.at[c], seq=near))
            self.onward.append(remote(there, there, send.at[4 + c], recv.at[4 + c], dp=me.partner()))

    def start(self):
        for copy in self.copies:
            copy.start()

    def forward(self):
        for copy, onward in zip(self.copies, self.onward):
            copy.wait_recv()
            onward.start()

    def finish(self):
        for copy in self.onward:
            copy.wait_recv()
        for copy in self.copies + self.onward:
            copy.wait_send()


class RowSum:
    def __init__(self, me, grads, landed, passed, came, send, recv):
        self.me, self.grads, self.landed, self.passed, self.came = me, grads, landed, passed, came
        self.pair = [
            remote(grads.at[self.rows(k, 1 - me.core), :], landed.at[k], send.at[k], recv.at[k], dp=me.partner())
            for k in range(4)
        ]
        self.across = [
            remote(passed.at[k - 1], came.at[k - 1], send.at[3 + k], recv.at[3 + k], dp=me.peer(k))
            for k in range(1, 4)
        ]

    def rows(self, k, core):
        return pl.ds(mult(96 * (2 * self.me.chip(k) + core), 32), 96)

    def start(self):
        for copy in self.pair:
            copy.start()

    def pass_on(self):
        for k in (3, 1, 2):
            self.pair[k].wait_recv()
            kept = self.grads[self.rows(k, self.me.core), :].astype(F32)
            self.passed[k - 1] = (kept + self.landed[k].astype(F32)).astype(BF16)
            self.across[k - 1].start()

    def total(self):
        self.pair[0].wait_recv()
        total = self.grads[self.rows(0, self.me.core), :].astype(F32) + self.landed[0].astype(F32)
        for k in range(3):
            self.across[k].wait_recv()
            total = total + self.came[k].astype(F32)
        return total

    def drain(self):
        for copy in self.pair + self.across:
            copy.wait_send()


def norm_rows(rows, gain, shift):
    centre = rows - jnp.mean(rows, axis=-1, keepdims=True)
    spread = jnp.mean(centre * centre, axis=-1, keepdims=True)
    return centre * lax.rsqrt(spread + 1e-06) * gain + shift


def norm_back(values, grad, gain):
    centre = values - jnp.mean(values, axis=-1, keepdims=True)
    rstd = lax.rsqrt(jnp.mean(centre * centre, axis=-1, keepdims=True) + 1e-06)
    xhat = centre * rstd
    u = grad * gain
    back = rstd * (
        u - jnp.mean(u, axis=-1, keepdims=True)
        - xhat * jnp.mean(u * xhat, axis=-1, keepdims=True)
    )
    return back, jnp.sum(grad * xhat, axis=0, keepdims=True), jnp.sum(grad, axis=0, keepdims=True)


ERFC = (
    0.19786723623605862, 0.190899613780153, 0.23209140755646218, -0.027655803526181202,
    0.6019196159005862, -0.6722756114657328, 0.7990689737520851, -0.3864325349090697,
    0.06451709047710916,
)


def normal_parts(h):
    bell = jnp.exp(-0.5 * (h * h))
    t = 1.0 / (1.0 + (0.35 * 0.5**0.5) * jnp.abs(h))
    poly = jnp.full_like(t, 0.5 * ERFC[8])
    for c in ERFC[7::-1]:
        poly = poly * t + 0.5 * c
    tail = poly * t * bell
    return jnp.where(h < 0, tail, 1.0 - tail), h * bell * 0.3989422804014327


def mix_columns(mixes):
    pad = jnp.zeros((120, 128), F32)
    return jnp.concatenate([jnp.concatenate([m, pad], axis=0).T for m in mixes], axis=0)


def by_head(v):
    lane = lax.broadcasted_iota(jnp.int32, v.shape, 1)
    zero = jnp.zeros_like(v)
    return jnp.concatenate(
        [jnp.where((lane >= HEAD * h) & (lane < HEAD * h + HEAD), v, zero) for h in range(3)], axis=0
    )


def from_heads(v):
    lane = lax.broadcasted_iota(jnp.int32, (256, 256), 1)
    total = jnp.where(lane < HEAD, v[0:256], 0.0)
    for h in range(1, 3):
        own = (lane >= HEAD * h) & (lane < HEAD * h + HEAD)
        total = jnp.where(own, v[256 * h : 256 * h + 256], total)
    return total


def block_kernel(
    x, mask, ids, pk, w3, wo, win, g, wout,
    o_out, o_tok, o_gwo, o_att, o_gwi, o_small, o_gao,
    pkall, pvec, xall, xown, w3a, woa, wina, qkv, pr, hd, hx, res, gates, mixs, n2a, ga, mixa,
    acc, pulls, sums, p_recv, c_send, c_recv, gate_send, gate_recv, gwi, gwb,
    ghs, ghx, gnp, gnx, gq, q_land, q_pass, q_came, o_land, o_pass, o_came, zq, zo, zoa,
    small, small_z, small_p, small_sum,
    S, R,
):
    me = Place()
    entry_barrier(me)
    dp, s = me.dp, me.s
    first = mult(64 * s, 64)
    rows96 = lambda d: pl.ds(mult(96 * d, 32), 96)
    small_in = Spread(me, pk, lambda d: pkall.at[d], S.at[10], R.at[10], "dp")
    zx = Spread(me, x, lambda q: xall.at[:, pl.ds(mult(64 * q, 64), 64), :], S.at[16], R.at[16], "seq")
    gather_w3 = PlaneGather(me, w3, lambda d: w3a.at[rows96(d), :], S.at[0], R.at[0])
    gather_wo = PlaneGather(me, wo, lambda d: woa.at[rows96(d), :], S.at[1], R.at[1])
    gather_g = PlaneGather(me, g, lambda d: ga.at[s, d], S.at[2], R.at[2])
    gather_n2 = PlaneGather(me, n2a.at[s, dp], lambda d: n2a.at[s, d], S.at[3], R.at[3], local=False)
    zg = Spread(me, g, lambda q: ga.at[q, dp], S.at[17], R.at[17], "seq", local=False, first=2)
    zn = Spread(me, n2a.at[s, dp], lambda q: n2a.at[q, dp], S.at[18], R.at[18], "seq", local=False, first=2)
    zm = Spread(me, mixs, lambda q: mixa.at[q, dp], S.at[19], R.at[19], "seq", local=False)
    mix_own = Spread(me, mixs, lambda d: mixa.at[s, d], S.at[11], R.at[11], "dp")
    hop_n2, hop_g = PlaneHop(me, n2a, S.at[4], R.at[4]), PlaneHop(me, ga, S.at[5], R.at[5])
    gathers, mixers = [None], []
    for k in range(1, 4):
        q = me.plane(k)
        if k > 1:
            gathers.append([
                PlaneGather(me, n2a.at[q, dp], lambda d, q=q: n2a.at[q, d], S.at[2 + 2 * k], R.at[2 + 2 * k], local=False),
                PlaneGather(me, ga.at[q, dp], lambda d, q=q: ga.at[q, d], S.at[3 + 2 * k], R.at[3 + 2 * k], local=False),
            ])
        mixers.append(
            Spread(me, mixa.at[q, dp], lambda d, q=q: mixa.at[q, d], S.at[11 + k], R.at[11 + k], "dp", local=False)
        )
    small_in.start()
    zx.start()
    gather_w3.start()
    gather_wo.start()
    gather_g.start()
    small_in.arrive()
    total = jnp.zeros((16, 768), F32)
    row = lax.broadcasted_iota(jnp.int32, (128, 768), 0)
    col = lax.broadcasted_iota(jnp.int32, (128, 768), 1)
    for j in range(8):
        spot = jnp.where((row < 96) & (row + 96 * j == col), 1.0, 0.0).astype(BF16)
        total = total + dot(pkall[j], spot)
    pvec[...] = total
    woa[768:832, :] = jnp.zeros((64, 768), BF16)
    o_gwo[...] = jnp.zeros_like(o_gwo)
    gwi[...] = jnp.zeros_like(gwi)
    gather_w3.forward()
    gather_wo.forward()
    gather_g.forward()
    a2a = []
    for e in range(4):
        p, h = e // 2, e % 2
        for k in range(1, 8):
            t = me.around(k)
            a2a.append(
                remote(
                    win.at[e, :, pl.ds(mult(384 * t, 128), 384)],
                    wina.at[p, rows96(dp), 384 * h : 384 * h + 384],
                    S.at[31 + e, k], R.at[31 + e, k], dp=t,
                )
            )
        a2a.append(
            pltpu.make_async_copy(
                win.at[e, :, pl.ds(mult(384 * dp, 128), 384)],
                wina.at[p, rows96(dp), 384 * h : 384 * h + 384],
                S.at[31 + e, 0],
            )
        )
    for copy in a2a[:16]:
        copy.start()
    acc[...] = jnp.zeros_like(acc)
    pulls[...] = jnp.zeros_like(pulls)
    gather_w3.diagonal()
    gather_wo.diagonal()
    gather_g.diagonal()
    zx.arrive()

    xown[...] = xall[:, pl.ds(first, 64), :]

    def ln_step(i, carry):
        xall[i] = norm_rows(xall[i].astype(F32), pvec[4:5, :], pvec[5:6, :]).astype(BF16)
        return carry

    lax.fori_loop(0, 2, ln_step, 0)
    gather_w3.finish()

    def attend(i, carry):
        for kind in range(3):
            qkv[kind, i] = dot(xall[i], w3a[:, 256 * kind : 256 * kind + 256]).astype(BF16)
        scores = dot(by_head(qkv[0, i]), qkv[1, i], NT) * HEAD ** (-0.5)
        scores = jnp.where(mask[pl.ds(i, 1), :] > 0, scores, -1e30)
        terms = jnp.exp(scores - jnp.max(scores, axis=-1, keepdims=True))
        probs = terms / jnp.sum(terms, axis=-1, keepdims=True)
        pr[i] = probs
        hd[i] = from_heads(dot(probs.astype(BF16), qkv[2, i])).astype(BF16)
        return carry

    lax.fori_loop(0, 2, attend, 0)
    deal_heads = Deal(me, lambda q: hd.at[:, pl.ds(mult(64 * q, 64), 64), :], lambda q: hx.at[q], S.at[20], R.at[20])
    deal_heads.start()
    hx[s] = hd[:, pl.ds(first, 64), :]
    gather_wo.finish()
    deal_heads.arrive()
    zg.start()
    tokens = xown[...].reshape(128, 768).astype(F32)
    mixed = tokens
    for q in range(4):
        mixed = mixed + dot(hx[q].reshape(128, 256), woa[192 * q : 192 * q + 256, :])
    res[...] = mixed
    own_n2 = norm_rows(mixed, pvec[6:7, :], pvec[7:8, :]).astype(BF16)
    n2a[s, dp] = own_n2
    gather_n2.start()
    zn.start()
    for copy in a2a[16:]:
        copy.start()
    router = jnp.concatenate([pvec[0:4, :].astype(BF16), jnp.zeros((124, 768), BF16)], axis=0)
    lane = lax.broadcasted_iota(jnp.int32, (128, 128), 1)
    logits = jnp.where(lane < 4, dot(own_n2, router, NT), -1e30)
    terms = jnp.exp(logits - jnp.max(logits, axis=-1, keepdims=True))
    probs4 = terms / jnp.sum(terms, axis=-1, keepdims=True)
    gates[...] = probs4
    chosen = (lane == ids[:, 0:1]) | (lane == ids[:, 1:2])
    mixs[...] = jnp.where(chosen, probs4, 0.0).T[0:8, :]
    mix_own.start()
    zm.start()
    gather_g.finish()
    hop_g.start()
    gather_n2.forward()
    gather_n2.diagonal()
    for copy in a2a[:16]:
        copy.wait()
    gather_n2.finish()
    hop_n2.start()
    mix_own.arrive()

    def pair_step(p, n2c, gc, columns):
        many = n2c.shape[0]
        lanes = lax.broadcasted_iota(jnp.int32, (many, 128), 1)
        low = jnp.sum(jnp.where(lanes == 2 * p, columns, 0.0), axis=1, keepdims=True)
        high = jnp.sum(jnp.where(lanes == 2 * p + 1, columns, 0.0), axis=1, keepdims=True)
        gate = jnp.where(lax.broadcasted_iota(jnp.int32, (many, 768), 1) < 384, low, high)
        hidden = dot(n2c, wina[p])
        pull = dot(gc, wout[p], NT)
        phi, slope = normal_parts(hidden)
        active = hidden * phi
        taken = (gate * active).astype(BF16)
        grad_hidden = (gate * pull * (phi + slope)).astype(BF16)
        gwi[p] += dot(n2c, grad_hidden, TN)
        return active, pull, taken, grad_hidden

    def pair_copy(k, which):
        other = 2 * me.chip(k) + 1 - me.core
        at = 4 * which + k
        return remote(sums.at[which, other], p_recv.at[which, k], S.at[29, at], R.at[29, at], dp=me.partner())

    def across_copy(k, which):
        at = 3 * which + k - 1
        return remote(
            c_send.at[which, k - 1], c_recv.at[which, k - 1], S.at[30, at], R.at[30, at], dp=me.peer(k)
        )

    def gate_copy(k, b):
        target = 2 * me.chip(k) + (1 - me.core if b else me.core)
        at = 2 * k + b
        return remote(gate_send.at[target], gate_recv.at[at], S.at[28, at], R.at[28, at], dp=target)

    def push(k, which):
        pair_copy(k, which).wait_recv()
        total = sums[which, 2 * me.chip(k) + me.core].astype(F32) + p_recv[which, k].astype(F32)
        c_send[which, k - 1] = total.astype(BF16)
        across_copy(k, which).start()

    def own_step(t, carry):
        p, i = lax.div(t, 4), lax.rem(t, 4)
        k = 3 - i
        c = me.chip(k)

        @pl.when(t == 4)
        def _():
            for copy in a2a[16:]:
                copy.wait()
            zg.arrive()
            gathers[1][1].start()
            zn.arrive()
            gathers[1][0].start()
            zm.arrive()
            for one in mixers:
                one.start()

        @pl.when(t == 6)
        def _():
            hop_g.forward()

        columns = mix_columns([mixa[s, 2 * c], mixa[s, 2 * c + 1]])
        n2c = n2a[s, pl.ds(2 * c, 2)].reshape(256, 768)
        gc = ga[s, pl.ds(2 * c, 2)].reshape(256, 768)
        active, pull, taken, grad_hidden = pair_step(p, n2c, gc, columns)
        acc[0, i] += dot(grad_hidden, wina[p], NT)
        acc[1, i] += dot(taken, wout[p])
        o_gwo[p] += dot(taken, gc, TN)
        inner = active * pull
        low = jnp.sum(inner[:, :384], axis=1, keepdims=True)
        high = jnp.sum(inner[:, 384:], axis=1, keepdims=True)
        lanes = lax.broadcasted_iota(jnp.int32, (256, 128), 1)
        pulls[i] = jnp.where(lanes == 2 * p, low, jnp.where(lanes == 2 * p + 1, high, pulls[i]))

        @pl.when(p == 1)
        def _():
            for b in range(2):
                sums[0, 2 * c + b] = acc[0, i, 128 * b : 128 * b + 128].astype(BF16)
                sums[1, 2 * c + b] = acc[1, i, 128 * b : 128 * b + 128].astype(BF16)
                gate_send[2 * c + b] = pulls[i, 128 * b : 128 * b + 128].T[0:8, :]
            pair_copy(k, 0).start()
            gate_copy(k, 1).start()

        @pl.when((p == 1) & (k > 0))
        def _():
            gate_copy(k, 0).start()

        @pl.when(t > 4)
        def _():
            push(k + 1, 0)

        return carry

    lax.fori_loop(0, 8, own_step, 0)
    pair_copy(0, 0).wait_recv()
    for k in range(4):
        pair_copy(k, 1).start()
    for k in range(4):
        if k:
            across_copy(k, 0).wait_recv()
            gate_copy(k, 0).wait_recv()
        gate_copy(k, 1).wait_recv()
    hop_n2.forward()

    def summed(which):
        total = sums[which, dp].astype(F32) + p_recv[which, 0].astype(F32)
        for k in range(3):
            total = total + c_recv[which, k].astype(F32)
        return total

    gate_sum = gate_send[dp]
    for k in range(1, 8):
        gate_sum = gate_sum + gate_recv[k]
    grad_gate = jnp.concatenate([gate_sum, jnp.zeros((120, 128), F32)], axis=0).T
    lane = lax.broadcasted_iota(jnp.int32, (128, 128), 1)
    chosen = (lane == ids[:, 0:1]) | (lane == ids[:, 1:2])
    grad_gate = jnp.where(chosen, grad_gate, 0.0)
    probs4 = gates[...]
    grad_logits = probs4 * (grad_gate - jnp.sum(probs4 * grad_gate, axis=-1, keepdims=True))
    grad_logits = grad_logits.astype(BF16)
    router = jnp.concatenate([pvec[0:4, :].astype(BF16), jnp.zeros((124, 768), BF16)], axis=0)
    small[...] = dot(grad_logits, n2a[s, dp], TN)[0:8, :]
    grad_n2 = summed(0) + dot(grad_logits, router)
    back, gain2, shift2 = norm_back(res[...], grad_n2, pvec[6:7, :])
    small[6:7, :] = gain2
    small[7:8, :] = shift2
    grad_res = back + ga[s, dp].astype(F32)
    o_tok[...] = grad_res
    grb = grad_res.astype(BF16)
    lane = lax.broadcasted_iota(jnp.int32, (128, 256), 1)
    for q in range(4):
        pulled = dot(grb, woa[192 * q : 192 * q + 256, :], NT)
        ghs[q] = jnp.where(lane < 192, pulled, 0.0).astype(BF16).reshape(2, 64, 256)
    deal_grads = Deal(me, lambda q: ghs.at[q], lambda q: ghx.at[q], S.at[21], R.at[21])
    deal_grads.start()
    ghx[s] = ghs[s]
    for q in range(4):
        gwb[192 * q : 192 * q + 192, :] = dot(hx[q].reshape(128, 256), grb, TN)[0:192].astype(BF16)
    sum_o = RowSum(me, gwb, o_land, o_pass, o_came, S.at[27], R.at[27])
    sum_o.start()
    for one in gathers[1]:
        one.forward()
    for one in gathers[2]:
        one.start()
    for one in mixers:
        one.arrive()
    hop_g.finish()
    hop_n2.finish()

    def attend_back(i, carry):
        grads = by_head(ghx[:, pl.ds(i, 1)].reshape(256, 256))
        queries = by_head(qkv[0, i])
        keys, vals, probs = qkv[1, i], qkv[2, i], pr[i]
        at = pl.ds(2 * i, 2)
        scale = HEAD ** (-0.5)
        p_recv[0, at, :, 512:768] = dot(probs.astype(BF16), grads, TN).astype(BF16).reshape(2, 128, 256)
        grad_probs = dot(grads, vals, NT)
        inner = jnp.sum(probs * grad_probs, axis=-1, keepdims=True)
        grad_scores = (probs * (grad_probs - inner)).astype(BF16)
        grad_q = (from_heads(dot(grad_scores, keys)) * scale).astype(BF16)
        p_recv[0, at, :, 0:256] = grad_q.reshape(2, 128, 256)
        grad_k = (dot(grad_scores, queries, TN) * scale).astype(BF16)
        p_recv[0, at, :, 256:512] = grad_k.reshape(2, 128, 256)
        gnp[i] = dot(p_recv[0, at].reshape(256, 768), w3a[...], NT).astype(BF16)
        return carry

    deal_norm = Deal(me, lambda q: gnp.at[:, pl.ds(mult(64 * q, 64), 64), :], lambda q: gnx.at[q], S.at[22], R.at[22])

    def weights(t, carry):
        at = pl.ds(mult(256 * t, 256), 256)
        gq[:, at] = dot(xall[...].reshape(512, 768), p_recv[0, :, :, at].reshape(512, 256), TN).astype(BF16)
        return carry

    sum_q = RowSum(me, gq, q_land, q_pass, q_came, S.at[26], R.at[26])
    spread_o = Spread(me, zo, lambda q: zoa.at[q], S.at[25], R.at[25], "seq")
    spread_q = Spread(me, zq, lambda q: o_att.at[q], S.at[24], R.at[24], "seq")
    spread_small = Spread(me, small, lambda q: small_z.at[q], S.at[23], R.at[23], "seq")
    plane_small = Spread(me, small_sum, lambda d: small_p.at[d], S.at[15], R.at[15], "dp")

    def reshard_copies(p):
        copies = []
        for h in range(2):
            e = 2 * p + h
            for k in range(8):
                t = me.around(k) if k else dp
                source = gwb.at[rows96(t), 384 * h : 384 * h + 384]
                target = o_gwi.at[e, :, pl.ds(mult(384 * dp, 128), 384)]
                if k:
                    copies.append(remote(source, target, S.at[35 + e, k], R.at[35 + e, k], dp=t))
                else:
                    copies.append(pltpu.make_async_copy(source, target, S.at[35 + e, 0]))
        return copies

    reshards = [reshard_copies(0), reshard_copies(1)]

    def reshard(p):
        def cast(t, carry):
            at = pl.ds(mult(96 * t, 32), 96)
            gwb[at, :] = gwi[p, at, :].astype(BF16)
            return carry

        lax.fori_loop(0, 8, cast, 0)
        for copy in reshards[p]:
            copy.start()

    def stage_1():
        sum_o.pass_on()
        for k in range(1, 4):
            push(k, 1)
        for one in gathers[1]:
            one.diagonal()

    def stage_2():
        deal_grads.arrive()
        lax.fori_loop(0, 2, attend_back, 0)
        deal_norm.start()
        gnx[s] = gnp[:, pl.ds(first, 64), :]
        lax.fori_loop(0, 3, weights, 0)
        sum_q.start()
        for one in gathers[2]:
            one.forward()

    def stage_3():
        sum_q.pass_on()
        for one in gathers[2]:
            one.diagonal()
        zo[...] = sum_o.total().astype(BF16)
        spread_o.start()

    def stage_4():
        for one in gathers[1]:
            one.finish()

    def stage_5():
        deal_norm.arrive()
        grad_n1 = jnp.zeros((128, 768), F32)
        for q in range(4):
            grad_n1 = grad_n1 + gnx[q].reshape(128, 768).astype(F32)
        tokens = xown[...].reshape(128, 768).astype(F32)
        back, gain1, shift1 = norm_back(tokens, grad_n1, pvec[4:5, :])
        o_tok[...] = back + o_tok[...]
        small[4:5, :] = gain1
        small[5:6, :] = shift1
        spread_small.start()

    def stage_6():
        zq[...] = sum_q.total().astype(BF16)
        spread_q.start()
        for one in gathers[2]:
            one.finish()

    def stage_7():
        pair_copy(0, 1).wait_recv()
        for k in range(1, 4):
            across_copy(k, 1).wait_recv()
        o_out[...] = (res[...] + summed(1)).astype(BF16)

    def stage_8():
        sum_o.drain()
        for which in range(2):
            for k in range(4):
                pair_copy(k, which).wait_send()
        reshard(0)
        spread_small.arrive()
        small_sum[...] = small_z[0] + small_z[1] + small_z[2] + small_z[3]
        plane_small.start()

    stages = (stage_1, stage_2, stage_3, stage_4, stage_5, stage_6, stage_7, stage_8)

    def other_step(t, carry):
        for at, stage in enumerate(stages):
            pl.when(t == at + 1)(stage)
        far = lax.div(t, 4)
        inner = lax.rem(t, 4)
        p = jnp.where(far == 0, lax.rem(t, 2), far - 1)
        q = me.plane(jnp.where(far == 0, 1, 2 + lax.div(inner, 2)))
        b = jnp.where(far == 0, lax.div(inner, 2), lax.rem(t, 2))
        columns = mix_columns([mixa[q, 4 * b + j] for j in range(4)])
        n2c = n2a[q, pl.ds(4 * b, 4)].reshape(512, 768)
        gc = ga[q, pl.ds(4 * b, 4)].reshape(512, 768)
        taken = pair_step(p, n2c, gc, columns)[2]

        @pl.when(t < 4)
        def _():
            o_gwo[p] += dot(taken, gc, TN)

        @pl.when((t >= 4) & (t < 8))
        def _():
            acc[lax.div(inner, 2), pl.ds(2 * lax.rem(inner, 2), 2)] = taken.astype(F32).reshape(2, 256, 768)

        @pl.when(t >= 8)
        def _():
            sums[lax.div(inner, 2), pl.ds(4 * lax.rem(inner, 2), 4)] = taken.reshape(4, 128, 768)

        return carry

    lax.fori_loop(0, 12, other_step, 0)
    for copy in reshards[0]:
        copy.wait()
    reshard(1)

    def last_products(j, carry):
        q = me.plane(2 + lax.div(j, 2))
        gc = ga[q, pl.ds(4 * lax.rem(j, 2), 4)].reshape(512, 768)
        h, b = lax.div(j, 2), lax.rem(j, 2)
        early = acc[h, pl.ds(2 * b, 2)].reshape(512, 768).astype(BF16)
        o_gwo[0] += dot(early, gc, TN)
        taken = sums[h, pl.ds(4 * b, 4)].reshape(512, 768)
        o_gwo[1] += dot(taken, gc, TN)
        return carry

    lax.fori_loop(0, 4, last_products, 0)
    plane_small.arrive()
    total = small_p[0]
    for k in range(1, 8):
        total = total + small_p[k]
    o_small[...] = total
    spread_o.arrive()
    total = zoa[0].astype(F32)
    for q in range(1, 4):
        total = total + zoa[q].astype(F32)
    o_gao[...] = total
    spread_q.arrive()
    for copy in reshards[1]:
        copy.wait()
    for which in range(2):
        for k in range(1, 4):
            across_copy(k, which).wait_send()
    for k in range(4):
        if k:
            gate_copy(k, 0).wait_send()
        gate_copy(k, 1).wait_send()
    for one in mixers + [
        small_in, zx, zg, zn, zm, mix_own, deal_heads, deal_grads, deal_norm, sum_q,
        spread_o, spread_q, spread_small, plane_small,
    ]:
        one.drain()


VM = pl.BlockSpec(memory_space=pltpu.VMEM)
ANY = pl.BlockSpec(memory_space=pl.ANY)
DMA = pltpu.SemaphoreType.DMA


def sds(shape, dtype=BF16):
    return jax.ShapeDtypeStruct(shape, dtype)


def run_block(x, mask, ids, pk, w3, wo, win, g, wout):
    V = pltpu.VMEM
    return pl.pallas_call(
        block_kernel,
        out_shape=[
            sds((128, 768)), sds((128, 768), F32), sds((2, 768, 768), F32), sds((4, 96, 768)),
            sds((4, 96, 3072)), sds((8, 768), F32), sds((96, 768), F32),
        ],
        in_specs=[ANY, VM, VM, VM, ANY, ANY, ANY, ANY, VM],
        out_specs=[VM, VM, VM, ANY, ANY, VM, VM],
        scratch_shapes=[
            V((8, 16, 128), BF16), V((16, 768), F32), V((2, 256, 768), BF16), V((2, 64, 768), BF16),
            V((768, 768), BF16), V((832, 768), BF16), V((2, 768, 768), BF16), V((3, 2, 256, 256), BF16),
            V((2, 768, 256), F32), V((2, 256, 256), BF16), V((4, 2, 64, 256), BF16), V((128, 768), F32),
            V((128, 128), F32), V((8, 128), F32), V((4, 8, 128, 768), BF16), V((4, 8, 128, 768), BF16),
            V((4, 8, 8, 128), F32),
            V((2, 4, 256, 768), F32), V((4, 256, 128), F32),
            V((2, 8, 128, 768), BF16),
            V((2, 4, 128, 768), BF16), V((2, 3, 128, 768), BF16), V((2, 3, 128, 768), BF16),
            V((8, 8, 128), F32), V((8, 8, 128), F32), V((2, 768, 768), F32), V((768, 768), BF16),
            V((4, 2, 64, 256), BF16), V((4, 2, 64, 256), BF16),
            V((2, 256, 768), BF16), V((4, 2, 64, 768), BF16), V((768, 768), BF16),
            V((4, 96, 768), BF16), V((3, 96, 768), BF16), V((3, 96, 768), BF16),
            V((4, 96, 768), BF16), V((3, 96, 768), BF16), V((3, 96, 768), BF16),
            V((96, 768), BF16), V((96, 768), BF16), V((4, 96, 768), BF16),
            V((8, 768), F32), V((4, 8, 768), F32), V((8, 8, 768), F32), V((8, 768), F32),
            DMA((40, 8)), DMA((40, 8)),
        ],
        compiler_params=pltpu.CompilerParams(
            collective_id=0, has_side_effects=True, vmem_limit_bytes=67043328
        ),
        name="block",
    )(x, mask, ids, pk, w3, wo, win, g, wout)


def widen_kernel(low, full, o_low, o_full):
    o_low[...] = low[...].astype(F32)
    o_full[...] = full[...]


def widen(low, full):
    def spec(rows, columns):
        return pl.BlockSpec((rows, columns), lambda i: (i, 0))

    return pl.pallas_call(
        widen_kernel,
        grid=(6,),
        out_shape=[sds((384, 3072), F32), sds((1536, 768), F32)],
        in_specs=[spec(64, 3072), spec(256, 768)],
        out_specs=[spec(64, 3072), spec(256, 768)],
        name="widen",
    )(low, full)


def pack_small(ln1_gain, ln1_bias, ln2_gain, ln2_bias, router):
    rows = jnp.concatenate(
        [router.T, ln1_gain[None], ln1_bias[None], ln2_gain[None], ln2_bias[None]], axis=0
    )
    return jnp.pad(rows, ((0, 8), (0, 32)))


def plane_body(tokens, key_mask, expert_ids, ln1_gain, ln1_bias, w_qkv, w_attn_out, ln2_gain,
               ln2_bias, router, w_in, w_out, cotangent):
    pk = pack_small(ln1_gain, ln1_bias, ln2_gain, ln2_bias, router)
    heads = lax.dynamic_slice_in_dim(w_qkv.reshape(96, 3, 4, 192), lax.axis_index("seq"), 1, axis=2)
    w3 = jnp.pad(heads[:, :, 0], ((0, 0), (0, 0), (0, 64))).reshape(96, 768)
    out, tok, gwo, att, gwi, small, gao = run_block(
        tokens, key_mask, expert_ids.reshape(128, 2), pk, w3, w_attn_out, w_in,
        cotangent.reshape(128, 768), w_out.reshape(2, 768, 768),
    )
    own = lax.dynamic_slice_in_dim(small, 96 * lax.axis_index("dp"), 96, axis=1)
    att = att.reshape(4, 96, 3, 256)[:, :, :, :192].transpose(1, 2, 0, 3).reshape(96, 2304)
    shape = tokens.shape
    gwi, gwo = widen(gwi.reshape(384, 3072), gwo.reshape(1536, 768))
    return (
        out.reshape(shape), tok.reshape(shape), own[4], own[5], att.astype(F32), gao, own[6], own[7],
        own[0:4].T, gwi.reshape(4, 96, 3072), gwo.reshape(4, 384, 768),
    )


TOPK = 2
MOST = 40
MICRO = 2


def layer_norm(inputs, norm_gain, norm_shift):
    centre = inputs - jnp.mean(inputs, axis=-1, keepdims=True)
    spread = jnp.mean(centre * centre, axis=-1, keepdims=True)
    return centre * lax.rsqrt(spread + 1e-06) * norm_gain + norm_shift


def softmax_rows(scores):
    row_max = jnp.max(scores, axis=-1, keepdims=True)
    expo_terms = jnp.exp(scores - row_max)
    return expo_terms / jnp.sum(expo_terms, axis=-1, keepdims=True)


def exact_gelu(inputs):
    return jax.nn.gelu(inputs, approximate=False)


def attention_scores(queries, key_rows, key_valid):
    scores = jnp.einsum(
        "bqhc,bkhc->bhqk", queries, key_rows, preferred_element_type=jnp.float32
    ) * HEAD ** (-0.5)
    return jnp.where(key_valid, scores, -1e30)


def reduce_end(grads):
    shares = (
        lax.psum_scatter(grads[0], "dp", scatter_dimension=0, tiled=True),
        lax.psum_scatter(grads[1], "dp", scatter_dimension=0, tiled=True),
        lax.psum_scatter(grads[2], "dp", scatter_dimension=0, tiled=True),
        lax.psum_scatter(grads[3], "dp", scatter_dimension=0, tiled=True),
        lax.psum_scatter(grads[4], "dp", scatter_dimension=0, tiled=True),
        lax.psum_scatter(grads[5], "dp", scatter_dimension=0, tiled=True),
        lax.psum_scatter(grads[6], "dp", scatter_dimension=0, tiled=True),
        lax.psum_scatter(grads[7], "dp", scatter_dimension=1, tiled=True),
        lax.psum_scatter(grads[8], "dp", scatter_dimension=1, tiled=True),
    )
    quarters = (
        lax.psum_scatter(
            shares[0].astype(jnp.bfloat16), "seq", scatter_dimension=0, tiled=True
        ).astype(jnp.float32),
        lax.psum_scatter(
            shares[1].astype(jnp.bfloat16), "seq", scatter_dimension=0, tiled=True
        ).astype(jnp.float32),
        lax.psum_scatter(
            shares[2].astype(jnp.bfloat16), "seq", scatter_dimension=0, tiled=True
        ).astype(jnp.float32),
        lax.psum_scatter(
            shares[3].astype(jnp.bfloat16), "seq", scatter_dimension=0, tiled=True
        ).astype(jnp.float32),
        lax.psum_scatter(
            shares[4].astype(jnp.bfloat16), "seq", scatter_dimension=0, tiled=True
        ).astype(jnp.float32),
        lax.psum_scatter(
            shares[5].astype(jnp.bfloat16), "seq", scatter_dimension=0, tiled=True
        ).astype(jnp.float32),
        lax.psum_scatter(
            shares[6].astype(jnp.bfloat16), "seq", scatter_dimension=0, tiled=True
        ).astype(jnp.float32),
        lax.psum_scatter(
            shares[7].astype(jnp.bfloat16), "seq", scatter_dimension=1, tiled=True
        ).astype(jnp.float32),
        lax.psum_scatter(
            shares[8].astype(jnp.bfloat16), "seq", scatter_dimension=1, tiled=True
        ).astype(jnp.float32),
    )
    return (
        lax.all_gather(quarters[0].astype(jnp.bfloat16), "seq", axis=0, tiled=True).astype(
            jnp.float32
        ),
        lax.all_gather(quarters[1].astype(jnp.bfloat16), "seq", axis=0, tiled=True).astype(
            jnp.float32
        ),
        lax.all_gather(quarters[2].astype(jnp.bfloat16), "seq", axis=0, tiled=True).astype(
            jnp.float32
        ),
        lax.all_gather(quarters[3].astype(jnp.bfloat16), "seq", axis=0, tiled=True).astype(
            jnp.float32
        ),
        lax.all_gather(quarters[4].astype(jnp.bfloat16), "seq", axis=0, tiled=True).astype(
            jnp.float32
        ),
        lax.all_gather(quarters[5].astype(jnp.bfloat16), "seq", axis=0, tiled=True).astype(
            jnp.float32
        ),
        lax.all_gather(quarters[6].astype(jnp.bfloat16), "seq", axis=0, tiled=True).astype(
            jnp.float32
        ),
        lax.all_gather(quarters[7].astype(jnp.bfloat16), "seq", axis=1, tiled=True).astype(
            jnp.float32
        ),
        lax.all_gather(quarters[8].astype(jnp.bfloat16), "seq", axis=1, tiled=True).astype(
            jnp.float32
        ),
    )


def micro_step(weights, tokens_part, mask_part, routes_part, grad_part):
    (
        norm1_gain,
        norm1_shift,
        qkv_weight,
        proj_weight,
        norm2_gain,
        norm2_shift,
        router_weight,
        inner_weight,
        outer_weight,
    ) = weights
    batch, places, features = tokens_part.shape
    groups = lax.axis_size("seq")
    length = mask_part.shape[1]
    group_width = features // groups
    local_heads = HEADS // groups
    experts = inner_weight.shape[0]
    capacity = batch * MOST
    token_count = batch * places
    gain_one = norm1_gain.astype(jnp.float32)
    shift_one = norm1_shift.astype(jnp.float32)
    gain_two = norm2_gain.astype(jnp.float32)
    shift_two = norm2_shift.astype(jnp.float32)
    inputs = tokens_part.astype(jnp.float32).reshape(token_count, features)
    normed = layer_norm(inputs, gain_one, shift_one).astype(jnp.bfloat16)
    packed = jnp.dot(normed, qkv_weight, preferred_element_type=jnp.float32).astype(jnp.bfloat16)
    packed = packed.reshape(batch, places, 3, groups, group_width)
    spread = lax.all_to_all(packed, "seq", split_axis=3, concat_axis=1, tiled=True)
    queries = spread[:, :, 0, 0].reshape(batch, length, local_heads, HEAD)
    key_rows = spread[:, :, 1, 0].reshape(batch, length, local_heads, HEAD)
    values = spread[:, :, 2, 0].reshape(batch, length, local_heads, HEAD)
    key_valid = mask_part[:, None, None, :] > 0
    scores = attention_scores(queries, key_rows, key_valid)
    row_max = jnp.max(scores, axis=-1, keepdims=True)
    expo_terms = jnp.exp(scores - row_max)
    row_total = jnp.sum(expo_terms, axis=-1, keepdims=True)
    log_total = row_max + jnp.log(row_total)
    attn_probs = (expo_terms / row_total).astype(jnp.bfloat16)
    mixed_heads = jnp.einsum(
        "bhqk,bkhc->bqhc", attn_probs, values, preferred_element_type=jnp.float32
    ).astype(jnp.bfloat16)
    joined = lax.all_to_all(
        mixed_heads.reshape(batch, length, 1, group_width),
        "seq",
        split_axis=1,
        concat_axis=2,
        tiled=True,
    )
    head_rows = joined.reshape(token_count, features)
    residual = inputs + jnp.dot(head_rows, proj_weight, preferred_element_type=jnp.float32)
    normed_two = layer_norm(residual, gain_two, shift_two).astype(jnp.bfloat16)
    gate_probs = softmax_rows(
        jnp.dot(normed_two, router_weight, preferred_element_type=jnp.float32)
    )
    routes = routes_part.reshape(token_count, TOPK)
    pair_experts = routes.reshape(-1)
    expert_range = jnp.arange(experts, dtype=jnp.int32)
    pair_onehot = (pair_experts[:, None] == expert_range[None, :]).astype(jnp.int32)
    earlier = jnp.cumsum(pair_onehot, axis=0) - pair_onehot
    slot_index = pair_experts * capacity + jnp.sum(earlier * pair_onehot, axis=1)
    expert_rows = (
        jnp.zeros((experts * capacity, features), jnp.bfloat16)
        .at[slot_index]
        .set(jnp.repeat(normed_two, TOPK, axis=0))
    )
    expert_rows = expert_rows.reshape(experts, capacity, features)
    hidden = jnp.einsum(
        "ecd,edf->ecf", expert_rows, inner_weight, preferred_element_type=jnp.float32
    )
    active = exact_gelu(hidden).astype(jnp.bfloat16)
    results = jnp.einsum(
        "ecf,efd->ecd", active, outer_weight, preferred_element_type=jnp.float32
    ).reshape(experts * capacity, features)
    picked = results[slot_index].reshape(token_count, TOPK, features)
    mixing = jnp.take_along_axis(gate_probs, routes, axis=1)
    outputs = residual + jnp.sum(mixing[:, :, None] * picked, axis=1)
    grad_out = grad_part.astype(jnp.float32).reshape(token_count, features)
    grad_gate = jnp.sum(grad_out[:, None, :] * picked, axis=2)
    grad_pairs = (
        (mixing[:, :, None] * grad_out[:, None, :])
        .reshape(token_count * TOPK, features)
        .astype(jnp.bfloat16)
    )
    grad_results = (
        jnp.zeros((experts * capacity, features), jnp.bfloat16).at[slot_index].set(grad_pairs)
    )
    grad_results = grad_results.reshape(experts, capacity, features)
    grad_active = jnp.einsum(
        "ecd,efd->ecf", grad_results, outer_weight, preferred_element_type=jnp.float32
    )
    gelu_pull = jax.vjp(exact_gelu, hidden)[1]
    grad_hidden = gelu_pull(grad_active)[0].astype(jnp.bfloat16)
    grad_outer = jnp.einsum(
        "ecf,ecd->efd", active, grad_results, preferred_element_type=jnp.float32
    )
    grad_inner = jnp.einsum(
        "ecd,ecf->edf", expert_rows, grad_hidden, preferred_element_type=jnp.float32
    )
    grad_rows = jnp.einsum(
        "ecf,edf->ecd", grad_hidden, inner_weight, preferred_element_type=jnp.float32
    ).astype(jnp.bfloat16)
    grad_rows = grad_rows.reshape(experts * capacity, features)
    grad_normed_two = jnp.sum(
        grad_rows[slot_index].reshape(token_count, TOPK, features).astype(jnp.float32), axis=1
    )
    chosen = (routes[:, :, None] == expert_range[None, None, :]).astype(jnp.float32)
    grad_gates = jnp.sum(grad_gate[:, :, None] * chosen, axis=1)
    grad_logits = gate_probs * (
        grad_gates - jnp.sum(gate_probs * grad_gates, axis=-1, keepdims=True)
    )
    grad_logits = grad_logits.astype(jnp.bfloat16)
    grad_router = jnp.dot(normed_two.T, grad_logits, preferred_element_type=jnp.float32)
    grad_normed_two = grad_normed_two + jnp.dot(
        grad_logits, router_weight.T, preferred_element_type=jnp.float32
    )
    norm_pull_two = jax.vjp(layer_norm, residual, gain_two, shift_two)[1]
    grad_residual, grad_gain_two, grad_shift_two = norm_pull_two(grad_normed_two)
    grad_residual = grad_residual + grad_out
    grad_attn = grad_residual.astype(jnp.bfloat16)
    grad_proj = jnp.dot(head_rows.T, grad_attn, preferred_element_type=jnp.float32)
    grad_heads = jnp.dot(grad_attn, proj_weight.T, preferred_element_type=jnp.float32).astype(
        jnp.bfloat16
    )
    grad_spread = lax.all_to_all(
        grad_heads.reshape(batch, places, groups, group_width),
        "seq",
        split_axis=2,
        concat_axis=1,
        tiled=True,
    )
    grad_mixed = grad_spread.reshape(batch, length, local_heads, HEAD)
    scores_again = attention_scores(queries, key_rows, key_valid)
    probs_full = jnp.exp(scores_again - log_total)
    probs_low = probs_full.astype(jnp.bfloat16)
    grad_values = jnp.einsum(
        "bhqk,bqhc->bkhc", probs_low, grad_mixed, preferred_element_type=jnp.float32
    )
    grad_probs = jnp.einsum(
        "bqhc,bkhc->bhqk", grad_mixed, values, preferred_element_type=jnp.float32
    )
    grad_scores = probs_full * (
        grad_probs - jnp.sum(probs_full * grad_probs, axis=-1, keepdims=True)
    )
    grad_scores = grad_scores.astype(jnp.bfloat16)
    grad_queries = jnp.einsum(
        "bhqk,bkhc->bqhc", grad_scores, key_rows, preferred_element_type=jnp.float32
    ) * HEAD ** (-0.5)
    grad_keys = jnp.einsum(
        "bhqk,bqhc->bkhc", grad_scores, queries, preferred_element_type=jnp.float32
    ) * HEAD ** (-0.5)
    stacked = jnp.stack([grad_queries, grad_keys, grad_values], axis=2).astype(jnp.bfloat16)
    stacked = stacked.reshape(batch, length, 3, 1, group_width)
    returned = lax.all_to_all(stacked, "seq", split_axis=1, concat_axis=3, tiled=True)
    grad_packed = returned.reshape(token_count, 3 * features)
    grad_qkv = jnp.dot(normed.T, grad_packed, preferred_element_type=jnp.float32)
    grad_normed = jnp.dot(grad_packed, qkv_weight.T, preferred_element_type=jnp.float32)
    norm_pull_one = jax.vjp(layer_norm, inputs, gain_one, shift_one)[1]
    grad_inputs, grad_gain_one, grad_shift_one = norm_pull_one(grad_normed)
    grad_tokens = (grad_inputs + grad_residual).reshape(batch, places, features)
    grads = (
        grad_gain_one,
        grad_shift_one,
        grad_qkv,
        grad_proj,
        grad_gain_two,
        grad_shift_two,
        grad_router,
        grad_inner,
        grad_outer,
    )
    return (outputs.astype(jnp.bfloat16).reshape(batch, places, features), grad_tokens, grads)


def body(
    tokens,
    key_mask,
    expert_ids,
    ln1_gain,
    ln1_bias,
    w_qkv,
    w_attn_out,
    ln2_gain,
    ln2_bias,
    router,
    w_in,
    w_out,
    cotangent,
):
    per_batch = tokens.shape[0] // MICRO
    totals = None
    out_parts = []
    grad_parts = []
    for batch_step in range(MICRO):
        fetched = (
            lax.all_gather(ln1_gain, "dp", axis=0, tiled=True),
            lax.all_gather(ln1_bias, "dp", axis=0, tiled=True),
            lax.all_gather(w_qkv, "dp", axis=0, tiled=True),
            lax.all_gather(w_attn_out, "dp", axis=0, tiled=True),
            lax.all_gather(ln2_gain, "dp", axis=0, tiled=True),
            lax.all_gather(ln2_bias, "dp", axis=0, tiled=True),
            lax.all_gather(router, "dp", axis=0, tiled=True),
            lax.all_gather(w_in, "dp", axis=1, tiled=True),
            lax.all_gather(w_out, "dp", axis=1, tiled=True),
        )
        first = batch_step * per_batch
        last = first + per_batch
        out_part, grad_part, grads = micro_step(
            fetched,
            tokens[first:last],
            key_mask[first:last],
            expert_ids[first:last],
            cotangent[first:last],
        )
        out_parts.append(out_part)
        grad_parts.append(grad_part)
        totals = grads if totals is None else jax.tree.map(jnp.add, totals, grads)
    totals = reduce_end(totals)
    return (
        jnp.concatenate(out_parts, axis=0),
        jnp.concatenate(grad_parts, axis=0),
        totals[0],
        totals[1],
        totals[2],
        totals[3],
        totals[4],
        totals[5],
        totals[6],
        totals[7],
        totals[8],
    )


def solution(mesh):
    placed = (
        P("dp", "seq", None),
        P("dp", None),
        P("dp", "seq", None),
        P("dp"),
        P("dp"),
        P("dp", None),
        P("dp", None),
        P("dp"),
        P("dp"),
        P("dp", None),
        P(None, "dp", None),
        P(None, "dp", None),
        P("dp", "seq", None),
    )
    whole = mesh.shape['dp'] == 8 and mesh.shape['seq'] == 4
    return jax.shard_map(
        plane_body if whole else body,
        mesh=mesh,
        in_specs=placed,
        out_specs=(
            P("dp", "seq", None),
            P("dp", "seq", None),
            P("dp"),
            P("dp"),
            P("dp", None),
            P("dp", None),
            P("dp"),
            P("dp"),
            P("dp", None),
            P(None, "dp", None),
            P(None, "dp", None),
        ),
        check_vma=False,
    )
```

```python
import jax
import jax.numpy as jnp
from jax import lax
from jax.experimental import pallas as pl
from jax.experimental.pallas import tpu as pltpu
from jax.sharding import PartitionSpec as P

MESH = pl.DeviceIdType.MESH
F32, BF16 = jnp.float32, jnp.bfloat16
HEADS = 12
HEAD = 64
NT = (((1,), (1,)), ((), ()))
TN = (((0,), (0,)), ((), ()))


def dot(a, b, dims=(((1,), (0,)), ((), ()))):
    return lax.dot_general(a, b, dims, preferred_element_type=F32)


def mult(value, by):
    return pl.multiple_of(value, by)


class Place:
    def __init__(self):
        self.dp = lax.axis_index("dp")
        self.s = lax.axis_index("seq")
        self.core = lax.rem(self.dp, 2)
        self.x = lax.rem(lax.div(self.dp, 2), 2)
        self.y = lax.div(self.dp, 4)

    def chip(self, k):
        if isinstance(k, int):
            kx, ky = k % 2, k // 2
        else:
            kx, ky = lax.rem(k, 2), lax.div(k, 2)
        x = self.x + kx * (1 - 2 * self.x)
        y = self.y + ky * (1 - 2 * self.y)
        return y * 2 + x

    def peer(self, k):
        return self.chip(k) * 2 + self.core

    def near(self):
        x = self.x + (1 - self.core) * (1 - 2 * self.x)
        y = self.y + self.core * (1 - 2 * self.y)
        return (y * 2 + x) * 2 + self.core

    def far(self):
        x = self.x + self.core * (1 - 2 * self.x)
        y = self.y + (1 - self.core) * (1 - 2 * self.y)
        return (y * 2 + x) * 2 + self.core

    def partner(self):
        return self.dp + 1 - 2 * self.core

    def around(self, k):
        return lax.rem(self.dp + k, 8)

    def plane(self, k):
        low, high = lax.rem(self.s, 2), lax.div(self.s, 2)
        if isinstance(k, int):
            kl, kh = k % 2, k // 2
        else:
            kl, kh = lax.rem(k, 2), lax.div(k, 2)
        return 2 * (high + kh * (1 - 2 * high)) + low + kl * (1 - 2 * low)


def entry_barrier(me):
    sem = pltpu.get_barrier_semaphore()
    for k in range(1, 8):
        pl.semaphore_signal(
            sem, inc=1, device_id={"dp": me.around(k)}, device_id_type=MESH
        )
    for k in range(1, 4):
        pl.semaphore_signal(
            sem, inc=1, device_id={"seq": me.plane(k)}, device_id_type=MESH
        )
    pl.semaphore_wait(sem, 10)


def remote(src, dst, send, recv, **where):
    return pltpu.make_async_remote_copy(
        src_ref=src, dst_ref=dst, send_sem=send, recv_sem=recv, device_id=where, device_id_type=MESH
    )


class PlaneGather:
    def __init__(self, me, src, place, send, recv, local=True):
        own = place(me.dp)
        self.sends = [
            remote(src, own, send.at[0], recv.at[0], dp=me.partner()),
            remote(src, own, send.at[1], recv.at[1], dp=me.peer(1)),
            remote(src, own, send.at[2], recv.at[2], dp=me.peer(2)),
        ]
        near = place(me.near())
        self.relay = remote(near, near, send.at[3], recv.at[3], dp=me.far())
        self.onward = []
        for k in range(1, 4):
            there = place(me.peer(k))
            self.onward.append(remote(there, there, send.at[3 + k], recv.at[3 + k], dp=me.partner()))
        self.local = pltpu.make_async_copy(src, own, send.at[7]) if local else None

    def start(self):
        for k in (1, 2, 0):
            self.sends[k].start()
        if self.local is not None:
            self.local.start()

    def forward(self):
        self.sends[1].wait_recv()
        self.sends[2].wait_recv()
        self.relay.start()
        self.onward[0].start()
        self.onward[1].start()

    def diagonal(self):
        self.relay.wait_recv()
        self.onward[2].start()

    def finish(self):
        self.sends[0].wait_recv()
        for copy in self.onward:
            copy.wait_recv()
        for copy in self.sends + self.onward + [self.relay]:
            copy.wait_send()
        if self.local is not None:
            self.local.wait()


class Spread:
    def __init__(self, me, src, place, send, recv, axis, local=True, first=1):
        count, step, own = (8, me.around, me.dp) if axis == "dp" else (4, me.plane, me.s)
        self.copies = [
            remote(src, place(own), send.at[k], recv.at[k], **{axis: step(k)})
            for k in range(first, count)
        ]
        self.local = pltpu.make_async_copy(src, place(own), send.at[0]) if local else None

    def start(self):
        for copy in self.copies:
            copy.start()
        if self.local is not None:
            self.local.start()

    def arrive(self):
        for copy in self.copies:
            copy.wait_recv()
        if self.local is not None:
            self.local.wait()

    def drain(self):
        for copy in self.copies:
            copy.wait_send()


class Deal:
    def __init__(self, me, source, place, send, recv):
        self.copies = [
            remote(source(me.plane(k)), place(me.s), send.at[k], recv.at[k], seq=me.plane(k))
            for k in range(1, 4)
        ]

    def start(self):
        for copy in self.copies:
            copy.start()

    def arrive(self):
        for copy in self.copies:
            copy.wait_recv()

    def drain(self):
        for copy in self.copies:
            copy.wait_send()


class PlaneHop:
    def __init__(self, me, blocks, send, recv):
        near = me.plane(1)
        self.copies, self.onward = [], []
        for c in range(4):
            d = 2 * c + me.core
            here, there = blocks.at[me.s, d], blocks.at[near, d]
            self.copies.append(remote(here, here, send.at[c], recv.at[c], seq=near))
            self.onward.append(remote(there, there, send.at[4 + c], recv.at[4 + c], dp=me.partner()))

    def start(self):
        for copy in self.copies:
            copy.start()

    def forward(self):
        for copy, onward in zip(self.copies, self.onward):
            copy.wait_recv()
            onward.start()

    def finish(self):
        for copy in self.onward:
            copy.wait_recv()
        for copy in self.copies + self.onward:
            copy.wait_send()


class RowSum:
    def __init__(self, me, grads, landed, passed, came, send, recv):
        self.me, self.grads, self.landed, self.passed, self.came = me, grads, landed, passed, came
        self.pair = [
            remote(grads.at[self.rows(k, 1 - me.core), :], landed.at[k], send.at[k], recv.at[k], dp=me.partner())
            for k in range(4)
        ]
        self.across = [
            remote(passed.at[k - 1], came.at[k - 1], send.at[3 + k], recv.at[3 + k], dp=me.peer(k))
            for k in range(1, 4)
        ]

    def rows(self, k, core):
        return pl.ds(mult(96 * (2 * self.me.chip(k) + core), 32), 96)

    def start(self):
        for copy in self.pair:
            copy.start()

    def pass_on(self):
        for k in (3, 1, 2):
            self.pair[k].wait_recv()
            kept = self.grads[self.rows(k, self.me.core), :].astype(F32)
            self.passed[k - 1] = (kept + self.landed[k].astype(F32)).astype(BF16)
            self.across[k - 1].start()

    def total(self):
        self.pair[0].wait_recv()
        total = self.grads[self.rows(0, self.me.core), :].astype(F32) + self.landed[0].astype(F32)
        for k in range(3):
            self.across[k].wait_recv()
            total = total + self.came[k].astype(F32)
        return total

    def drain(self):
        for copy in self.pair + self.across:
            copy.wait_send()


def norm_rows(rows, gain, shift):
    centre = rows - jnp.mean(rows, axis=-1, keepdims=True)
    spread = jnp.mean(centre * centre, axis=-1, keepdims=True)
    return centre * lax.rsqrt(spread + 1e-06) * gain + shift


def norm_back(values, grad, gain):
    centre = values - jnp.mean(values, axis=-1, keepdims=True)
    rstd = lax.rsqrt(jnp.mean(centre * centre, axis=-1, keepdims=True) + 1e-06)
    xhat = centre * rstd
    u = grad * gain
    back = rstd * (
        u - jnp.mean(u, axis=-1, keepdims=True)
        - xhat * jnp.mean(u * xhat, axis=-1, keepdims=True)
    )
    return back, jnp.sum(grad * xhat, axis=0, keepdims=True), jnp.sum(grad, axis=0, keepdims=True)


ERFC = (
    0.19786723623605862, 0.190899613780153, 0.23209140755646218, -0.027655803526181202,
    0.6019196159005862, -0.6722756114657328, 0.7990689737520851, -0.3864325349090697,
    0.06451709047710916,
)


def normal_parts(h):
    bell = jnp.exp(-0.5 * (h * h))
    t = 1.0 / (1.0 + (0.35 * 0.5**0.5) * jnp.abs(h))
    poly = jnp.full_like(t, 0.5 * ERFC[8])
    for c in ERFC[7::-1]:
        poly = poly * t + 0.5 * c
    tail = poly * t * bell
    return jnp.where(h < 0, tail, 1.0 - tail), h * bell * 0.3989422804014327


def mix_columns(mixes):
    pad = jnp.zeros((120, 128), F32)
    return jnp.concatenate([jnp.concatenate([m, pad], axis=0).T for m in mixes], axis=0)


def by_head(v):
    lane = lax.broadcasted_iota(jnp.int32, v.shape, 1)
    zero = jnp.zeros_like(v)
    return jnp.concatenate(
        [jnp.where((lane >= HEAD * h) & (lane < HEAD * h + HEAD), v, zero) for h in range(3)], axis=0
    )


def from_heads(v):
    lane = lax.broadcasted_iota(jnp.int32, (256, 256), 1)
    total = jnp.where(lane < HEAD, v[0:256], 0.0)
    for h in range(1, 3):
        own = (lane >= HEAD * h) & (lane < HEAD * h + HEAD)
        total = jnp.where(own, v[256 * h : 256 * h + 256], total)
    return total


def block_kernel(
    x, mask, ids, pk, w3, wo, win, g, wout,
    o_out, o_tok, o_gwo, o_att, o_gwi, o_small, o_gao,
    pkall, pvec, xall, xown, w3a, woa, wina, qkv, pr, hd, hx, res, gates, mixs, n2a, ga, mixa,
    acc, pulls, sums, p_recv, c_send, c_recv, gate_send, gate_recv, gwi, gwb,
    ghs, ghx, gnp, gnx, gq, q_land, q_pass, q_came, o_land, o_pass, o_came, zq, zo, zoa,
    small, small_z, small_p, small_sum,
    S, R,
):
    me = Place()
    entry_barrier(me)
    dp, s = me.dp, me.s
    first = mult(64 * s, 64)
    rows96 = lambda d: pl.ds(mult(96 * d, 32), 96)
    small_in = Spread(me, pk, lambda d: pkall.at[d], S.at[10], R.at[10], "dp")
    zx = Spread(me, x, lambda q: xall.at[:, pl.ds(mult(64 * q, 64), 64), :], S.at[16], R.at[16], "seq")
    gather_w3 = PlaneGather(me, w3, lambda d: w3a.at[rows96(d), :], S.at[0], R.at[0])
    gather_wo = PlaneGather(me, wo, lambda d: woa.at[rows96(d), :], S.at[1], R.at[1])
    gather_g = PlaneGather(me, g, lambda d: ga.at[s, d], S.at[2], R.at[2])
    gather_n2 = PlaneGather(me, n2a.at[s, dp], lambda d: n2a.at[s, d], S.at[3], R.at[3], local=False)
    zg = Spread(me, g, lambda q: ga.at[q, dp], S.at[17], R.at[17], "seq", local=False, first=2)
    zn = Spread(me, n2a.at[s, dp], lambda q: n2a.at[q, dp], S.at[18], R.at[18], "seq", local=False, first=2)
    zm = Spread(me, mixs, lambda q: mixa.at[q, dp], S.at[19], R.at[19], "seq", local=False)
    mix_own = Spread(me, mixs, lambda d: mixa.at[s, d], S.at[11], R.at[11], "dp")
    hop_n2, hop_g = PlaneHop(me, n2a, S.at[4], R.at[4]), PlaneHop(me, ga, S.at[5], R.at[5])
    gathers, mixers = [None], []
    for k in range(1, 4):
        q = me.plane(k)
        if k > 1:
            gathers.append([
                PlaneGather(me, n2a.at[q, dp], lambda d, q=q: n2a.at[q, d], S.at[2 + 2 * k], R.at[2 + 2 * k], local=False),
                PlaneGather(me, ga.at[q, dp], lambda d, q=q: ga.at[q, d], S.at[3 + 2 * k], R.at[3 + 2 * k], local=False),
            ])
        mixers.append(
            Spread(me, mixa.at[q, dp], lambda d, q=q: mixa.at[q, d], S.at[11 + k], R.at[11 + k], "dp", local=False)
        )
    small_in.start()
    zx.start()
    gather_w3.start()
    gather_wo.start()
    gather_g.start()
    small_in.arrive()
    total = jnp.zeros((16, 768), F32)
    row = lax.broadcasted_iota(jnp.int32, (128, 768), 0)
    col = lax.broadcasted_iota(jnp.int32, (128, 768), 1)
    for j in range(8):
        spot = jnp.where((row < 96) & (row + 96 * j == col), 1.0, 0.0).astype(BF16)
        total = total + dot(pkall[j], spot)
    pvec[...] = total
    woa[768:832, :] = jnp.zeros((64, 768), BF16)
    o_gwo[...] = jnp.zeros_like(o_gwo)
    gwi[...] = jnp.zeros_like(gwi)
    gather_w3.forward()
    gather_wo.forward()
    gather_g.forward()
    a2a = []
    for e in range(4):
        p, h = e // 2, e % 2
        for k in range(1, 8):
            t = me.around(k)
            a2a.append(
                remote(
                    win.at[e, :, pl.ds(mult(384 * t, 128), 384)],
                    wina.at[p, rows96(dp), 384 * h : 384 * h + 384],
                    S.at[31 + e, k], R.at[31 + e, k], dp=t,
                )
            )
        a2a.append(
            pltpu.make_async_copy(
                win.at[e, :, pl.ds(mult(384 * dp, 128), 384)],
                wina.at[p, rows96(dp), 384 * h : 384 * h + 384],
                S.at[31 + e, 0],
            )
        )
    for copy in a2a[:16]:
        copy.start()
    acc[...] = jnp.zeros_like(acc)
    pulls[...] = jnp.zeros_like(pulls)
    gather_w3.diagonal()
    gather_wo.diagonal()
    gather_g.diagonal()
    zx.arrive()

    xown[...] = xall[:, pl.ds(first, 64), :]

    def ln_step(i, carry):
        xall[i] = norm_rows(xall[i].astype(F32), pvec[4:5, :], pvec[5:6, :]).astype(BF16)
        return carry

    lax.fori_loop(0, 2, ln_step, 0)
    gather_w3.finish()

    def attend(i, carry):
        for kind in range(3):
            qkv[kind, i] = dot(xall[i], w3a[:, 256 * kind : 256 * kind + 256]).astype(BF16)
        scores = dot(by_head(qkv[0, i]), qkv[1, i], NT) * HEAD ** (-0.5)
        scores = jnp.where(mask[pl.ds(i, 1), :] > 0, scores, -1e30)
        terms = jnp.exp(scores - jnp.max(scores, axis=-1, keepdims=True))
        probs = terms / jnp.sum(terms, axis=-1, keepdims=True)
        pr[i] = probs
        hd[i] = from_heads(dot(probs.astype(BF16), qkv[2, i])).astype(BF16)
        return carry

    lax.fori_loop(0, 2, attend, 0)
    deal_heads = Deal(me, lambda q: hd.at[:, pl.ds(mult(64 * q, 64), 64), :], lambda q: hx.at[q], S.at[20], R.at[20])
    deal_heads.start()
    hx[s] = hd[:, pl.ds(first, 64), :]
    gather_wo.finish()
    deal_heads.arrive()
    zg.start()
    tokens = xown[...].reshape(128, 768).astype(F32)
    mixed = tokens
    for q in range(4):
        mixed = mixed + dot(hx[q].reshape(128, 256), woa[192 * q : 192 * q + 256, :])
    res[...] = mixed
    own_n2 = norm_rows(mixed, pvec[6:7, :], pvec[7:8, :]).astype(BF16)
    n2a[s, dp] = own_n2
    gather_n2.start()
    zn.start()
    for copy in a2a[16:]:
        copy.start()
    router = jnp.concatenate([pvec[0:4, :].astype(BF16), jnp.zeros((124, 768), BF16)], axis=0)
    lane = lax.broadcasted_iota(jnp.int32, (128, 128), 1)
    logits = jnp.where(lane < 4, dot(own_n2, router, NT), -1e30)
    terms = jnp.exp(logits - jnp.max(logits, axis=-1, keepdims=True))
    probs4 = terms / jnp.sum(terms, axis=-1, keepdims=True)
    gates[...] = probs4
    chosen = (lane == ids[:, 0:1]) | (lane == ids[:, 1:2])
    mixs[...] = jnp.where(chosen, probs4, 0.0).T[0:8, :]
    mix_own.start()
    zm.start()
    gather_g.finish()
    hop_g.start()
    gather_n2.forward()
    gather_n2.diagonal()
    for copy in a2a[:16]:
        copy.wait()
    gather_n2.finish()
    hop_n2.start()
    mix_own.arrive()

    def pair_step(p, n2c, gc, columns):
        many = n2c.shape[0]
        lanes = lax.broadcasted_iota(jnp.int32, (many, 128), 1)
        low = jnp.sum(jnp.where(lanes == 2 * p, columns, 0.0), axis=1, keepdims=True)
        high = jnp.sum(jnp.where(lanes == 2 * p + 1, columns, 0.0), axis=1, keepdims=True)
        gate = jnp.where(lax.broadcasted_iota(jnp.int32, (many, 768), 1) < 384, low, high)
        hidden = dot(n2c, wina[p])
        pull = dot(gc, wout[p], NT)
        phi, slope = normal_parts(hidden)
        active = hidden * phi
        taken = (gate * active).astype(BF16)
        grad_hidden = (gate * pull * (phi + slope)).astype(BF16)
        gwi[p] += dot(n2c, grad_hidden, TN)
        return active, pull, taken, grad_hidden

    def pair_copy(k, which):
        other = 2 * me.chip(k) + 1 - me.core
        at = 4 * which + k
        return remote(sums.at[which, other], p_recv.at[which, k], S.at[29, at], R.at[29, at], dp=me.partner())

    def across_copy(k, which):
        at = 3 * which + k - 1
        return remote(
            c_send.at[which, k - 1], c_recv.at[which, k - 1], S.at[30, at], R.at[30, at], dp=me.peer(k)
        )

    def gate_copy(k, b):
        target = 2 * me.chip(k) + (1 - me.core if b else me.core)
        at = 2 * k + b
        return remote(gate_send.at[target], gate_recv.at[at], S.at[28, at], R.at[28, at], dp=target)

    def push(k, which):
        pair_copy(k, which).wait_recv()
        total = sums[which, 2 * me.chip(k) + me.core].astype(F32) + p_recv[which, k].astype(F32)
        c_send[which, k - 1] = total.astype(BF16)
        across_copy(k, which).start()

    def own_step(t, carry):
        p, i = lax.div(t, 4), lax.rem(t, 4)
        k = 3 - i
        c = me.chip(k)

        @pl.when(t == 4)
        def _():
            for copy in a2a[16:]:
                copy.wait()
            zg.arrive()
            gathers[1][1].start()
            zn.arrive()
            gathers[1][0].start()
            zm.arrive()
            for one in mixers:
                one.start()

        @pl.when(t == 6)
        def _():
            hop_g.forward()

        columns = mix_columns([mixa[s, 2 * c], mixa[s, 2 * c + 1]])
        n2c = n2a[s, pl.ds(2 * c, 2)].reshape(256, 768)
        gc = ga[s, pl.ds(2 * c, 2)].reshape(256, 768)
        active, pull, taken, grad_hidden = pair_step(p, n2c, gc, columns)
        acc[0, i] += dot(grad_hidden, wina[p], NT)
        acc[1, i] += dot(taken, wout[p])
        o_gwo[p] += dot(taken, gc, TN)
        inner = active * pull
        low = jnp.sum(inner[:, :384], axis=1, keepdims=True)
        high = jnp.sum(inner[:, 384:], axis=1, keepdims=True)
        lanes = lax.broadcasted_iota(jnp.int32, (256, 128), 1)
        pulls[i] = jnp.where(lanes == 2 * p, low, jnp.where(lanes == 2 * p + 1, high, pulls[i]))

        @pl.when(p == 1)
        def _():
            for b in range(2):
                sums[0, 2 * c + b] = acc[0, i, 128 * b : 128 * b + 128].astype(BF16)
                sums[1, 2 * c + b] = acc[1, i, 128 * b : 128 * b + 128].astype(BF16)
                gate_send[2 * c + b] = pulls[i, 128 * b : 128 * b + 128].T[0:8, :]
            pair_copy(k, 0).start()
            gate_copy(k, 1).start()

        @pl.when((p == 1) & (k > 0))
        def _():
            gate_copy(k, 0).start()

        @pl.when(t > 4)
        def _():
            push(k + 1, 0)

        return carry

    lax.fori_loop(0, 8, own_step, 0)
    pair_copy(0, 0).wait_recv()
    for k in range(4):
        pair_copy(k, 1).start()
    for k in range(4):
        if k:
            across_copy(k, 0).wait_recv()
            gate_copy(k, 0).wait_recv()
        gate_copy(k, 1).wait_recv()
    hop_n2.forward()

    def summed(which):
        total = sums[which, dp].astype(F32) + p_recv[which, 0].astype(F32)
        for k in range(3):
            total = total + c_recv[which, k].astype(F32)
        return total

    gate_sum = gate_send[dp]
    for k in range(1, 8):
        gate_sum = gate_sum + gate_recv[k]
    grad_gate = jnp.concatenate([gate_sum, jnp.zeros((120, 128), F32)], axis=0).T
    lane = lax.broadcasted_iota(jnp.int32, (128, 128), 1)
    chosen = (lane == ids[:, 0:1]) | (lane == ids[:, 1:2])
    grad_gate = jnp.where(chosen, grad_gate, 0.0)
    probs4 = gates[...]
    grad_logits = probs4 * (grad_gate - jnp.sum(probs4 * grad_gate, axis=-1, keepdims=True))
    grad_logits = grad_logits.astype(BF16)
    router = jnp.concatenate([pvec[0:4, :].astype(BF16), jnp.zeros((124, 768), BF16)], axis=0)
    small[...] = dot(grad_logits, n2a[s, dp], TN)[0:8, :]
    grad_n2 = summed(0) + dot(grad_logits, router)
    back, gain2, shift2 = norm_back(res[...], grad_n2, pvec[6:7, :])
    small[6:7, :] = gain2
    small[7:8, :] = shift2
    grad_res = back + ga[s, dp].astype(F32)
    o_tok[...] = grad_res
    grb = grad_res.astype(BF16)
    lane = lax.broadcasted_iota(jnp.int32, (128, 256), 1)
    for q in range(4):
        pulled = dot(grb, woa[192 * q : 192 * q + 256, :], NT)
        ghs[q] = jnp.where(lane < 192, pulled, 0.0).astype(BF16).reshape(2, 64, 256)
    deal_grads = Deal(me, lambda q: ghs.at[q], lambda q: ghx.at[q], S.at[21], R.at[21])
    deal_grads.start()
    ghx[s] = ghs[s]
    for q in range(4):
        gwb[192 * q : 192 * q + 192, :] = dot(hx[q].reshape(128, 256), grb, TN)[0:192].astype(BF16)
    sum_o = RowSum(me, gwb, o_land, o_pass, o_came, S.at[27], R.at[27])
    sum_o.start()
    for one in gathers[1]:
        one.forward()
    for one in gathers[2]:
        one.start()
    for one in mixers:
        one.arrive()
    hop_g.finish()
    hop_n2.finish()

    def attend_back(i, carry):
        grads = by_head(ghx[:, pl.ds(i, 1)].reshape(256, 256))
        queries = by_head(qkv[0, i])
        keys, vals, probs = qkv[1, i], qkv[2, i], pr[i]
        at = pl.ds(2 * i, 2)
        scale = HEAD ** (-0.5)
        p_recv[0, at, :, 512:768] = dot(probs.astype(BF16), grads, TN).astype(BF16).reshape(2, 128, 256)
        grad_probs = dot(grads, vals, NT)
        inner = jnp.sum(probs * grad_probs, axis=-1, keepdims=True)
        grad_scores = (probs * (grad_probs - inner)).astype(BF16)
        grad_q = (from_heads(dot(grad_scores, keys)) * scale).astype(BF16)
        p_recv[0, at, :, 0:256] = grad_q.reshape(2, 128, 256)
        grad_k = (dot(grad_scores, queries, TN) * scale).astype(BF16)
        p_recv[0, at, :, 256:512] = grad_k.reshape(2, 128, 256)
        gnp[i] = dot(p_recv[0, at].reshape(256, 768), w3a[...], NT).astype(BF16)
        return carry

    deal_norm = Deal(me, lambda q: gnp.at[:, pl.ds(mult(64 * q, 64), 64), :], lambda q: gnx.at[q], S.at[22], R.at[22])

    def weights(t, carry):
        at = pl.ds(mult(256 * t, 256), 256)
        gq[:, at] = dot(xall[...].reshape(512, 768), p_recv[0, :, :, at].reshape(512, 256), TN).astype(BF16)
        return carry

    sum_q = RowSum(me, gq, q_land, q_pass, q_came, S.at[26], R.at[26])
    spread_o = Spread(me, zo, lambda q: zoa.at[q], S.at[25], R.at[25], "seq")
    spread_q = Spread(me, zq, lambda q: o_att.at[q], S.at[24], R.at[24], "seq")
    spread_small = Spread(me, small, lambda q: small_z.at[q], S.at[23], R.at[23], "seq")
    plane_small = Spread(me, small_sum, lambda d: small_p.at[d], S.at[15], R.at[15], "dp")

    def reshard_copies(p):
        copies = []
        for h in range(2):
            e = 2 * p + h
            for k in range(8):
                t = me.around(k) if k else dp
                source = gwb.at[rows96(t), 384 * h : 384 * h + 384]
                target = o_gwi.at[e, :, pl.ds(mult(384 * dp, 128), 384)]
                if k:
                    copies.append(remote(source, target, S.at[35 + e, k], R.at[35 + e, k], dp=t))
                else:
                    copies.append(pltpu.make_async_copy(source, target, S.at[35 + e, 0]))
        return copies

    reshards = [reshard_copies(0), reshard_copies(1)]

    def reshard(p):
        def cast(t, carry):
            at = pl.ds(mult(96 * t, 32), 96)
            gwb[at, :] = gwi[p, at, :].astype(BF16)
            return carry

        lax.fori_loop(0, 8, cast, 0)
        for copy in reshards[p]:
            copy.start()

    def stage_1():
        sum_o.pass_on()
        for k in range(1, 4):
            push(k, 1)
        for one in gathers[1]:
            one.diagonal()

    def stage_2():
        deal_grads.arrive()
        lax.fori_loop(0, 2, attend_back, 0)
        deal_norm.start()
        gnx[s] = gnp[:, pl.ds(first, 64), :]
        lax.fori_loop(0, 3, weights, 0)
        sum_q.start()
        for one in gathers[2]:
            one.forward()

    def stage_3():
        sum_q.pass_on()
        for one in gathers[2]:
            one.diagonal()
        zo[...] = sum_o.total().astype(BF16)
        spread_o.start()

    def stage_4():
        for one in gathers[1]:
            one.finish()

    def stage_5():
        deal_norm.arrive()
        grad_n1 = jnp.zeros((128, 768), F32)
        for q in range(4):
            grad_n1 = grad_n1 + gnx[q].reshape(128, 768).astype(F32)
        tokens = xown[...].reshape(128, 768).astype(F32)
        back, gain1, shift1 = norm_back(tokens, grad_n1, pvec[4:5, :])
        o_tok[...] = back + o_tok[...]
        small[4:5, :] = gain1
        small[5:6, :] = shift1
        spread_small.start()

    def stage_6():
        zq[...] = sum_q.total().astype(BF16)
        spread_q.start()
        for one in gathers[2]:
            one.finish()

    def stage_7():
        pair_copy(0, 1).wait_recv()
        for k in range(1, 4):
            across_copy(k, 1).wait_recv()
        o_out[...] = (res[...] + summed(1)).astype(BF16)

    def stage_8():
        sum_o.drain()
        for which in range(2):
            for k in range(4):
                pair_copy(k, which).wait_send()
        reshard(0)
        spread_small.arrive()
        small_sum[...] = small_z[0] + small_z[1] + small_z[2] + small_z[3]
        plane_small.start()

    stages = (stage_1, stage_2, stage_3, stage_4, stage_5, stage_6, stage_7, stage_8)

    def other_step(t, carry):
        for at, stage in enumerate(stages):
            pl.when(t == at + 1)(stage)
        far = lax.div(t, 4)
        inner = lax.rem(t, 4)
        p = jnp.where(far == 0, lax.rem(t, 2), far - 1)
        q = me.plane(jnp.where(far == 0, 1, 2 + lax.div(inner, 2)))
        b = jnp.where(far == 0, lax.div(inner, 2), lax.rem(t, 2))
        columns = mix_columns([mixa[q, 4 * b + j] for j in range(4)])
        n2c = n2a[q, pl.ds(4 * b, 4)].reshape(512, 768)
        gc = ga[q, pl.ds(4 * b, 4)].reshape(512, 768)
        taken = pair_step(p, n2c, gc, columns)[2]

        @pl.when(t < 4)
        def _():
            o_gwo[p] += dot(taken, gc, TN)

        @pl.when((t >= 4) & (t < 8))
        def _():
            acc[lax.div(inner, 2), pl.ds(2 * lax.rem(inner, 2), 2)] = taken.astype(F32).reshape(2, 256, 768)

        @pl.when(t >= 8)
        def _():
            sums[lax.div(inner, 2), pl.ds(4 * lax.rem(inner, 2), 4)] = taken.reshape(4, 128, 768)

        return carry

    lax.fori_loop(0, 12, other_step, 0)
    for copy in reshards[0]:
        copy.wait()
    reshard(1)

    def last_products(j, carry):
        q = me.plane(2 + lax.div(j, 2))
        gc = ga[q, pl.ds(4 * lax.rem(j, 2), 4)].reshape(512, 768)
        h, b = lax.div(j, 2), lax.rem(j, 2)
        early = acc[h, pl.ds(2 * b, 2)].reshape(512, 768).astype(BF16)
        o_gwo[0] += dot(early, gc, TN)
        taken = sums[h, pl.ds(4 * b, 4)].reshape(512, 768)
        o_gwo[1] += dot(taken, gc, TN)
        return carry

    lax.fori_loop(0, 4, last_products, 0)
    plane_small.arrive()
    total = small_p[0]
    for k in range(1, 8):
        total = total + small_p[k]
    o_small[...] = total
    spread_o.arrive()
    total = zoa[0].astype(F32)
    for q in range(1, 4):
        total = total + zoa[q].astype(F32)
    o_gao[...] = total
    spread_q.arrive()
    for copy in reshards[1]:
        copy.wait()
    for which in range(2):
        for k in range(1, 4):
            across_copy(k, which).wait_send()
    for k in range(4):
        if k:
            gate_copy(k, 0).wait_send()
        gate_copy(k, 1).wait_send()
    for one in mixers + [
        small_in, zx, zg, zn, zm, mix_own, deal_heads, deal_grads, deal_norm, sum_q,
        spread_o, spread_q, spread_small, plane_small,
    ]:
        one.drain()


VM = pl.BlockSpec(memory_space=pltpu.VMEM)
ANY = pl.BlockSpec(memory_space=pl.ANY)
DMA = pltpu.SemaphoreType.DMA


def sds(shape, dtype=BF16):
    return jax.ShapeDtypeStruct(shape, dtype)


def run_block(x, mask, ids, pk, w3, wo, win, g, wout):
    V = pltpu.VMEM
    return pl.pallas_call(
        block_kernel,
        out_shape=[
            sds((128, 768)), sds((128, 768), F32), sds((2, 768, 768), F32), sds((4, 96, 768)),
            sds((4, 96, 3072)), sds((8, 768), F32), sds((96, 768), F32),
        ],
        in_specs=[ANY, VM, VM, VM, ANY, ANY, ANY, ANY, VM],
        out_specs=[VM, VM, VM, ANY, ANY, VM, VM],
        scratch_shapes=[
            V((8, 16, 128), BF16), V((16, 768), F32), V((2, 256, 768), BF16), V((2, 64, 768), BF16),
            V((768, 768), BF16), V((832, 768), BF16), V((2, 768, 768), BF16), V((3, 2, 256, 256), BF16),
            V((2, 768, 256), F32), V((2, 256, 256), BF16), V((4, 2, 64, 256), BF16), V((128, 768), F32),
            V((128, 128), F32), V((8, 128), F32), V((4, 8, 128, 768), BF16), V((4, 8, 128, 768), BF16),
            V((4, 8, 8, 128), F32),
            V((2, 4, 256, 768), F32), V((4, 256, 128), F32),
            V((2, 8, 128, 768), BF16),
            V((2, 4, 128, 768), BF16), V((2, 3, 128, 768), BF16), V((2, 3, 128, 768), BF16),
            V((8, 8, 128), F32), V((8, 8, 128), F32), V((2, 768, 768), F32), V((768, 768), BF16),
            V((4, 2, 64, 256), BF16), V((4, 2, 64, 256), BF16),
            V((2, 256, 768), BF16), V((4, 2, 64, 768), BF16), V((768, 768), BF16),
            V((4, 96, 768), BF16), V((3, 96, 768), BF16), V((3, 96, 768), BF16),
            V((4, 96, 768), BF16), V((3, 96, 768), BF16), V((3, 96, 768), BF16),
            V((96, 768), BF16), V((96, 768), BF16), V((4, 96, 768), BF16),
            V((8, 768), F32), V((4, 8, 768), F32), V((8, 8, 768), F32), V((8, 768), F32),
            DMA((40, 8)), DMA((40, 8)),
        ],
        compiler_params=pltpu.CompilerParams(
            collective_id=0, has_side_effects=True, vmem_limit_bytes=67043328
        ),
        name="block",
    )(x, mask, ids, pk, w3, wo, win, g, wout)


def widen_kernel(low, full, att, tok, out, gao, o_low, o_full, o_att, o_tok, o_out, o_gao):
    o_low[...] = low[...].astype(F32)
    o_full[...] = full[...]
    o_tok[...] = tok[...]
    o_out[...] = out[...]

    @pl.when(pl.program_id(0) == 0)
    def _():
        o_gao[...] = gao[...]
        for kind in range(3):
            for q in range(4):
                at = 768 * kind + 192 * q
                o_att[:, at : at + 192] = att[q, :, 256 * kind : 256 * kind + 192].astype(F32)


def widen(low, full, att, tok, out, gao):
    def spec(rows, columns):
        return pl.BlockSpec((rows, columns), lambda i: (i, 0))

    def whole(*shape):
        return pl.BlockSpec(shape, lambda i: (0,) * len(shape))

    return pl.pallas_call(
        widen_kernel,
        grid=(8,),
        out_shape=[
            sds((384, 3072), F32), sds((1536, 768), F32), sds((96, 2304), F32),
            sds((128, 768), F32), sds((128, 768)), sds((96, 768), F32),
        ],
        in_specs=[
            spec(48, 3072), spec(192, 768), whole(4, 96, 768), spec(16, 768), spec(16, 768), whole(96, 768),
        ],
        out_specs=[
            spec(48, 3072), spec(192, 768), whole(96, 2304), spec(16, 768), spec(16, 768), whole(96, 768),
        ],
        name="widen",
    )(low, full, att, tok, out, gao)


def pack_small(ln1_gain, ln1_bias, ln2_gain, ln2_bias, router):
    rows = jnp.concatenate(
        [router.T, ln1_gain[None], ln1_bias[None], ln2_gain[None], ln2_bias[None]], axis=0
    )
    return jnp.pad(rows, ((0, 8), (0, 32)))


def plane_body(tokens, key_mask, expert_ids, ln1_gain, ln1_bias, w_qkv, w_attn_out, ln2_gain,
               ln2_bias, router, w_in, w_out, cotangent):
    pk = pack_small(ln1_gain, ln1_bias, ln2_gain, ln2_bias, router)
    first = 192 * lax.axis_index("seq")
    parts = [lax.dynamic_slice_in_dim(w_qkv, 768 * kind + first, 192, axis=1) for kind in range(3)]
    w3 = jnp.concatenate([jnp.pad(part, ((0, 0), (0, 64))) for part in parts], axis=1)
    out, tok, gwo, att, gwi, small, gao = run_block(
        tokens, key_mask, expert_ids.reshape(128, 2), pk, w3, w_attn_out, w_in,
        cotangent.reshape(128, 768), w_out.reshape(2, 768, 768),
    )
    own = lax.dynamic_slice_in_dim(small, 96 * lax.axis_index("dp"), 96, axis=1)
    shape = tokens.shape
    gwi, gwo, att, tok, out, gao = widen(
        gwi.reshape(384, 3072), gwo.reshape(1536, 768), att, tok, out, gao
    )
    return (
        out.reshape(shape), tok.reshape(shape), own[4], own[5], att, gao, own[6], own[7],
        own[0:4].T, gwi.reshape(4, 96, 3072), gwo.reshape(4, 384, 768),
    )


TOPK = 2
MOST = 40
MICRO = 2


def layer_norm(inputs, norm_gain, norm_shift):
    centre = inputs - jnp.mean(inputs, axis=-1, keepdims=True)
    spread = jnp.mean(centre * centre, axis=-1, keepdims=True)
    return centre * lax.rsqrt(spread + 1e-06) * norm_gain + norm_shift


def softmax_rows(scores):
    row_max = jnp.max(scores, axis=-1, keepdims=True)
    expo_terms = jnp.exp(scores - row_max)
    return expo_terms / jnp.sum(expo_terms, axis=-1, keepdims=True)


def exact_gelu(inputs):
    return jax.nn.gelu(inputs, approximate=False)


def attention_scores(queries, key_rows, key_valid):
    scores = jnp.einsum(
        "bqhc,bkhc->bhqk", queries, key_rows, preferred_element_type=jnp.float32
    ) * HEAD ** (-0.5)
    return jnp.where(key_valid, scores, -1e30)


def reduce_end(grads):
    shares = (
        lax.psum_scatter(grads[0], "dp", scatter_dimension=0, tiled=True),
        lax.psum_scatter(grads[1], "dp", scatter_dimension=0, tiled=True),
        lax.psum_scatter(grads[2], "dp", scatter_dimension=0, tiled=True),
        lax.psum_scatter(grads[3], "dp", scatter_dimension=0, tiled=True),
        lax.psum_scatter(grads[4], "dp", scatter_dimension=0, tiled=True),
        lax.psum_scatter(grads[5], "dp", scatter_dimension=0, tiled=True),
        lax.psum_scatter(grads[6], "dp", scatter_dimension=0, tiled=True),
        lax.psum_scatter(grads[7], "dp", scatter_dimension=1, tiled=True),
        lax.psum_scatter(grads[8], "dp", scatter_dimension=1, tiled=True),
    )
    quarters = (
        lax.psum_scatter(
            shares[0].astype(jnp.bfloat16), "seq", scatter_dimension=0, tiled=True
        ).astype(jnp.float32),
        lax.psum_scatter(
            shares[1].astype(jnp.bfloat16), "seq", scatter_dimension=0, tiled=True
        ).astype(jnp.float32),
        lax.psum_scatter(
            shares[2].astype(jnp.bfloat16), "seq", scatter_dimension=0, tiled=True
        ).astype(jnp.float32),
        lax.psum_scatter(
            shares[3].astype(jnp.bfloat16), "seq", scatter_dimension=0, tiled=True
        ).astype(jnp.float32),
        lax.psum_scatter(
            shares[4].astype(jnp.bfloat16), "seq", scatter_dimension=0, tiled=True
        ).astype(jnp.float32),
        lax.psum_scatter(
            shares[5].astype(jnp.bfloat16), "seq", scatter_dimension=0, tiled=True
        ).astype(jnp.float32),
        lax.psum_scatter(
            shares[6].astype(jnp.bfloat16), "seq", scatter_dimension=0, tiled=True
        ).astype(jnp.float32),
        lax.psum_scatter(
            shares[7].astype(jnp.bfloat16), "seq", scatter_dimension=1, tiled=True
        ).astype(jnp.float32),
        lax.psum_scatter(
            shares[8].astype(jnp.bfloat16), "seq", scatter_dimension=1, tiled=True
        ).astype(jnp.float32),
    )
    return (
        lax.all_gather(quarters[0].astype(jnp.bfloat16), "seq", axis=0, tiled=True).astype(
            jnp.float32
        ),
        lax.all_gather(quarters[1].astype(jnp.bfloat16), "seq", axis=0, tiled=True).astype(
            jnp.float32
        ),
        lax.all_gather(quarters[2].astype(jnp.bfloat16), "seq", axis=0, tiled=True).astype(
            jnp.float32
        ),
        lax.all_gather(quarters[3].astype(jnp.bfloat16), "seq", axis=0, tiled=True).astype(
            jnp.float32
        ),
        lax.all_gather(quarters[4].astype(jnp.bfloat16), "seq", axis=0, tiled=True).astype(
            jnp.float32
        ),
        lax.all_gather(quarters[5].astype(jnp.bfloat16), "seq", axis=0, tiled=True).astype(
            jnp.float32
        ),
        lax.all_gather(quarters[6].astype(jnp.bfloat16), "seq", axis=0, tiled=True).astype(
            jnp.float32
        ),
        lax.all_gather(quarters[7].astype(jnp.bfloat16), "seq", axis=1, tiled=True).astype(
            jnp.float32
        ),
        lax.all_gather(quarters[8].astype(jnp.bfloat16), "seq", axis=1, tiled=True).astype(
            jnp.float32
        ),
    )


def micro_step(weights, tokens_part, mask_part, routes_part, grad_part):
    (
        norm1_gain,
        norm1_shift,
        qkv_weight,
        proj_weight,
        norm2_gain,
        norm2_shift,
        router_weight,
        inner_weight,
        outer_weight,
    ) = weights
    batch, places, features = tokens_part.shape
    groups = lax.axis_size("seq")
    length = mask_part.shape[1]
    group_width = features // groups
    local_heads = HEADS // groups
    experts = inner_weight.shape[0]
    capacity = batch * MOST
    token_count = batch * places
    gain_one = norm1_gain.astype(jnp.float32)
    shift_one = norm1_shift.astype(jnp.float32)
    gain_two = norm2_gain.astype(jnp.float32)
    shift_two = norm2_shift.astype(jnp.float32)
    inputs = tokens_part.astype(jnp.float32).reshape(token_count, features)
    normed = layer_norm(inputs, gain_one, shift_one).astype(jnp.bfloat16)
    packed = jnp.dot(normed, qkv_weight, preferred_element_type=jnp.float32).astype(jnp.bfloat16)
    packed = packed.reshape(batch, places, 3, groups, group_width)
    spread = lax.all_to_all(packed, "seq", split_axis=3, concat_axis=1, tiled=True)
    queries = spread[:, :, 0, 0].reshape(batch, length, local_heads, HEAD)
    key_rows = spread[:, :, 1, 0].reshape(batch, length, local_heads, HEAD)
    values = spread[:, :, 2, 0].reshape(batch, length, local_heads, HEAD)
    key_valid = mask_part[:, None, None, :] > 0
    scores = attention_scores(queries, key_rows, key_valid)
    row_max = jnp.max(scores, axis=-1, keepdims=True)
    expo_terms = jnp.exp(scores - row_max)
    row_total = jnp.sum(expo_terms, axis=-1, keepdims=True)
    log_total = row_max + jnp.log(row_total)
    attn_probs = (expo_terms / row_total).astype(jnp.bfloat16)
    mixed_heads = jnp.einsum(
        "bhqk,bkhc->bqhc", attn_probs, values, preferred_element_type=jnp.float32
    ).astype(jnp.bfloat16)
    joined = lax.all_to_all(
        mixed_heads.reshape(batch, length, 1, group_width),
        "seq",
        split_axis=1,
        concat_axis=2,
        tiled=True,
    )
    head_rows = joined.reshape(token_count, features)
    residual = inputs + jnp.dot(head_rows, proj_weight, preferred_element_type=jnp.float32)
    normed_two = layer_norm(residual, gain_two, shift_two).astype(jnp.bfloat16)
    gate_probs = softmax_rows(
        jnp.dot(normed_two, router_weight, preferred_element_type=jnp.float32)
    )
    routes = routes_part.reshape(token_count, TOPK)
    pair_experts = routes.reshape(-1)
    expert_range = jnp.arange(experts, dtype=jnp.int32)
    pair_onehot = (pair_experts[:, None] == expert_range[None, :]).astype(jnp.int32)
    earlier = jnp.cumsum(pair_onehot, axis=0) - pair_onehot
    slot_index = pair_experts * capacity + jnp.sum(earlier * pair_onehot, axis=1)
    expert_rows = (
        jnp.zeros((experts * capacity, features), jnp.bfloat16)
        .at[slot_index]
        .set(jnp.repeat(normed_two, TOPK, axis=0))
    )
    expert_rows = expert_rows.reshape(experts, capacity, features)
    hidden = jnp.einsum(
        "ecd,edf->ecf", expert_rows, inner_weight, preferred_element_type=jnp.float32
    )
    active = exact_gelu(hidden).astype(jnp.bfloat16)
    results = jnp.einsum(
        "ecf,efd->ecd", active, outer_weight, preferred_element_type=jnp.float32
    ).reshape(experts * capacity, features)
    picked = results[slot_index].reshape(token_count, TOPK, features)
    mixing = jnp.take_along_axis(gate_probs, routes, axis=1)
    outputs = residual + jnp.sum(mixing[:, :, None] * picked, axis=1)
    grad_out = grad_part.astype(jnp.float32).reshape(token_count, features)
    grad_gate = jnp.sum(grad_out[:, None, :] * picked, axis=2)
    grad_pairs = (
        (mixing[:, :, None] * grad_out[:, None, :])
        .reshape(token_count * TOPK, features)
        .astype(jnp.bfloat16)
    )
    grad_results = (
        jnp.zeros((experts * capacity, features), jnp.bfloat16).at[slot_index].set(grad_pairs)
    )
    grad_results = grad_results.reshape(experts, capacity, features)
    grad_active = jnp.einsum(
        "ecd,efd->ecf", grad_results, outer_weight, preferred_element_type=jnp.float32
    )
    gelu_pull = jax.vjp(exact_gelu, hidden)[1]
    grad_hidden = gelu_pull(grad_active)[0].astype(jnp.bfloat16)
    grad_outer = jnp.einsum(
        "ecf,ecd->efd", active, grad_results, preferred_element_type=jnp.float32
    )
    grad_inner = jnp.einsum(
        "ecd,ecf->edf", expert_rows, grad_hidden, preferred_element_type=jnp.float32
    )
    grad_rows = jnp.einsum(
        "ecf,edf->ecd", grad_hidden, inner_weight, preferred_element_type=jnp.float32
    ).astype(jnp.bfloat16)
    grad_rows = grad_rows.reshape(experts * capacity, features)
    grad_normed_two = jnp.sum(
        grad_rows[slot_index].reshape(token_count, TOPK, features).astype(jnp.float32), axis=1
    )
    chosen = (routes[:, :, None] == expert_range[None, None, :]).astype(jnp.float32)
    grad_gates = jnp.sum(grad_gate[:, :, None] * chosen, axis=1)
    grad_logits = gate_probs * (
        grad_gates - jnp.sum(gate_probs * grad_gates, axis=-1, keepdims=True)
    )
    grad_logits = grad_logits.astype(jnp.bfloat16)
    grad_router = jnp.dot(normed_two.T, grad_logits, preferred_element_type=jnp.float32)
    grad_normed_two = grad_normed_two + jnp.dot(
        grad_logits, router_weight.T, preferred_element_type=jnp.float32
    )
    norm_pull_two = jax.vjp(layer_norm, residual, gain_two, shift_two)[1]
    grad_residual, grad_gain_two, grad_shift_two = norm_pull_two(grad_normed_two)
    grad_residual = grad_residual + grad_out
    grad_attn = grad_residual.astype(jnp.bfloat16)
    grad_proj = jnp.dot(head_rows.T, grad_attn, preferred_element_type=jnp.float32)
    grad_heads = jnp.dot(grad_attn, proj_weight.T, preferred_element_type=jnp.float32).astype(
        jnp.bfloat16
    )
    grad_spread = lax.all_to_all(
        grad_heads.reshape(batch, places, groups, group_width),
        "seq",
        split_axis=2,
        concat_axis=1,
        tiled=True,
    )
    grad_mixed = grad_spread.reshape(batch, length, local_heads, HEAD)
    scores_again = attention_scores(queries, key_rows, key_valid)
    probs_full = jnp.exp(scores_again - log_total)
    probs_low = probs_full.astype(jnp.bfloat16)
    grad_values = jnp.einsum(
        "bhqk,bqhc->bkhc", probs_low, grad_mixed, preferred_element_type=jnp.float32
    )
    grad_probs = jnp.einsum(
        "bqhc,bkhc->bhqk", grad_mixed, values, preferred_element_type=jnp.float32
    )
    grad_scores = probs_full * (
        grad_probs - jnp.sum(probs_full * grad_probs, axis=-1, keepdims=True)
    )
    grad_scores = grad_scores.astype(jnp.bfloat16)
    grad_queries = jnp.einsum(
        "bhqk,bkhc->bqhc", grad_scores, key_rows, preferred_element_type=jnp.float32
    ) * HEAD ** (-0.5)
    grad_keys = jnp.einsum(
        "bhqk,bqhc->bkhc", grad_scores, queries, preferred_element_type=jnp.float32
    ) * HEAD ** (-0.5)
    stacked = jnp.stack([grad_queries, grad_keys, grad_values], axis=2).astype(jnp.bfloat16)
    stacked = stacked.reshape(batch, length, 3, 1, group_width)
    returned = lax.all_to_all(stacked, "seq", split_axis=1, concat_axis=3, tiled=True)
    grad_packed = returned.reshape(token_count, 3 * features)
    grad_qkv = jnp.dot(normed.T, grad_packed, preferred_element_type=jnp.float32)
    grad_normed = jnp.dot(grad_packed, qkv_weight.T, preferred_element_type=jnp.float32)
    norm_pull_one = jax.vjp(layer_norm, inputs, gain_one, shift_one)[1]
    grad_inputs, grad_gain_one, grad_shift_one = norm_pull_one(grad_normed)
    grad_tokens = (grad_inputs + grad_residual).reshape(batch, places, features)
    grads = (
        grad_gain_one,
        grad_shift_one,
        grad_qkv,
        grad_proj,
        grad_gain_two,
        grad_shift_two,
        grad_router,
        grad_inner,
        grad_outer,
    )
    return (outputs.astype(jnp.bfloat16).reshape(batch, places, features), grad_tokens, grads)


def body(
    tokens,
    key_mask,
    expert_ids,
    ln1_gain,
    ln1_bias,
    w_qkv,
    w_attn_out,
    ln2_gain,
    ln2_bias,
    router,
    w_in,
    w_out,
    cotangent,
):
    per_batch = tokens.shape[0] // MICRO
    totals = None
    out_parts = []
    grad_parts = []
    for batch_step in range(MICRO):
        fetched = (
            lax.all_gather(ln1_gain, "dp", axis=0, tiled=True),
            lax.all_gather(ln1_bias, "dp", axis=0, tiled=True),
            lax.all_gather(w_qkv, "dp", axis=0, tiled=True),
            lax.all_gather(w_attn_out, "dp", axis=0, tiled=True),
            lax.all_gather(ln2_gain, "dp", axis=0, tiled=True),
            lax.all_gather(ln2_bias, "dp", axis=0, tiled=True),
            lax.all_gather(router, "dp", axis=0, tiled=True),
            lax.all_gather(w_in, "dp", axis=1, tiled=True),
            lax.all_gather(w_out, "dp", axis=1, tiled=True),
        )
        first = batch_step * per_batch
        last = first + per_batch
        out_part, grad_part, grads = micro_step(
            fetched,
            tokens[first:last],
            key_mask[first:last],
            expert_ids[first:last],
            cotangent[first:last],
        )
        out_parts.append(out_part)
        grad_parts.append(grad_part)
        totals = grads if totals is None else jax.tree.map(jnp.add, totals, grads)
    totals = reduce_end(totals)
    return (
        jnp.concatenate(out_parts, axis=0),
        jnp.concatenate(grad_parts, axis=0),
        totals[0],
        totals[1],
        totals[2],
        totals[3],
        totals[4],
        totals[5],
        totals[6],
        totals[7],
        totals[8],
    )


def solution(mesh):
    placed = (
        P("dp", "seq", None),
        P("dp", None),
        P("dp", "seq", None),
        P("dp"),
        P("dp"),
        P("dp", None),
        P("dp", None),
        P("dp"),
        P("dp"),
        P("dp", None),
        P(None, "dp", None),
        P(None, "dp", None),
        P("dp", "seq", None),
    )
    whole = mesh.shape['dp'] == 8 and mesh.shape['seq'] == 4
    return jax.shard_map(
        plane_body if whole else body,
        mesh=mesh,
        in_specs=placed,
        out_specs=(
            P("dp", "seq", None),
            P("dp", "seq", None),
            P("dp"),
            P("dp"),
            P("dp", None),
            P("dp", None),
            P("dp"),
            P("dp"),
            P("dp", None),
            P(None, "dp", None),
            P(None, "dp", None),
        ),
        check_vma=False,
    )
```

```python
import jax
import jax.numpy as jnp
from jax import lax
from jax.experimental import pallas as pl
from jax.experimental.pallas import tpu as pltpu
from jax.sharding import PartitionSpec as P

MESH = pl.DeviceIdType.MESH
F32, BF16 = jnp.float32, jnp.bfloat16
HEADS = 12
HEAD = 64
NT = (((1,), (1,)), ((), ()))
TN = (((0,), (0,)), ((), ()))


def dot(a, b, dims=(((1,), (0,)), ((), ()))):
    return lax.dot_general(a, b, dims, preferred_element_type=F32)


def mult(value, by):
    return pl.multiple_of(value, by)


class Place:
    def __init__(self):
        self.dp = lax.axis_index("dp")
        self.s = lax.axis_index("seq")
        self.core = lax.rem(self.dp, 2)
        self.x = lax.rem(lax.div(self.dp, 2), 2)
        self.y = lax.div(self.dp, 4)

    def chip(self, k):
        if isinstance(k, int):
            kx, ky = k % 2, k // 2
        else:
            kx, ky = lax.rem(k, 2), lax.div(k, 2)
        x = self.x + kx * (1 - 2 * self.x)
        y = self.y + ky * (1 - 2 * self.y)
        return y * 2 + x

    def peer(self, k):
        return self.chip(k) * 2 + self.core

    def near(self):
        x = self.x + (1 - self.core) * (1 - 2 * self.x)
        y = self.y + self.core * (1 - 2 * self.y)
        return (y * 2 + x) * 2 + self.core

    def far(self):
        x = self.x + self.core * (1 - 2 * self.x)
        y = self.y + (1 - self.core) * (1 - 2 * self.y)
        return (y * 2 + x) * 2 + self.core

    def partner(self):
        return self.dp + 1 - 2 * self.core

    def around(self, k):
        return lax.rem(self.dp + k, 8)

    def plane(self, k):
        low, high = lax.rem(self.s, 2), lax.div(self.s, 2)
        if isinstance(k, int):
            kl, kh = k % 2, k // 2
        else:
            kl, kh = lax.rem(k, 2), lax.div(k, 2)
        return 2 * (high + kh * (1 - 2 * high)) + low + kl * (1 - 2 * low)


def entry_barrier(me):
    sem = pltpu.get_barrier_semaphore()
    for k in range(1, 8):
        pl.semaphore_signal(
            sem, inc=1, device_id={"dp": me.around(k)}, device_id_type=MESH
        )
    for k in range(1, 4):
        pl.semaphore_signal(
            sem, inc=1, device_id={"seq": me.plane(k)}, device_id_type=MESH
        )
    pl.semaphore_wait(sem, 10)


def remote(src, dst, send, recv, **where):
    return pltpu.make_async_remote_copy(
        src_ref=src, dst_ref=dst, send_sem=send, recv_sem=recv, device_id=where, device_id_type=MESH
    )


class PlaneGather:
    def __init__(self, me, src, place, send, recv, local=True):
        own = place(me.dp)
        self.sends = [
            remote(src, own, send.at[0], recv.at[0], dp=me.partner()),
            remote(src, own, send.at[1], recv.at[1], dp=me.peer(1)),
            remote(src, own, send.at[2], recv.at[2], dp=me.peer(2)),
        ]
        near = place(me.near())
        self.relay = remote(near, near, send.at[3], recv.at[3], dp=me.far())
        self.onward = []
        for k in range(1, 4):
            there = place(me.peer(k))
            self.onward.append(remote(there, there, send.at[3 + k], recv.at[3 + k], dp=me.partner()))
        self.local = pltpu.make_async_copy(src, own, send.at[7]) if local else None

    def start(self):
        for k in (1, 2, 0):
            self.sends[k].start()
        if self.local is not None:
            self.local.start()

    def forward(self):
        self.sends[1].wait_recv()
        self.sends[2].wait_recv()
        self.relay.start()
        self.onward[0].start()
        self.onward[1].start()

    def diagonal(self):
        self.relay.wait_recv()
        self.onward[2].start()

    def finish(self):
        self.sends[0].wait_recv()
        for copy in self.onward:
            copy.wait_recv()
        for copy in self.sends + self.onward + [self.relay]:
            copy.wait_send()
        if self.local is not None:
            self.local.wait()


class Spread:
    def __init__(self, me, src, place, send, recv, axis, local=True, first=1):
        count, step, own = (8, me.around, me.dp) if axis == "dp" else (4, me.plane, me.s)
        self.copies = [
            remote(src, place(own), send.at[k], recv.at[k], **{axis: step(k)})
            for k in range(first, count)
        ]
        self.local = pltpu.make_async_copy(src, place(own), send.at[0]) if local else None

    def start(self):
        for copy in self.copies:
            copy.start()
        if self.local is not None:
            self.local.start()

    def arrive(self):
        for copy in self.copies:
            copy.wait_recv()
        if self.local is not None:
            self.local.wait()

    def drain(self):
        for copy in self.copies:
            copy.wait_send()


class Deal:
    def __init__(self, me, source, place, send, recv):
        self.copies = [
            remote(source(me.plane(k)), place(me.s), send.at[k], recv.at[k], seq=me.plane(k))
            for k in range(1, 4)
        ]

    def start(self):
        for copy in self.copies:
            copy.start()

    def arrive(self):
        for copy in self.copies:
            copy.wait_recv()

    def drain(self):
        for copy in self.copies:
            copy.wait_send()


class PlaneHop:
    def __init__(self, me, blocks, send, recv):
        near = me.plane(1)
        self.copies, self.onward = [], []
        for c in range(4):
            d = 2 * c + me.core
            here, there = blocks.at[me.s, d], blocks.at[near, d]
            self.copies.append(remote(here, here, send.at[c], recv.at[c], seq=near))
            self.onward.append(remote(there, there, send.at[4 + c], recv.at[4 + c], dp=me.partner()))

    def start(self):
        for copy in self.copies:
            copy.start()

    def forward(self):
        for copy, onward in zip(self.copies, self.onward):
            copy.wait_recv()
            onward.start()

    def finish(self):
        for copy in self.onward:
            copy.wait_recv()
        for copy in self.copies + self.onward:
            copy.wait_send()


class RowSum:
    def __init__(self, me, grads, landed, passed, came, send, recv):
        self.me, self.grads, self.landed, self.passed, self.came = me, grads, landed, passed, came
        self.pair = [
            remote(grads.at[self.rows(k, 1 - me.core), :], landed.at[k], send.at[k], recv.at[k], dp=me.partner())
            for k in range(4)
        ]
        self.across = [
            remote(passed.at[k - 1], came.at[k - 1], send.at[3 + k], recv.at[3 + k], dp=me.peer(k))
            for k in range(1, 4)
        ]

    def rows(self, k, core):
        return pl.ds(mult(96 * (2 * self.me.chip(k) + core), 32), 96)

    def start(self):
        for copy in self.pair:
            copy.start()

    def pass_on(self):
        for k in (3, 1, 2):
            self.pair[k].wait_recv()
            kept = self.grads[self.rows(k, self.me.core), :].astype(F32)
            self.passed[k - 1] = (kept + self.landed[k].astype(F32)).astype(BF16)
            self.across[k - 1].start()

    def total(self):
        self.pair[0].wait_recv()
        total = self.grads[self.rows(0, self.me.core), :].astype(F32) + self.landed[0].astype(F32)
        for k in range(3):
            self.across[k].wait_recv()
            total = total + self.came[k].astype(F32)
        return total

    def drain(self):
        for copy in self.pair + self.across:
            copy.wait_send()


def norm_rows(rows, gain, shift):
    centre = rows - jnp.mean(rows, axis=-1, keepdims=True)
    spread = jnp.mean(centre * centre, axis=-1, keepdims=True)
    return centre * lax.rsqrt(spread + 1e-06) * gain + shift


def norm_back(values, grad, gain):
    centre = values - jnp.mean(values, axis=-1, keepdims=True)
    rstd = lax.rsqrt(jnp.mean(centre * centre, axis=-1, keepdims=True) + 1e-06)
    xhat = centre * rstd
    u = grad * gain
    back = rstd * (
        u - jnp.mean(u, axis=-1, keepdims=True)
        - xhat * jnp.mean(u * xhat, axis=-1, keepdims=True)
    )
    return back, jnp.sum(grad * xhat, axis=0, keepdims=True), jnp.sum(grad, axis=0, keepdims=True)


ERFC = (
    0.19786723623605862, 0.190899613780153, 0.23209140755646218, -0.027655803526181202,
    0.6019196159005862, -0.6722756114657328, 0.7990689737520851, -0.3864325349090697,
    0.06451709047710916,
)


def normal_parts(h):
    bell = jnp.exp(-0.5 * (h * h))
    t = 1.0 / (1.0 + (0.35 * 0.5**0.5) * jnp.abs(h))
    poly = jnp.full_like(t, 0.5 * ERFC[8])
    for c in ERFC[7::-1]:
        poly = poly * t + 0.5 * c
    tail = poly * t * bell
    return jnp.where(h < 0, tail, 1.0 - tail), h * bell * 0.3989422804014327


def mix_columns(mixes):
    pad = jnp.zeros((120, 128), F32)
    return jnp.concatenate([jnp.concatenate([m, pad], axis=0).T for m in mixes], axis=0)


def by_head(v):
    lane = lax.broadcasted_iota(jnp.int32, v.shape, 1)
    zero = jnp.zeros_like(v)
    return jnp.concatenate(
        [jnp.where((lane >= HEAD * h) & (lane < HEAD * h + HEAD), v, zero) for h in range(3)], axis=0
    )


def from_heads(v):
    lane = lax.broadcasted_iota(jnp.int32, (256, 256), 1)
    total = jnp.where(lane < HEAD, v[0:256], 0.0)
    for h in range(1, 3):
        own = (lane >= HEAD * h) & (lane < HEAD * h + HEAD)
        total = jnp.where(own, v[256 * h : 256 * h + 256], total)
    return total


def block_kernel(
    x, mask, ids, pk, w3, wo, win, g, wout,
    o_out, o_tok, o_gwo, o_att, o_gwi, o_small, o_gao,
    pkall, pvec, xall, xown, w3a, woa, wina, qkv, pr, hd, hx, res, gates, mixs, n2a, ga, mixa,
    acc, pulls, sums, p_recv, c_send, c_recv, gate_send, gate_recv, gwi, gwb,
    ghs, ghx, gnp, gnx, gq, q_land, q_pass, q_came, o_land, o_pass, o_came, zq, zo, zoa,
    small, small_z, small_p, small_sum,
    S, R,
):
    me = Place()
    entry_barrier(me)
    dp, s = me.dp, me.s
    first = mult(64 * s, 64)
    rows96 = lambda d: pl.ds(mult(96 * d, 32), 96)
    small_in = Spread(me, pk, lambda d: pkall.at[d], S.at[10], R.at[10], "dp")
    zx = Spread(me, x, lambda q: xall.at[:, pl.ds(mult(64 * q, 64), 64), :], S.at[16], R.at[16], "seq")
    gather_w3 = PlaneGather(me, w3, lambda d: w3a.at[rows96(d), :], S.at[0], R.at[0])
    gather_wo = PlaneGather(me, wo, lambda d: woa.at[rows96(d), :], S.at[1], R.at[1])
    gather_g = PlaneGather(me, g, lambda d: ga.at[s, d], S.at[2], R.at[2])
    gather_n2 = PlaneGather(me, n2a.at[s, dp], lambda d: n2a.at[s, d], S.at[3], R.at[3], local=False)
    zg = Spread(me, g, lambda q: ga.at[q, dp], S.at[17], R.at[17], "seq", local=False, first=2)
    zn = Spread(me, n2a.at[s, dp], lambda q: n2a.at[q, dp], S.at[18], R.at[18], "seq", local=False, first=2)
    zm = Spread(me, mixs, lambda q: mixa.at[q, dp], S.at[19], R.at[19], "seq", local=False)
    mix_own = Spread(me, mixs, lambda d: mixa.at[s, d], S.at[11], R.at[11], "dp")
    hop_n2, hop_g = PlaneHop(me, n2a, S.at[4], R.at[4]), PlaneHop(me, ga, S.at[5], R.at[5])
    gathers, mixers = [None], []
    for k in range(1, 4):
        q = me.plane(k)
        if k > 1:
            gathers.append([
                PlaneGather(me, n2a.at[q, dp], lambda d, q=q: n2a.at[q, d], S.at[2 + 2 * k], R.at[2 + 2 * k], local=False),
                PlaneGather(me, ga.at[q, dp], lambda d, q=q: ga.at[q, d], S.at[3 + 2 * k], R.at[3 + 2 * k], local=False),
            ])
        mixers.append(
            Spread(me, mixa.at[q, dp], lambda d, q=q: mixa.at[q, d], S.at[11 + k], R.at[11 + k], "dp", local=False)
        )
    small_in.start()
    zx.start()
    gather_w3.start()
    gather_wo.start()
    gather_g.start()
    small_in.arrive()
    total = jnp.zeros((16, 768), F32)
    row = lax.broadcasted_iota(jnp.int32, (128, 768), 0)
    col = lax.broadcasted_iota(jnp.int32, (128, 768), 1)
    for j in range(8):
        spot = jnp.where((row < 96) & (row + 96 * j == col), 1.0, 0.0).astype(BF16)
        total = total + dot(pkall[j], spot)
    pvec[...] = total
    woa[768:832, :] = jnp.zeros((64, 768), BF16)
    o_gwo[...] = jnp.zeros_like(o_gwo)
    gwi[...] = jnp.zeros_like(gwi)
    gather_w3.forward()
    gather_wo.forward()
    gather_g.forward()
    a2a = []
    for e in range(4):
        p, h = e // 2, e % 2
        for k in range(1, 8):
            t = me.around(k)
            a2a.append(
                remote(
                    win.at[e, :, pl.ds(mult(384 * t, 128), 384)],
                    wina.at[p, rows96(dp), 384 * h : 384 * h + 384],
                    S.at[31 + e, k], R.at[31 + e, k], dp=t,
                )
            )
        a2a.append(
            pltpu.make_async_copy(
                win.at[e, :, pl.ds(mult(384 * dp, 128), 384)],
                wina.at[p, rows96(dp), 384 * h : 384 * h + 384],
                S.at[31 + e, 0],
            )
        )
    for copy in a2a:
        copy.start()
    acc[...] = jnp.zeros_like(acc)
    pulls[...] = jnp.zeros_like(pulls)
    gather_w3.diagonal()
    gather_wo.diagonal()
    gather_g.diagonal()
    zx.arrive()

    xown[...] = xall[:, pl.ds(first, 64), :]

    def ln_step(i, carry):
        xall[i] = norm_rows(xall[i].astype(F32), pvec[4:5, :], pvec[5:6, :]).astype(BF16)
        return carry

    lax.fori_loop(0, 2, ln_step, 0)
    gather_w3.finish()

    def attend(i, carry):
        for kind in range(3):
            qkv[kind, i] = dot(xall[i], w3a[:, 256 * kind : 256 * kind + 256]).astype(BF16)
        scores = dot(by_head(qkv[0, i]), qkv[1, i], NT) * HEAD ** (-0.5)
        scores = jnp.where(mask[pl.ds(i, 1), :] > 0, scores, -1e30)
        terms = jnp.exp(scores - jnp.max(scores, axis=-1, keepdims=True))
        probs = terms / jnp.sum(terms, axis=-1, keepdims=True)
        pr[i] = probs
        hd[i] = from_heads(dot(probs.astype(BF16), qkv[2, i])).astype(BF16)
        return carry

    lax.fori_loop(0, 2, attend, 0)
    deal_heads = Deal(me, lambda q: hd.at[:, pl.ds(mult(64 * q, 64), 64), :], lambda q: hx.at[q], S.at[20], R.at[20])
    deal_heads.start()
    hx[s] = hd[:, pl.ds(first, 64), :]
    gather_wo.finish()
    deal_heads.arrive()
    zg.start()
    tokens = xown[...].reshape(128, 768).astype(F32)
    mixed = tokens
    for q in range(4):
        mixed = mixed + dot(hx[q].reshape(128, 256), woa[192 * q : 192 * q + 256, :])
    res[...] = mixed
    own_n2 = norm_rows(mixed, pvec[6:7, :], pvec[7:8, :]).astype(BF16)
    n2a[s, dp] = own_n2
    gather_n2.start()
    zn.start()
    router = jnp.concatenate([pvec[0:4, :].astype(BF16), jnp.zeros((124, 768), BF16)], axis=0)
    lane = lax.broadcasted_iota(jnp.int32, (128, 128), 1)
    logits = jnp.where(lane < 4, dot(own_n2, router, NT), -1e30)
    terms = jnp.exp(logits - jnp.max(logits, axis=-1, keepdims=True))
    probs4 = terms / jnp.sum(terms, axis=-1, keepdims=True)
    gates[...] = probs4
    chosen = (lane == ids[:, 0:1]) | (lane == ids[:, 1:2])
    mixs[...] = jnp.where(chosen, probs4, 0.0).T[0:8, :]
    mix_own.start()
    zm.start()
    gather_g.finish()
    hop_g.start()
    gather_n2.forward()
    gather_n2.diagonal()
    for copy in a2a[:16]:
        copy.wait()
    gather_n2.finish()
    hop_n2.start()
    mix_own.arrive()

    def pair_step(p, n2c, gc, columns):
        many = n2c.shape[0]
        lanes = lax.broadcasted_iota(jnp.int32, (many, 128), 1)
        low = jnp.sum(jnp.where(lanes == 2 * p, columns, 0.0), axis=1, keepdims=True)
        high = jnp.sum(jnp.where(lanes == 2 * p + 1, columns, 0.0), axis=1, keepdims=True)
        gate = jnp.where(lax.broadcasted_iota(jnp.int32, (many, 768), 1) < 384, low, high)
        hidden = dot(n2c, wina[p])
        pull = dot(gc, wout[p], NT)
        phi, slope = normal_parts(hidden)
        active = hidden * phi
        taken = (gate * active).astype(BF16)
        grad_hidden = (gate * pull * (phi + slope)).astype(BF16)
        gwi[p] += dot(n2c, grad_hidden, TN)
        return active, pull, taken, grad_hidden

    def pair_copy(k, which):
        other = 2 * me.chip(k) + 1 - me.core
        at = 4 * which + k
        return remote(sums.at[which, other], p_recv.at[which, k], S.at[29, at], R.at[29, at], dp=me.partner())

    def across_copy(k, which):
        at = 3 * which + k - 1
        return remote(
            c_send.at[which, k - 1], c_recv.at[which, k - 1], S.at[30, at], R.at[30, at], dp=me.peer(k)
        )

    def gate_copy(k, b):
        target = 2 * me.chip(k) + (1 - me.core if b else me.core)
        at = 2 * k + b
        return remote(gate_send.at[target], gate_recv.at[at], S.at[28, at], R.at[28, at], dp=target)

    def push(k, which):
        pair_copy(k, which).wait_recv()
        total = sums[which, 2 * me.chip(k) + me.core].astype(F32) + p_recv[which, k].astype(F32)
        c_send[which, k - 1] = total.astype(BF16)
        across_copy(k, which).start()

    def own_step(t, carry):
        p, i = lax.div(t, 4), lax.rem(t, 4)
        k = 3 - i
        c = me.chip(k)

        @pl.when(t == 4)
        def _():
            for copy in a2a[16:]:
                copy.wait()
            zg.arrive()
            gathers[1][1].start()
            zn.arrive()
            gathers[1][0].start()
            zm.arrive()
            for one in mixers:
                one.start()

        @pl.when(t == 6)
        def _():
            hop_g.forward()

        columns = mix_columns([mixa[s, 2 * c], mixa[s, 2 * c + 1]])
        n2c = n2a[s, pl.ds(2 * c, 2)].reshape(256, 768)
        gc = ga[s, pl.ds(2 * c, 2)].reshape(256, 768)
        active, pull, taken, grad_hidden = pair_step(p, n2c, gc, columns)
        acc[0, i] += dot(grad_hidden, wina[p], NT)
        acc[1, i] += dot(taken, wout[p])
        o_gwo[p] += dot(taken, gc, TN)
        inner = active * pull
        low = jnp.sum(inner[:, :384], axis=1, keepdims=True)
        high = jnp.sum(inner[:, 384:], axis=1, keepdims=True)
        lanes = lax.broadcasted_iota(jnp.int32, (256, 128), 1)
        pulls[i] = jnp.where(lanes == 2 * p, low, jnp.where(lanes == 2 * p + 1, high, pulls[i]))

        @pl.when(p == 1)
        def _():
            for b in range(2):
                sums[0, 2 * c + b] = acc[0, i, 128 * b : 128 * b + 128].astype(BF16)
                sums[1, 2 * c + b] = acc[1, i, 128 * b : 128 * b + 128].astype(BF16)
                gate_send[2 * c + b] = pulls[i, 128 * b : 128 * b + 128].T[0:8, :]
            pair_copy(k, 0).start()
            gate_copy(k, 1).start()

        @pl.when((p == 1) & (k > 0))
        def _():
            gate_copy(k, 0).start()

        @pl.when(t > 4)
        def _():
            push(k + 1, 0)

        return carry

    lax.fori_loop(0, 8, own_step, 0)
    pair_copy(0, 0).wait_recv()
    for k in range(4):
        pair_copy(k, 1).start()
    for k in range(4):
        if k:
            across_copy(k, 0).wait_recv()
            gate_copy(k, 0).wait_recv()
        gate_copy(k, 1).wait_recv()
    hop_n2.forward()

    def summed(which):
        total = sums[which, dp].astype(F32) + p_recv[which, 0].astype(F32)
        for k in range(3):
            total = total + c_recv[which, k].astype(F32)
        return total

    gate_sum = gate_send[dp]
    for k in range(1, 8):
        gate_sum = gate_sum + gate_recv[k]
    grad_gate = jnp.concatenate([gate_sum, jnp.zeros((120, 128), F32)], axis=0).T
    lane = lax.broadcasted_iota(jnp.int32, (128, 128), 1)
    chosen = (lane == ids[:, 0:1]) | (lane == ids[:, 1:2])
    grad_gate = jnp.where(chosen, grad_gate, 0.0)
    probs4 = gates[...]
    grad_logits = probs4 * (grad_gate - jnp.sum(probs4 * grad_gate, axis=-1, keepdims=True))
    grad_logits = grad_logits.astype(BF16)
    router = jnp.concatenate([pvec[0:4, :].astype(BF16), jnp.zeros((124, 768), BF16)], axis=0)
    small[...] = dot(grad_logits, n2a[s, dp], TN)[0:8, :]
    grad_n2 = summed(0) + dot(grad_logits, router)
    back, gain2, shift2 = norm_back(res[...], grad_n2, pvec[6:7, :])
    small[6:7, :] = gain2
    small[7:8, :] = shift2
    grad_res = back + ga[s, dp].astype(F32)
    o_tok[...] = grad_res
    grb = grad_res.astype(BF16)
    lane = lax.broadcasted_iota(jnp.int32, (128, 256), 1)
    for q in range(4):
        pulled = dot(grb, woa[192 * q : 192 * q + 256, :], NT)
        ghs[q] = jnp.where(lane < 192, pulled, 0.0).astype(BF16).reshape(2, 64, 256)
    deal_grads = Deal(me, lambda q: ghs.at[q], lambda q: ghx.at[q], S.at[21], R.at[21])
    deal_grads.start()
    ghx[s] = ghs[s]
    for q in range(4):
        gwb[192 * q : 192 * q + 192, :] = dot(hx[q].reshape(128, 256), grb, TN)[0:192].astype(BF16)
    sum_o = RowSum(me, gwb, o_land, o_pass, o_came, S.at[27], R.at[27])
    sum_o.start()
    for one in gathers[1]:
        one.forward()
    for one in gathers[2]:
        one.start()
    for one in mixers:
        one.arrive()
    hop_g.finish()
    hop_n2.finish()

    def attend_back(i, carry):
        grads = by_head(ghx[:, pl.ds(i, 1)].reshape(256, 256))
        queries = by_head(qkv[0, i])
        keys, vals, probs = qkv[1, i], qkv[2, i], pr[i]
        at = pl.ds(2 * i, 2)
        scale = HEAD ** (-0.5)
        p_recv[0, at, :, 512:768] = dot(probs.astype(BF16), grads, TN).astype(BF16).reshape(2, 128, 256)
        grad_probs = dot(grads, vals, NT)
        inner = jnp.sum(probs * grad_probs, axis=-1, keepdims=True)
        grad_scores = (probs * (grad_probs - inner)).astype(BF16)
        grad_q = (from_heads(dot(grad_scores, keys)) * scale).astype(BF16)
        p_recv[0, at, :, 0:256] = grad_q.reshape(2, 128, 256)
        grad_k = (dot(grad_scores, queries, TN) * scale).astype(BF16)
        p_recv[0, at, :, 256:512] = grad_k.reshape(2, 128, 256)
        gnp[i] = dot(p_recv[0, at].reshape(256, 768), w3a[...], NT).astype(BF16)
        return carry

    deal_norm = Deal(me, lambda q: gnp.at[:, pl.ds(mult(64 * q, 64), 64), :], lambda q: gnx.at[q], S.at[22], R.at[22])

    def weights(t, carry):
        at = pl.ds(mult(256 * t, 256), 256)
        gq[:, at] = dot(xall[...].reshape(512, 768), p_recv[0, :, :, at].reshape(512, 256), TN).astype(BF16)
        return carry

    sum_q = RowSum(me, gq, q_land, q_pass, q_came, S.at[26], R.at[26])
    spread_o = Spread(me, zo, lambda q: zoa.at[q], S.at[25], R.at[25], "seq")
    spread_q = Spread(me, zq, lambda q: o_att.at[q], S.at[24], R.at[24], "seq")
    spread_small = Spread(me, small, lambda q: small_z.at[q], S.at[23], R.at[23], "seq")
    plane_small = Spread(me, small_sum, lambda d: small_p.at[d], S.at[15], R.at[15], "dp")

    def reshard_copies(p):
        copies = []
        for h in range(2):
            e = 2 * p + h
            for k in range(8):
                t = me.around(k) if k else dp
                source = gwb.at[rows96(t), 384 * h : 384 * h + 384]
                target = o_gwi.at[e, :, pl.ds(mult(384 * dp, 128), 384)]
                if k:
                    copies.append(remote(source, target, S.at[35 + e, k], R.at[35 + e, k], dp=t))
                else:
                    copies.append(pltpu.make_async_copy(source, target, S.at[35 + e, 0]))
        return copies

    reshards = [reshard_copies(0), reshard_copies(1)]

    def reshard(p):
        def cast(t, carry):
            at = pl.ds(mult(96 * t, 32), 96)
            gwb[at, :] = gwi[p, at, :].astype(BF16)
            return carry

        lax.fori_loop(0, 8, cast, 0)
        for copy in reshards[p]:
            copy.start()

    def stage_1():
        sum_o.pass_on()
        for k in range(1, 4):
            push(k, 1)
        for one in gathers[1]:
            one.diagonal()

    def stage_2():
        deal_grads.arrive()
        lax.fori_loop(0, 2, attend_back, 0)
        deal_norm.start()
        gnx[s] = gnp[:, pl.ds(first, 64), :]
        lax.fori_loop(0, 3, weights, 0)
        sum_q.start()
        for one in gathers[2]:
            one.forward()

    def stage_3():
        sum_q.pass_on()
        for one in gathers[2]:
            one.diagonal()
        zo[...] = sum_o.total().astype(BF16)
        spread_o.start()

    def stage_4():
        for one in gathers[1]:
            one.finish()

    def stage_5():
        deal_norm.arrive()
        grad_n1 = jnp.zeros((128, 768), F32)
        for q in range(4):
            grad_n1 = grad_n1 + gnx[q].reshape(128, 768).astype(F32)
        tokens = xown[...].reshape(128, 768).astype(F32)
        back, gain1, shift1 = norm_back(tokens, grad_n1, pvec[4:5, :])
        o_tok[...] = back + o_tok[...]
        small[4:5, :] = gain1
        small[5:6, :] = shift1
        spread_small.start()

    def stage_6():
        zq[...] = sum_q.total().astype(BF16)
        spread_q.start()
        for one in gathers[2]:
            one.finish()

    def stage_7():
        pair_copy(0, 1).wait_recv()
        for k in range(1, 4):
            across_copy(k, 1).wait_recv()
        o_out[...] = (res[...] + summed(1)).astype(BF16)

    def stage_8():
        sum_o.drain()
        for which in range(2):
            for k in range(4):
                pair_copy(k, which).wait_send()
        reshard(0)
        spread_small.arrive()
        small_sum[...] = small_z[0] + small_z[1] + small_z[2] + small_z[3]
        plane_small.start()

    stages = (stage_1, stage_2, stage_3, stage_4, stage_5, stage_6, stage_7, stage_8)

    def other_step(t, carry):
        for at, stage in enumerate(stages):
            pl.when(t == at + 1)(stage)
        far = lax.div(t, 4)
        inner = lax.rem(t, 4)
        p = jnp.where(far == 0, lax.rem(t, 2), far - 1)
        q = me.plane(jnp.where(far == 0, 1, 2 + lax.div(inner, 2)))
        b = jnp.where(far == 0, lax.div(inner, 2), lax.rem(t, 2))
        columns = mix_columns([mixa[q, 4 * b + j] for j in range(4)])
        n2c = n2a[q, pl.ds(4 * b, 4)].reshape(512, 768)
        gc = ga[q, pl.ds(4 * b, 4)].reshape(512, 768)
        taken = pair_step(p, n2c, gc, columns)[2]

        @pl.when(t < 4)
        def _():
            o_gwo[p] += dot(taken, gc, TN)

        @pl.when((t >= 4) & (t < 8))
        def _():
            acc[lax.div(inner, 2), pl.ds(2 * lax.rem(inner, 2), 2)] = taken.astype(F32).reshape(2, 256, 768)

        @pl.when(t >= 8)
        def _():
            sums[lax.div(inner, 2), pl.ds(4 * lax.rem(inner, 2), 4)] = taken.reshape(4, 128, 768)

        return carry

    lax.fori_loop(0, 12, other_step, 0)
    for copy in reshards[0]:
        copy.wait()
    reshard(1)

    def last_products(j, carry):
        q = me.plane(2 + lax.div(j, 2))
        gc = ga[q, pl.ds(4 * lax.rem(j, 2), 4)].reshape(512, 768)
        h, b = lax.div(j, 2), lax.rem(j, 2)
        early = acc[h, pl.ds(2 * b, 2)].reshape(512, 768).astype(BF16)
        o_gwo[0] += dot(early, gc, TN)
        taken = sums[h, pl.ds(4 * b, 4)].reshape(512, 768)
        o_gwo[1] += dot(taken, gc, TN)
        return carry

    lax.fori_loop(0, 4, last_products, 0)
    plane_small.arrive()
    total = small_p[0]
    for k in range(1, 8):
        total = total + small_p[k]
    o_small[...] = total
    spread_o.arrive()
    total = zoa[0].astype(F32)
    for q in range(1, 4):
        total = total + zoa[q].astype(F32)
    o_gao[...] = total
    spread_q.arrive()
    for copy in reshards[1]:
        copy.wait()
    for which in range(2):
        for k in range(1, 4):
            across_copy(k, which).wait_send()
    for k in range(4):
        if k:
            gate_copy(k, 0).wait_send()
        gate_copy(k, 1).wait_send()
    for one in mixers + [
        small_in, zx, zg, zn, zm, mix_own, deal_heads, deal_grads, deal_norm, sum_q,
        spread_o, spread_q, spread_small, plane_small,
    ]:
        one.drain()


VM = pl.BlockSpec(memory_space=pltpu.VMEM)
ANY = pl.BlockSpec(memory_space=pl.ANY)
DMA = pltpu.SemaphoreType.DMA


def sds(shape, dtype=BF16):
    return jax.ShapeDtypeStruct(shape, dtype)


def run_block(x, mask, ids, pk, w3, wo, win, g, wout):
    V = pltpu.VMEM
    return pl.pallas_call(
        block_kernel,
        out_shape=[
            sds((128, 768)), sds((128, 768), F32), sds((2, 768, 768), F32), sds((4, 96, 768)),
            sds((4, 96, 3072)), sds((8, 768), F32), sds((96, 768), F32),
        ],
        in_specs=[ANY, VM, VM, VM, ANY, ANY, ANY, ANY, VM],
        out_specs=[VM, VM, VM, ANY, ANY, VM, VM],
        scratch_shapes=[
            V((8, 16, 128), BF16), V((16, 768), F32), V((2, 256, 768), BF16), V((2, 64, 768), BF16),
            V((768, 768), BF16), V((832, 768), BF16), V((2, 768, 768), BF16), V((3, 2, 256, 256), BF16),
            V((2, 768, 256), F32), V((2, 256, 256), BF16), V((4, 2, 64, 256), BF16), V((128, 768), F32),
            V((128, 128), F32), V((8, 128), F32), V((4, 8, 128, 768), BF16), V((4, 8, 128, 768), BF16),
            V((4, 8, 8, 128), F32),
            V((2, 4, 256, 768), F32), V((4, 256, 128), F32),
            V((2, 8, 128, 768), BF16),
            V((2, 4, 128, 768), BF16), V((2, 3, 128, 768), BF16), V((2, 3, 128, 768), BF16),
            V((8, 8, 128), F32), V((8, 8, 128), F32), V((2, 768, 768), F32), V((768, 768), BF16),
            V((4, 2, 64, 256), BF16), V((4, 2, 64, 256), BF16),
            V((2, 256, 768), BF16), V((4, 2, 64, 768), BF16), V((768, 768), BF16),
            V((4, 96, 768), BF16), V((3, 96, 768), BF16), V((3, 96, 768), BF16),
            V((4, 96, 768), BF16), V((3, 96, 768), BF16), V((3, 96, 768), BF16),
            V((96, 768), BF16), V((96, 768), BF16), V((4, 96, 768), BF16),
            V((8, 768), F32), V((4, 8, 768), F32), V((8, 8, 768), F32), V((8, 768), F32),
            DMA((40, 8)), DMA((40, 8)),
        ],
        compiler_params=pltpu.CompilerParams(
            collective_id=0, has_side_effects=True, vmem_limit_bytes=67043328
        ),
        name="block",
    )(x, mask, ids, pk, w3, wo, win, g, wout)


def widen_kernel(low, full, att, tok, out, gao, o_low, o_full, o_att, o_tok, o_out, o_gao):
    o_low[...] = low[...].astype(F32)
    o_full[...] = full[...]
    o_tok[...] = tok[...]
    o_out[...] = out[...]

    @pl.when(pl.program_id(0) == 0)
    def _():
        o_gao[...] = gao[...]
        for kind in range(3):
            for q in range(4):
                at = 768 * kind + 192 * q
                o_att[:, at : at + 192] = att[q, :, 256 * kind : 256 * kind + 192].astype(F32)


def widen(low, full, att, tok, out, gao):
    def spec(rows, columns):
        return pl.BlockSpec((rows, columns), lambda i: (i, 0))

    def whole(*shape):
        return pl.BlockSpec(shape, lambda i: (0,) * len(shape))

    return pl.pallas_call(
        widen_kernel,
        grid=(8,),
        out_shape=[
            sds((384, 3072), F32), sds((1536, 768), F32), sds((96, 2304), F32),
            sds((128, 768), F32), sds((128, 768)), sds((96, 768), F32),
        ],
        in_specs=[
            spec(48, 3072), spec(192, 768), whole(4, 96, 768), spec(16, 768), spec(16, 768), whole(96, 768),
        ],
        out_specs=[
            spec(48, 3072), spec(192, 768), whole(96, 2304), spec(16, 768), spec(16, 768), whole(96, 768),
        ],
        name="widen",
    )(low, full, att, tok, out, gao)


def pack_small(ln1_gain, ln1_bias, ln2_gain, ln2_bias, router):
    rows = jnp.concatenate(
        [router.T, ln1_gain[None], ln1_bias[None], ln2_gain[None], ln2_bias[None]], axis=0
    )
    return jnp.pad(rows, ((0, 8), (0, 32)))


def plane_body(tokens, key_mask, expert_ids, ln1_gain, ln1_bias, w_qkv, w_attn_out, ln2_gain,
               ln2_bias, router, w_in, w_out, cotangent):
    pk = pack_small(ln1_gain, ln1_bias, ln2_gain, ln2_bias, router)
    first = 192 * lax.axis_index("seq")
    parts = [lax.dynamic_slice_in_dim(w_qkv, 768 * kind + first, 192, axis=1) for kind in range(3)]
    w3 = jnp.concatenate([jnp.pad(part, ((0, 0), (0, 64))) for part in parts], axis=1)
    out, tok, gwo, att, gwi, small, gao = run_block(
        tokens, key_mask, expert_ids.reshape(128, 2), pk, w3, w_attn_out, w_in,
        cotangent.reshape(128, 768), w_out.reshape(2, 768, 768),
    )
    own = lax.dynamic_slice_in_dim(small, 96 * lax.axis_index("dp"), 96, axis=1)
    shape = tokens.shape
    gwi, gwo, att, tok, out, gao = widen(
        gwi.reshape(384, 3072), gwo.reshape(1536, 768), att, tok, out, gao
    )
    return (
        out.reshape(shape), tok.reshape(shape), own[4], own[5], att, gao, own[6], own[7],
        own[0:4].T, gwi.reshape(4, 96, 3072), gwo.reshape(4, 384, 768),
    )


TOPK = 2
MOST = 40
MICRO = 2


def layer_norm(inputs, norm_gain, norm_shift):
    centre = inputs - jnp.mean(inputs, axis=-1, keepdims=True)
    spread = jnp.mean(centre * centre, axis=-1, keepdims=True)
    return centre * lax.rsqrt(spread + 1e-06) * norm_gain + norm_shift


def softmax_rows(scores):
    row_max = jnp.max(scores, axis=-1, keepdims=True)
    expo_terms = jnp.exp(scores - row_max)
    return expo_terms / jnp.sum(expo_terms, axis=-1, keepdims=True)


def exact_gelu(inputs):
    return jax.nn.gelu(inputs, approximate=False)


def attention_scores(queries, key_rows, key_valid):
    scores = jnp.einsum(
        "bqhc,bkhc->bhqk", queries, key_rows, preferred_element_type=jnp.float32
    ) * HEAD ** (-0.5)
    return jnp.where(key_valid, scores, -1e30)


def reduce_end(grads):
    shares = (
        lax.psum_scatter(grads[0], "dp", scatter_dimension=0, tiled=True),
        lax.psum_scatter(grads[1], "dp", scatter_dimension=0, tiled=True),
        lax.psum_scatter(grads[2], "dp", scatter_dimension=0, tiled=True),
        lax.psum_scatter(grads[3], "dp", scatter_dimension=0, tiled=True),
        lax.psum_scatter(grads[4], "dp", scatter_dimension=0, tiled=True),
        lax.psum_scatter(grads[5], "dp", scatter_dimension=0, tiled=True),
        lax.psum_scatter(grads[6], "dp", scatter_dimension=0, tiled=True),
        lax.psum_scatter(grads[7], "dp", scatter_dimension=1, tiled=True),
        lax.psum_scatter(grads[8], "dp", scatter_dimension=1, tiled=True),
    )
    quarters = (
        lax.psum_scatter(
            shares[0].astype(jnp.bfloat16), "seq", scatter_dimension=0, tiled=True
        ).astype(jnp.float32),
        lax.psum_scatter(
            shares[1].astype(jnp.bfloat16), "seq", scatter_dimension=0, tiled=True
        ).astype(jnp.float32),
        lax.psum_scatter(
            shares[2].astype(jnp.bfloat16), "seq", scatter_dimension=0, tiled=True
        ).astype(jnp.float32),
        lax.psum_scatter(
            shares[3].astype(jnp.bfloat16), "seq", scatter_dimension=0, tiled=True
        ).astype(jnp.float32),
        lax.psum_scatter(
            shares[4].astype(jnp.bfloat16), "seq", scatter_dimension=0, tiled=True
        ).astype(jnp.float32),
        lax.psum_scatter(
            shares[5].astype(jnp.bfloat16), "seq", scatter_dimension=0, tiled=True
        ).astype(jnp.float32),
        lax.psum_scatter(
            shares[6].astype(jnp.bfloat16), "seq", scatter_dimension=0, tiled=True
        ).astype(jnp.float32),
        lax.psum_scatter(
            shares[7].astype(jnp.bfloat16), "seq", scatter_dimension=1, tiled=True
        ).astype(jnp.float32),
        lax.psum_scatter(
            shares[8].astype(jnp.bfloat16), "seq", scatter_dimension=1, tiled=True
        ).astype(jnp.float32),
    )
    return (
        lax.all_gather(quarters[0].astype(jnp.bfloat16), "seq", axis=0, tiled=True).astype(
            jnp.float32
        ),
        lax.all_gather(quarters[1].astype(jnp.bfloat16), "seq", axis=0, tiled=True).astype(
            jnp.float32
        ),
        lax.all_gather(quarters[2].astype(jnp.bfloat16), "seq", axis=0, tiled=True).astype(
            jnp.float32
        ),
        lax.all_gather(quarters[3].astype(jnp.bfloat16), "seq", axis=0, tiled=True).astype(
            jnp.float32
        ),
        lax.all_gather(quarters[4].astype(jnp.bfloat16), "seq", axis=0, tiled=True).astype(
            jnp.float32
        ),
        lax.all_gather(quarters[5].astype(jnp.bfloat16), "seq", axis=0, tiled=True).astype(
            jnp.float32
        ),
        lax.all_gather(quarters[6].astype(jnp.bfloat16), "seq", axis=0, tiled=True).astype(
            jnp.float32
        ),
        lax.all_gather(quarters[7].astype(jnp.bfloat16), "seq", axis=1, tiled=True).astype(
            jnp.float32
        ),
        lax.all_gather(quarters[8].astype(jnp.bfloat16), "seq", axis=1, tiled=True).astype(
            jnp.float32
        ),
    )


def micro_step(weights, tokens_part, mask_part, routes_part, grad_part):
    (
        norm1_gain,
        norm1_shift,
        qkv_weight,
        proj_weight,
        norm2_gain,
        norm2_shift,
        router_weight,
        inner_weight,
        outer_weight,
    ) = weights
    batch, places, features = tokens_part.shape
    groups = lax.axis_size("seq")
    length = mask_part.shape[1]
    group_width = features // groups
    local_heads = HEADS // groups
    experts = inner_weight.shape[0]
    capacity = batch * MOST
    token_count = batch * places
    gain_one = norm1_gain.astype(jnp.float32)
    shift_one = norm1_shift.astype(jnp.float32)
    gain_two = norm2_gain.astype(jnp.float32)
    shift_two = norm2_shift.astype(jnp.float32)
    inputs = tokens_part.astype(jnp.float32).reshape(token_count, features)
    normed = layer_norm(inputs, gain_one, shift_one).astype(jnp.bfloat16)
    packed = jnp.dot(normed, qkv_weight, preferred_element_type=jnp.float32).astype(jnp.bfloat16)
    packed = packed.reshape(batch, places, 3, groups, group_width)
    spread = lax.all_to_all(packed, "seq", split_axis=3, concat_axis=1, tiled=True)
    queries = spread[:, :, 0, 0].reshape(batch, length, local_heads, HEAD)
    key_rows = spread[:, :, 1, 0].reshape(batch, length, local_heads, HEAD)
    values = spread[:, :, 2, 0].reshape(batch, length, local_heads, HEAD)
    key_valid = mask_part[:, None, None, :] > 0
    scores = attention_scores(queries, key_rows, key_valid)
    row_max = jnp.max(scores, axis=-1, keepdims=True)
    expo_terms = jnp.exp(scores - row_max)
    row_total = jnp.sum(expo_terms, axis=-1, keepdims=True)
    log_total = row_max + jnp.log(row_total)
    attn_probs = (expo_terms / row_total).astype(jnp.bfloat16)
    mixed_heads = jnp.einsum(
        "bhqk,bkhc->bqhc", attn_probs, values, preferred_element_type=jnp.float32
    ).astype(jnp.bfloat16)
    joined = lax.all_to_all(
        mixed_heads.reshape(batch, length, 1, group_width),
        "seq",
        split_axis=1,
        concat_axis=2,
        tiled=True,
    )
    head_rows = joined.reshape(token_count, features)
    residual = inputs + jnp.dot(head_rows, proj_weight, preferred_element_type=jnp.float32)
    normed_two = layer_norm(residual, gain_two, shift_two).astype(jnp.bfloat16)
    gate_probs = softmax_rows(
        jnp.dot(normed_two, router_weight, preferred_element_type=jnp.float32)
    )
    routes = routes_part.reshape(token_count, TOPK)
    pair_experts = routes.reshape(-1)
    expert_range = jnp.arange(experts, dtype=jnp.int32)
    pair_onehot = (pair_experts[:, None] == expert_range[None, :]).astype(jnp.int32)
    earlier = jnp.cumsum(pair_onehot, axis=0) - pair_onehot
    slot_index = pair_experts * capacity + jnp.sum(earlier * pair_onehot, axis=1)
    expert_rows = (
        jnp.zeros((experts * capacity, features), jnp.bfloat16)
        .at[slot_index]
        .set(jnp.repeat(normed_two, TOPK, axis=0))
    )
    expert_rows = expert_rows.reshape(experts, capacity, features)
    hidden = jnp.einsum(
        "ecd,edf->ecf", expert_rows, inner_weight, preferred_element_type=jnp.float32
    )
    active = exact_gelu(hidden).astype(jnp.bfloat16)
    results = jnp.einsum(
        "ecf,efd->ecd", active, outer_weight, preferred_element_type=jnp.float32
    ).reshape(experts * capacity, features)
    picked = results[slot_index].reshape(token_count, TOPK, features)
    mixing = jnp.take_along_axis(gate_probs, routes, axis=1)
    outputs = residual + jnp.sum(mixing[:, :, None] * picked, axis=1)
    grad_out = grad_part.astype(jnp.float32).reshape(token_count, features)
    grad_gate = jnp.sum(grad_out[:, None, :] * picked, axis=2)
    grad_pairs = (
        (mixing[:, :, None] * grad_out[:, None, :])
        .reshape(token_count * TOPK, features)
        .astype(jnp.bfloat16)
    )
    grad_results = (
        jnp.zeros((experts * capacity, features), jnp.bfloat16).at[slot_index].set(grad_pairs)
    )
    grad_results = grad_results.reshape(experts, capacity, features)
    grad_active = jnp.einsum(
        "ecd,efd->ecf", grad_results, outer_weight, preferred_element_type=jnp.float32
    )
    gelu_pull = jax.vjp(exact_gelu, hidden)[1]
    grad_hidden = gelu_pull(grad_active)[0].astype(jnp.bfloat16)
    grad_outer = jnp.einsum(
        "ecf,ecd->efd", active, grad_results, preferred_element_type=jnp.float32
    )
    grad_inner = jnp.einsum(
        "ecd,ecf->edf", expert_rows, grad_hidden, preferred_element_type=jnp.float32
    )
    grad_rows = jnp.einsum(
        "ecf,edf->ecd", grad_hidden, inner_weight, preferred_element_type=jnp.float32
    ).astype(jnp.bfloat16)
    grad_rows = grad_rows.reshape(experts * capacity, features)
    grad_normed_two = jnp.sum(
        grad_rows[slot_index].reshape(token_count, TOPK, features).astype(jnp.float32), axis=1
    )
    chosen = (routes[:, :, None] == expert_range[None, None, :]).astype(jnp.float32)
    grad_gates = jnp.sum(grad_gate[:, :, None] * chosen, axis=1)
    grad_logits = gate_probs * (
        grad_gates - jnp.sum(gate_probs * grad_gates, axis=-1, keepdims=True)
    )
    grad_logits = grad_logits.astype(jnp.bfloat16)
    grad_router = jnp.dot(normed_two.T, grad_logits, preferred_element_type=jnp.float32)
    grad_normed_two = grad_normed_two + jnp.dot(
        grad_logits, router_weight.T, preferred_element_type=jnp.float32
    )
    norm_pull_two = jax.vjp(layer_norm, residual, gain_two, shift_two)[1]
    grad_residual, grad_gain_two, grad_shift_two = norm_pull_two(grad_normed_two)
    grad_residual = grad_residual + grad_out
    grad_attn = grad_residual.astype(jnp.bfloat16)
    grad_proj = jnp.dot(head_rows.T, grad_attn, preferred_element_type=jnp.float32)
    grad_heads = jnp.dot(grad_attn, proj_weight.T, preferred_element_type=jnp.float32).astype(
        jnp.bfloat16
    )
    grad_spread = lax.all_to_all(
        grad_heads.reshape(batch, places, groups, group_width),
        "seq",
        split_axis=2,
        concat_axis=1,
        tiled=True,
    )
    grad_mixed = grad_spread.reshape(batch, length, local_heads, HEAD)
    scores_again = attention_scores(queries, key_rows, key_valid)
    probs_full = jnp.exp(scores_again - log_total)
    probs_low = probs_full.astype(jnp.bfloat16)
    grad_values = jnp.einsum(
        "bhqk,bqhc->bkhc", probs_low, grad_mixed, preferred_element_type=jnp.float32
    )
    grad_probs = jnp.einsum(
        "bqhc,bkhc->bhqk", grad_mixed, values, preferred_element_type=jnp.float32
    )
    grad_scores = probs_full * (
        grad_probs - jnp.sum(probs_full * grad_probs, axis=-1, keepdims=True)
    )
    grad_scores = grad_scores.astype(jnp.bfloat16)
    grad_queries = jnp.einsum(
        "bhqk,bkhc->bqhc", grad_scores, key_rows, preferred_element_type=jnp.float32
    ) * HEAD ** (-0.5)
    grad_keys = jnp.einsum(
        "bhqk,bqhc->bkhc", grad_scores, queries, preferred_element_type=jnp.float32
    ) * HEAD ** (-0.5)
    stacked = jnp.stack([grad_queries, grad_keys, grad_values], axis=2).astype(jnp.bfloat16)
    stacked = stacked.reshape(batch, length, 3, 1, group_width)
    returned = lax.all_to_all(stacked, "seq", split_axis=1, concat_axis=3, tiled=True)
    grad_packed = returned.reshape(token_count, 3 * features)
    grad_qkv = jnp.dot(normed.T, grad_packed, preferred_element_type=jnp.float32)
    grad_normed = jnp.dot(grad_packed, qkv_weight.T, preferred_element_type=jnp.float32)
    norm_pull_one = jax.vjp(layer_norm, inputs, gain_one, shift_one)[1]
    grad_inputs, grad_gain_one, grad_shift_one = norm_pull_one(grad_normed)
    grad_tokens = (grad_inputs + grad_residual).reshape(batch, places, features)
    grads = (
        grad_gain_one,
        grad_shift_one,
        grad_qkv,
        grad_proj,
        grad_gain_two,
        grad_shift_two,
        grad_router,
        grad_inner,
        grad_outer,
    )
    return (outputs.astype(jnp.bfloat16).reshape(batch, places, features), grad_tokens, grads)


def body(
    tokens,
    key_mask,
    expert_ids,
    ln1_gain,
    ln1_bias,
    w_qkv,
    w_attn_out,
    ln2_gain,
    ln2_bias,
    router,
    w_in,
    w_out,
    cotangent,
):
    per_batch = tokens.shape[0] // MICRO
    totals = None
    out_parts = []
    grad_parts = []
    for batch_step in range(MICRO):
        fetched = (
            lax.all_gather(ln1_gain, "dp", axis=0, tiled=True),
            lax.all_gather(ln1_bias, "dp", axis=0, tiled=True),
            lax.all_gather(w_qkv, "dp", axis=0, tiled=True),
            lax.all_gather(w_attn_out, "dp", axis=0, tiled=True),
            lax.all_gather(ln2_gain, "dp", axis=0, tiled=True),
            lax.all_gather(ln2_bias, "dp", axis=0, tiled=True),
            lax.all_gather(router, "dp", axis=0, tiled=True),
            lax.all_gather(w_in, "dp", axis=1, tiled=True),
            lax.all_gather(w_out, "dp", axis=1, tiled=True),
        )
        first = batch_step * per_batch
        last = first + per_batch
        out_part, grad_part, grads = micro_step(
            fetched,
            tokens[first:last],
            key_mask[first:last],
            expert_ids[first:last],
            cotangent[first:last],
        )
        out_parts.append(out_part)
        grad_parts.append(grad_part)
        totals = grads if totals is None else jax.tree.map(jnp.add, totals, grads)
    totals = reduce_end(totals)
    return (
        jnp.concatenate(out_parts, axis=0),
        jnp.concatenate(grad_parts, axis=0),
        totals[0],
        totals[1],
        totals[2],
        totals[3],
        totals[4],
        totals[5],
        totals[6],
        totals[7],
        totals[8],
    )


def solution(mesh):
    placed = (
        P("dp", "seq", None),
        P("dp", None),
        P("dp", "seq", None),
        P("dp"),
        P("dp"),
        P("dp", None),
        P("dp", None),
        P("dp"),
        P("dp"),
        P("dp", None),
        P(None, "dp", None),
        P(None, "dp", None),
        P("dp", "seq", None),
    )
    whole = mesh.shape['dp'] == 8 and mesh.shape['seq'] == 4
    return jax.shard_map(
        plane_body if whole else body,
        mesh=mesh,
        in_specs=placed,
        out_specs=(
            P("dp", "seq", None),
            P("dp", "seq", None),
            P("dp"),
            P("dp"),
            P("dp", None),
            P("dp", None),
            P("dp"),
            P("dp"),
            P("dp", None),
            P(None, "dp", None),
            P(None, "dp", None),
        ),
        check_vma=False,
    )
```
